32 devices in a mesh: lon: 8 (over z, x), lat: 4 (over y, core).
Axes of the slice: x: 2, y: 2, z: 4, core: 2. Of those that a mesh axis runs over, the one named last changes fastest.
Arguments:
- fields: bfloat16 [128, 256, 256], P('lat', 'lon'), may hold values from -6 to 6
- cotangent: bfloat16 [128, 256, 256], P('lat', 'lon'), may hold values from -6 to 6
- dw_kernel: bfloat16 [7, 7, 256], replicated, may hold values from -0.875 to 0.875
- dw_bias: bfloat16 [256], replicated, may hold values from -3 to 3
- norm_gain: bfloat16 [256], replicated, may hold values from 0.099609375 to 1.8984375
- layer_norm_offset: bfloat16 [256], replicated, may hold values from -3 to 3
- w_expand: bfloat16 [256, 1024], replicated, may hold values from -0.375 to 0.375
- b_expand: bfloat16 [1024], replicated, may hold values from -3 to 3
- w_project: bfloat16 [1024, 256], replicated, may hold values from -0.1875 to 0.1875
- b_project: bfloat16 [256], replicated, may hold values from -3 to 3
Outputs:
- block_out: bfloat16 [128, 256, 256], P('lat', 'lon')
- grad_fields: bfloat16 [128, 256, 256], P('lat', 'lon')
- grad_kernel: float32 [7, 7, 256], replicated
- grad_dw_bias: float32 [256], replicated
- grad_gain: float32 [256], replicated
- grad_shift: float32 [256], replicated
- grad_expand: float32 [256, 1024], replicated
- grad_b_expand: float32 [1024], replicated
- grad_project: float32 [1024, 256], replicated
- grad_b_project: float32 [256], replicated
The draws below stay inside these ranges and needn't reach their ends.
All inputs are finite; a program needn't handle non-finite values.
Results may differ from the reference program's by a relative error of at most 0.0075.
Values may be sent and summed in bfloat16 or wider, within the bound.
No kernel may reach another device: no remote copies, remote signals or barrier semaphores. Data moves between devices by JAX's collectives and lax.ppermute only.
A program may use at most 64 MiB of HBM per device.

```python
import math
import jax
import jax.numpy as jnp
from jax import lax

C = 256
H = 1024
NLAT = 128
NLON = 256


def shard_levels(rng, shape, cuts, least, top_value):
    gain, own = 1.0, jax.random.fold_in(rng, 6)
    for axis_at, blocks in cuts:
        steps = jnp.exp(jax.random.uniform(jax.random.fold_in(own, axis_at), (blocks,), jnp.float32, least / len(cuts), top_value / len(cuts)))
        gain = gain * jnp.repeat(steps, shape[axis_at] // blocks).reshape([-1 if axis == axis_at else 1 for axis in range(len(shape))])
    return gain


def bell_draw(own_key, extent, spread, limit, shards=(), held_as=jnp.bfloat16):
    entries = spread * jax.random.normal(own_key, extent, jnp.float32)
    if shards:
        entries = entries * shard_levels(own_key, extent, shards, -0.22, 0.18)
    return jnp.clip(entries, -limit, limit).astype(held_as)


def setup_inputs(seed: int = 0) -> dict:
    streams_of = jax.random.split(jax.random.key(seed), 11)
    return {
        "fields": bell_draw(streams_of[0], (NLAT, NLON, C), 1.0, 6.0, ((0, 4), (1, 8))),
        "cotangent": bell_draw(streams_of[1], (NLAT, NLON, C), 1.0, 6.0, ((0, 4), (1, 8))),
        "dw_kernel": bell_draw(streams_of[2], (7, 7, C), 49 ** -0.5, 0.875),
        "dw_bias": bell_draw(streams_of[3], (C,), 0.5, 3.0),
        "norm_gain": jnp.clip(1.0 + 0.18 * jax.random.normal(streams_of[4], (C,), jnp.float32), 0.099609375, 1.8984375).astype(jnp.bfloat16),
        "layer_norm_offset": bell_draw(streams_of[5], (C,), 0.5, 3.0),
        "w_expand": bell_draw(streams_of[6], (C, H), C ** -0.5, 0.375),
        "b_expand": bell_draw(streams_of[7], (H,), 0.5, 3.0),
        "w_project": bell_draw(streams_of[8], (H, C), H ** -0.5, 0.1875),
        "b_project": bell_draw(streams_of[9], (C,), 0.5, 3.0),
    }


EPS = 1e-06

def sphere_pad(field):
    half = field.shape[1] // 2
    rolled = jnp.roll(field, -half, axis=1)
    tall = jnp.concatenate([rolled[2::-1], field, rolled[:-4:-1]], axis=0)
    return jnp.concatenate([tall[:, -3:], tall, tall[:, :3]], axis=1)

def gelu_parts(values):
    normal_cdf = 0.5 * (1.0 + jax.scipy.special.erf(values * (1.0 / math.sqrt(2.0))))
    density = jnp.exp(-0.5 * values * values) * (1.0 / math.sqrt(2.0 * math.pi))
    return (values * normal_cdf, normal_cdf + values * density)

def depthwise(padded, kernel, rows, cols):
    weights = kernel.astype(jnp.float32)
    total = jnp.zeros((rows, cols, kernel.shape[2]), jnp.float32)
    for row_off in range(7):
        for col_off in range(7):
            total = total + weights[row_off, col_off] * padded[row_off:row_off + rows, col_off:col_off + cols].astype(jnp.float32)
    return total

def contract_rows(left, right):
    return lax.dot_general(left, right, (((0,), (0,)), ((), ())), preferred_element_type=jnp.float32)

def reference(fields, cotangent, dw_kernel, dw_bias, norm_gain, layer_norm_offset, w_expand, b_expand, w_project, b_project):
    rows_total = fields.shape[0]
    cols = fields.shape[1]
    chans = fields.shape[2]
    padded = sphere_pad(fields)
    step = math.gcd(rows_total, 16)
    blocks = rows_total // step
    norm_scale_factor = norm_gain.astype(jnp.float32)

    def forward_block(index):
        start = index * step
        pad_block = lax.dynamic_slice_in_dim(padded, start, step + 6, 0)
        field_block = lax.dynamic_slice_in_dim(fields, start, step, 0).reshape(-1, chans)
        cot_block = lax.dynamic_slice_in_dim(cotangent, start, step, 0).reshape(-1, chans)
        conv = depthwise(pad_block, dw_kernel, step, cols).reshape(-1, chans) + dw_bias.astype(jnp.float32)
        mean_removed = conv - lax.optimization_barrier(jnp.mean(conv, axis=-1, keepdims=True))
        inverse_deviation = lax.rsqrt(lax.optimization_barrier(jnp.mean(mean_removed * mean_removed, axis=-1, keepdims=True)) + EPS)
        standardized_input = mean_removed * inverse_deviation
        normalized_input = (standardized_input * norm_scale_factor + layer_norm_offset.astype(jnp.float32)).astype(jnp.bfloat16)
        pre = jnp.dot(normalized_input, w_expand, preferred_element_type=jnp.float32) + b_expand.astype(jnp.float32)
        active, slope = gelu_parts(pre)
        hidden = active.astype(jnp.bfloat16)
        branch = jnp.dot(hidden, w_project, preferred_element_type=jnp.float32) + b_project.astype(jnp.float32)
        output = (field_block.astype(jnp.float32) + branch).astype(jnp.bfloat16)
        grad_proj = contract_rows(hidden, cot_block)
        grad_bproj = lax.optimization_barrier(jnp.sum(cot_block.astype(jnp.float32), axis=0))
        d_hidden = jnp.dot(cot_block, w_project.T, preferred_element_type=jnp.float32)
        d_pre = (d_hidden * slope).astype(jnp.bfloat16)
        grad_exp = contract_rows(normalized_input, d_pre)
        grad_bexp = lax.optimization_barrier(jnp.sum(d_pre.astype(jnp.float32), axis=0))
        normalized_gradient = jnp.dot(d_pre, w_expand.T, preferred_element_type=jnp.float32)
        gain_gradient = lax.optimization_barrier(jnp.sum(normalized_gradient * standardized_input, axis=0))
        grad_sh = lax.optimization_barrier(jnp.sum(normalized_gradient, axis=0))
        scaled_output = normalized_gradient * norm_scale_factor
        conv_gradient = inverse_deviation * (scaled_output - lax.optimization_barrier(jnp.mean(scaled_output, axis=-1, keepdims=True)) - standardized_input * lax.optimization_barrier(jnp.mean(scaled_output * standardized_input, axis=-1, keepdims=True)))
        return (output.reshape(step, cols, chans), conv_gradient.astype(jnp.bfloat16).reshape(step, cols, chans), (grad_proj, grad_bproj, grad_exp, grad_bexp, gain_gradient, grad_sh))
    out_blocks, dconv_blocks, partials = lax.map(forward_block, jnp.arange(blocks, dtype=jnp.int32))
    block_out = out_blocks.reshape(fields.shape)
    conv_gradient = dconv_blocks.reshape(fields.shape)
    grad_proj, grad_bproj, grad_exp, grad_bexp, gain_gradient, grad_sh = [lax.optimization_barrier(jnp.sum(item, axis=0)) for item in partials]

    def adjoint_block(index, carry):
        grad_pad, grad_kern = carry
        start = index * step
        pad_block = lax.dynamic_slice_in_dim(padded, start, step + 6, 0).astype(jnp.float32)
        cot_conv = lax.dynamic_slice_in_dim(conv_gradient, start, step, 0).astype(jnp.float32)

        def conv_only(block_in, kern):
            return depthwise(block_in, kern, step, cols)
        unused, pull = jax.vjp(conv_only, pad_block, dw_kernel.astype(jnp.float32))
        grad_block, kern_part = pull(cot_conv)
        current = lax.dynamic_slice_in_dim(grad_pad, start, step + 6, 0)
        grad_pad = lax.dynamic_update_slice_in_dim(grad_pad, current + grad_block, start, 0)
        return (grad_pad, grad_kern + kern_part)
    grad_pad, grad_kern = lax.fori_loop(0, blocks, adjoint_block, (jnp.zeros((rows_total + 6, cols + 6, chans), jnp.float32), jnp.zeros((7, 7, chans), jnp.float32)))
    unused, pad_pull = jax.vjp(sphere_pad, fields.astype(jnp.float32))
    grad_plain, = pad_pull(grad_pad)
    grad_fields = (cotangent.astype(jnp.float32) + grad_plain).astype(jnp.bfloat16)
    grad_dwb = lax.optimization_barrier(jnp.sum(conv_gradient.astype(jnp.float32), axis=(0, 1)))
    scale_factor = 1.0 / math.sqrt(rows_total * cols)
    return (block_out, grad_fields, grad_kern * scale_factor, grad_dwb * scale_factor, gain_gradient * scale_factor, grad_sh * scale_factor, grad_exp * scale_factor, grad_bexp * scale_factor, grad_proj * scale_factor, grad_bproj * scale_factor)
```

```python
import math

import jax
import jax.numpy as jnp
from jax import lax
from jax.sharding import PartitionSpec as P

EPS = 1e-06


def flat_pairs(target):
    lons, lats = lax.axis_size("lon"), lax.axis_size("lat")
    pairs = []
    for lon in range(lons):
        for lat in range(lats):
            to_lon, to_lat = target(lon, lat)
            pairs.append((lon * lats + lat, to_lon * lats + to_lat))
    return pairs


def send(value, target):
    return lax.ppermute(value, ("lon", "lat"), flat_pairs(target))


def lon_margins(field):
    lons = lax.axis_size("lon")
    odd = lax.axis_index("lon") % 2 == 1
    first, last = field[:, :3], field[:, -3:]
    inner = send(jnp.where(odd, first, last), lambda lon, lat: (lon ^ 1, lat))
    outer = send(
        jnp.where(odd, last, first),
        lambda lon, lat: ((lon + 1) % lons if lon % 2 else (lon - 1) % lons, lat),
    )
    west = jnp.where(odd, inner, outer)
    east = jnp.where(odd, outer, inner)
    return jnp.concatenate([west, field, east], axis=1)


def lat_margins(wide):
    lons, lats = lax.axis_size("lon"), lax.axis_size("lat")
    lat = lax.axis_index("lat")
    odd = lat % 2 == 1
    pole = (lat == 0) | (lat == lats - 1)
    first, last = wide[:3], wide[-3:]

    def beyond(lon, lat):
        if lat == 0 or lat == lats - 1:
            return ((lon + lons // 2) % lons, lat)
        return (lon, lat + 1 if lat % 2 else lat - 1)

    outgoing = jnp.where(odd, last, first)
    outgoing = jnp.where(pole, outgoing[::-1], outgoing)
    far = send(outgoing, beyond)
    near = send(jnp.where(odd, first, last), lambda lon, lat: (lon, lat ^ 1))
    north = jnp.where(odd, near, far)
    south = jnp.where(odd, far, near)
    return north, south


def axis_bits():
    lon_bits = [("lon", bit) for bit in range((lax.axis_size("lon") - 1).bit_length())]
    lat_bits = [("lat", bit) for bit in range(1, (lax.axis_size("lat") - 1).bit_length())]
    steps = []
    while lon_bits or lat_bits:
        if lon_bits:
            steps.append(lon_bits.pop(0))
        if lat_bits:
            steps.append(lat_bits.pop(0))
    return steps


def flip(place, step):
    lon, lat = place
    axis, bit = step
    return (lon ^ (1 << bit), lat) if axis == "lon" else (lon, lat ^ (1 << bit))


def summed(keep, give):
    core = lax.axis_index("lat") % 2
    steps = axis_bits()
    other = list(steps)
    for at in range(0, len(steps) - 1, 2):
        other[at], other[at + 1] = other[at + 1], other[at]

    def exchange(value, at):
        return send(value, lambda lon, lat: flip((lon, lat), (other if lat % 2 else steps)[at]))

    def bit_of(at):
        def bit(step):
            return lax.shift_right_logical(lax.axis_index(step[0]), step[1]) & 1

        return jnp.where(core == 1, bit(other[at]), bit(steps[at]))

    total = keep + send(give, lambda lon, lat: (lon, lat ^ 1)).astype(jnp.float32)
    halvings = min(2, len(steps))
    for at in range(halvings):
        half = total.shape[0] // 2
        bit = bit_of(at)
        outgoing = lax.dynamic_slice_in_dim(total, (1 - bit) * half, half, 0)
        mine = lax.dynamic_slice_in_dim(total, bit * half, half, 0)
        total = mine + exchange(outgoing.astype(jnp.bfloat16), at).astype(jnp.float32)
    sent = total.astype(jnp.bfloat16)
    for at in range(halvings, len(steps)):
        got = exchange(sent, at)
        sent = (sent.astype(jnp.float32) + got.astype(jnp.float32)).astype(jnp.bfloat16)
    for at in reversed(range(halvings)):
        got = exchange(sent, at)
        low = bit_of(at) == 0
        sent = jnp.concatenate([jnp.where(low, sent, got), jnp.where(low, got, sent)], axis=0)
    got = send(sent, lambda lon, lat: (lon, lat ^ 1))
    return jnp.where(core == 0, sent, got), jnp.where(core == 0, got, sent)


def gelu_parts(values):
    normal_cdf = 0.5 * (1.0 + jax.scipy.special.erf(values * (1.0 / math.sqrt(2.0))))
    density = jnp.exp(-0.5 * values * values) * (1.0 / math.sqrt(2.0 * math.pi))
    return (values * normal_cdf, normal_cdf + values * density)


def contract_rows(left, right):
    return lax.dot_general(
        left, right, (((0,), (0,)), ((), ())), preferred_element_type=jnp.float32
    )


def sphere_pad(field):
    lat = lax.axis_index("lat")
    wide = lon_margins(field)
    top, bottom = lat_margins(wide)
    return (
        jnp.concatenate([top, wide, bottom], axis=0),
        lat == 0,
        lat == lax.axis_size("lat") - 1,
    )


def local(
    fields,
    cotangent,
    dw_kernel,
    dw_bias,
    norm_gain,
    layer_norm_offset,
    w_expand,
    b_expand,
    w_project,
    b_project,
):
    rows = fields.shape[0]
    cols = fields.shape[1]
    chans = fields.shape[2]
    scale_factor = 1.0 / math.sqrt(rows * cols * lax.axis_size("lat") * lax.axis_size("lon"))
    weights = dw_kernel.astype(jnp.float32)
    norm_scale_factor = norm_gain.astype(jnp.float32)
    padded, north, south = sphere_pad(fields)
    conv = jnp.zeros((rows, cols, chans), jnp.float32)
    for row_off in range(7):
        for col_off in range(7):
            conv = conv + weights[row_off, col_off] * padded[
                row_off : row_off + rows, col_off : col_off + cols
            ].astype(jnp.float32)
    conv = conv.reshape(-1, chans) + dw_bias.astype(jnp.float32)
    mean_removed = conv - jnp.mean(conv, axis=-1, keepdims=True)
    inverse_deviation = lax.rsqrt(
        jnp.mean(mean_removed * mean_removed, axis=-1, keepdims=True) + EPS
    )
    standardized_input = mean_removed * inverse_deviation
    normalized_input = (
        standardized_input * norm_scale_factor + layer_norm_offset.astype(jnp.float32)
    ).astype(jnp.bfloat16)
    pre = jnp.dot(normalized_input, w_expand, preferred_element_type=jnp.float32) + b_expand.astype(
        jnp.float32
    )
    active, slope = gelu_parts(pre)
    hidden = active.astype(jnp.bfloat16)
    branch = jnp.dot(hidden, w_project, preferred_element_type=jnp.float32) + b_project.astype(
        jnp.float32
    )
    flat_fields = fields.reshape(-1, chans)
    block_out = (
        (flat_fields.astype(jnp.float32) + branch).astype(jnp.bfloat16).reshape(rows, cols, chans)
    )
    flat_cot = cotangent.reshape(-1, chans)
    grad_proj = contract_rows(hidden, flat_cot) * scale_factor
    grad_bproj = jnp.sum(flat_cot.astype(jnp.float32), axis=0) * scale_factor
    d_hidden = jnp.dot(flat_cot, w_project.T, preferred_element_type=jnp.float32)
    d_pre = (d_hidden * slope).astype(jnp.bfloat16)
    grad_exp = contract_rows(normalized_input, d_pre) * scale_factor
    grad_bexp = jnp.sum(d_pre.astype(jnp.float32), axis=0) * scale_factor
    normalized_gradient = jnp.dot(d_pre, w_expand.T, preferred_element_type=jnp.float32)
    gain_gradient = jnp.sum(normalized_gradient * standardized_input, axis=0) * scale_factor
    grad_sh = jnp.sum(normalized_gradient, axis=0) * scale_factor
    scaled_output = normalized_gradient * norm_scale_factor
    conv_gradient = inverse_deviation * (
        scaled_output
        - jnp.mean(scaled_output, axis=-1, keepdims=True)
        - standardized_input * jnp.mean(scaled_output * standardized_input, axis=-1, keepdims=True)
    )
    conv_gradient = conv_gradient.astype(jnp.bfloat16).reshape(rows, cols, chans)
    grad_dwb = jnp.sum(conv_gradient.astype(jnp.float32), axis=(0, 1)) * scale_factor
    dconv_wide = conv_gradient.astype(jnp.float32)
    kern_terms = []
    for row_off in range(7):
        for col_off in range(7):
            window = padded[row_off : row_off + rows, col_off : col_off + cols].astype(jnp.float32)
            kern_terms.append(jnp.sum(dconv_wide * window, axis=(0, 1)))
    grad_kern = jnp.stack(kern_terms, axis=0).reshape(7, 7, chans) * scale_factor
    dpad, north, south = sphere_pad(conv_gradient)
    zero_rows = jnp.zeros((3, cols + 6, chans), jnp.bfloat16)
    inner = jnp.concatenate(
        [jnp.where(north, zero_rows, dpad[:3]), dpad[3:-3], jnp.where(south, zero_rows, dpad[-3:])],
        axis=0,
    )
    spacer = jnp.zeros((6, cols + 6, chans), jnp.bfloat16)
    fold_north = jnp.concatenate([jnp.where(north, dpad[:3], zero_rows), spacer], axis=0)
    fold_south = jnp.concatenate([spacer, jnp.where(south, dpad[-3:], zero_rows)], axis=0)
    adjoint = jnp.zeros((rows, cols, chans), jnp.float32)
    north_term = jnp.zeros((3, cols, chans), jnp.float32)
    south_term = jnp.zeros((3, cols, chans), jnp.float32)
    for row_off in range(7):
        for col_off in range(7):
            weight = weights[row_off, col_off]
            col_from = 6 - col_off
            adjoint = adjoint + weight * inner[
                6 - row_off : 6 - row_off + rows, col_from : col_from + cols
            ].astype(jnp.float32)
            north_term = north_term + weight * fold_north[
                row_off : row_off + 3, col_from : col_from + cols
            ].astype(jnp.float32)
            south_term = south_term + weight * fold_south[
                row_off : row_off + 3, col_from : col_from + cols
            ].astype(jnp.float32)
    adjoint = adjoint.at[:3].add(north_term)
    adjoint = adjoint.at[rows - 3 :].add(south_term)
    grad_fields = (cotangent.astype(jnp.float32) + adjoint).astype(jnp.bfloat16)
    hidden_units = w_expand.shape[1]
    pieces = hidden_units // chans
    small = [
        grad_kern.reshape(49, chans),
        grad_dwb.reshape(1, chans),
        gain_gradient.reshape(1, chans),
        grad_sh.reshape(1, chans),
        grad_bproj.reshape(1, chans),
        grad_bexp.reshape(pieces, chans),
        jnp.zeros((128 - 53 - pieces, chans), jnp.float32),
    ]
    expand_rows = grad_exp.reshape(chans, pieces, chans).swapaxes(0, 1).reshape(-1, chans)
    first = jnp.concatenate([expand_rows, jnp.concatenate(small, axis=0)[:64]], axis=0)
    second = jnp.concatenate([grad_proj, jnp.concatenate(small, axis=0)[64:128]], axis=0)
    core = lax.axis_index("lat") % 2
    keep = jnp.where(core == 0, first, second)
    give = jnp.where(core == 0, second, first).astype(jnp.bfloat16)
    first, second = summed(keep, give)
    first = first.astype(jnp.float32)
    second = second.astype(jnp.float32)
    sum_exp = first[:hidden_units].reshape(pieces, chans, chans).swapaxes(0, 1).reshape(chans, -1)
    sum_proj = second[:hidden_units]
    rest = first[hidden_units:]
    sum_kern = rest[:49].reshape(7, 7, chans)
    sum_dwb, sum_gn, sum_sh, sum_bproj = rest[49], rest[50], rest[51], rest[52]
    sum_bexp = rest[53 : 53 + pieces].reshape(-1)
    return (
        block_out,
        grad_fields,
        sum_kern,
        sum_dwb,
        sum_gn,
        sum_sh,
        sum_exp,
        sum_bexp,
        sum_proj,
        sum_bproj,
    )


def solution(mesh):
    placed = (P("lat", "lon", None), P("lat", "lon", None), P(), P(), P(), P(), P(), P(), P(), P())
    return jax.shard_map(
        local,
        mesh=mesh,
        in_specs=placed,
        out_specs=(
            P("lat", "lon", None),
            P("lat", "lon", None),
            P(),
            P(),
            P(),
            P(),
            P(),
            P(),
            P(),
            P(),
        ),
        check_vma=False,
    )
```

```python
import functools
import math

import jax
import jax.numpy as jnp
from jax import lax
from jax.experimental import pallas as pl
from jax.experimental.pallas import tpu as pltpu
from jax.sharding import PartitionSpec as P

EPS = 1e-06


def flat_pairs(target):
    lons, lats = lax.axis_size("lon"), lax.axis_size("lat")
    pairs = []
    for lon in range(lons):
        for lat in range(lats):
            to_lon, to_lat = target(lon, lat)
            pairs.append((lon * lats + lat, to_lon * lats + to_lat))
    return pairs


def send(value, target):
    return lax.ppermute(value, ("lon", "lat"), flat_pairs(target))


def lon_margins(field):
    lons = lax.axis_size("lon")
    odd = lax.axis_index("lon") % 2 == 1
    first, last = field[:, :3], field[:, -3:]
    inner = send(jnp.where(odd, first, last), lambda lon, lat: (lon ^ 1, lat))
    outer = send(
        jnp.where(odd, last, first),
        lambda lon, lat: ((lon + 1) % lons if lon % 2 else (lon - 1) % lons, lat),
    )
    west = jnp.where(odd, inner, outer)
    east = jnp.where(odd, outer, inner)
    return jnp.concatenate([west, field, east], axis=1)


def lat_margins(wide):
    lons, lats = lax.axis_size("lon"), lax.axis_size("lat")
    lat = lax.axis_index("lat")
    odd = lat % 2 == 1
    pole = (lat == 0) | (lat == lats - 1)
    first, last = wide[:3], wide[-3:]

    def beyond(lon, lat):
        if lat == 0 or lat == lats - 1:
            return ((lon + lons // 2) % lons, lat)
        return (lon, lat + 1 if lat % 2 else lat - 1)

    outgoing = jnp.where(odd, last, first)
    outgoing = jnp.where(pole, outgoing[::-1], outgoing)
    far = send(outgoing, beyond)
    near = send(jnp.where(odd, first, last), lambda lon, lat: (lon, lat ^ 1))
    north = jnp.where(odd, near, far)
    south = jnp.where(odd, far, near)
    return north, south


def axis_bits():
    lon_bits = [("lon", bit) for bit in range((lax.axis_size("lon") - 1).bit_length())]
    lat_bits = [("lat", bit) for bit in range(1, (lax.axis_size("lat") - 1).bit_length())]
    steps = []
    while lon_bits or lat_bits:
        if lon_bits:
            steps.append(lon_bits.pop(0))
        if lat_bits:
            steps.append(lat_bits.pop(0))
    return steps


def flip(place, step):
    lon, lat = place
    axis, bit = step
    return (lon ^ (1 << bit), lat) if axis == "lon" else (lon, lat ^ (1 << bit))


def summed(keep, give):
    core = lax.axis_index("lat") % 2
    steps = axis_bits()
    other = list(steps)
    for at in range(0, len(steps) - 1, 2):
        other[at], other[at + 1] = other[at + 1], other[at]

    def exchange(value, at):
        return send(value, lambda lon, lat: flip((lon, lat), (other if lat % 2 else steps)[at]))

    def bit_of(at):
        def bit(step):
            return lax.shift_right_logical(lax.axis_index(step[0]), step[1]) & 1

        return jnp.where(core == 1, bit(other[at]), bit(steps[at]))

    total = keep + send(give, lambda lon, lat: (lon, lat ^ 1)).astype(jnp.float32)
    halvings = min(2, len(steps))
    for at in range(halvings):
        half = total.shape[0] // 2
        bit = bit_of(at)
        outgoing = lax.dynamic_slice_in_dim(total, (1 - bit) * half, half, 0)
        mine = lax.dynamic_slice_in_dim(total, bit * half, half, 0)
        total = mine + exchange(outgoing.astype(jnp.bfloat16), at).astype(jnp.float32)
    sent = total.astype(jnp.bfloat16)
    for at in range(halvings, len(steps)):
        got = exchange(sent, at)
        sent = (sent.astype(jnp.float32) + got.astype(jnp.float32)).astype(jnp.bfloat16)
    for at in reversed(range(halvings)):
        got = exchange(sent, at)
        low = bit_of(at) == 0
        sent = jnp.concatenate([jnp.where(low, sent, got), jnp.where(low, got, sent)], axis=0)
    got = send(sent, lambda lon, lat: (lon, lat ^ 1))
    return jnp.where(core == 0, sent, got), jnp.where(core == 0, got, sent)


def gelu_parts(values):
    normal_cdf = 0.5 * (1.0 + jax.scipy.special.erf(values * (1.0 / math.sqrt(2.0))))
    density = jnp.exp(-0.5 * values * values) * (1.0 / math.sqrt(2.0 * math.pi))
    return (values * normal_cdf, normal_cdf + values * density)


LANES = 128
SUBLANES = 8


def slot_rows(ref, lane, row, start, count):
    return ref[lane, row, pl.ds(start, SUBLANES, stride=count), :]


def spread_weights(weight_ref, spread_ref):
    for lane in range(spread_ref.shape[0]):
        for tap in range(49):
            row = weight_ref[tap : tap + 1, lane * LANES : (lane + 1) * LANES]
            spread_ref[lane, tap] = jnp.broadcast_to(row.astype(jnp.float32), (SUBLANES, LANES))


def split_lanes(source_ref, wide_ref):
    rows = source_ref.shape[0]

    def body(row, carry):
        for lane in range(wide_ref.shape[0]):
            wide_ref[lane, row] = source_ref[row, :, lane * LANES : (lane + 1) * LANES].astype(
                jnp.float32
            )
        return carry

    lax.fori_loop(0, rows, body, 0)


def main_kernel(
    scale_factor,
    padded_ref,
    fields_ref,
    cot_ref,
    dw_ref,
    chan_ref,
    b_expand_ref,
    w_expand_ref,
    w_project_ref,
    out_ref,
    dconv_ref,
    expand_ref,
    project_ref,
    small_ref,
    wide_ref,
    spread_ref,
    conv_ref,
    dwide_ref,
):
    tiles = wide_ref.shape[0]
    rows = conv_ref.shape[1]
    cols = conv_ref.shape[2]
    chans = tiles * LANES
    slots = cols // SUBLANES
    hidden_units = w_expand_ref.shape[1]
    pieces = hidden_units // chans
    block_rows = 8
    blocks = rows // block_rows
    cells = block_rows * cols
    spread_weights(dw_ref, spread_ref)
    split_lanes(padded_ref, wide_ref)

    def conv_block(at, carry):
        lane, start = at // (rows // 4), (at % (rows // 4)) * 4
        totals = [[jnp.zeros((SUBLANES, LANES), jnp.float32)] * slots for unused in range(4)]
        for row in range(10):
            loaded = [
                slot_rows(wide_ref, lane, start + row, place, slots) for place in range(slots + 6)
            ]
            for row_off in range(7):
                to = row - row_off
                if 0 <= to < 4:
                    for col_off in range(7):
                        weight = spread_ref[lane, row_off * 7 + col_off]
                        for slot in range(slots):
                            totals[to][slot] = totals[to][slot] + weight * loaded[slot + col_off]
        for to in range(4):
            for slot in range(slots):
                conv_ref[lane, start + to, pl.ds(slot, SUBLANES, stride=slots), :] = totals[to][slot]
        return carry

    lax.fori_loop(0, tiles * (rows // 4), conv_block, 0)

    expand_ref[...] = jnp.zeros_like(expand_ref)
    project_ref[...] = jnp.zeros_like(project_ref)
    small_ref[...] = jnp.zeros_like(small_ref)
    dw_bias = chan_ref[0:1].astype(jnp.float32)
    gain = chan_ref[1:2].astype(jnp.float32)
    offset = chan_ref[2:3].astype(jnp.float32)
    b_project = chan_ref[3:4].astype(jnp.float32)

    def mlp_block(block, carry):
        row = block * block_rows
        conv = jnp.concatenate(
            [conv_ref[lane, pl.ds(row, block_rows)].reshape(cells, LANES) for lane in range(tiles)],
            axis=1,
        )
        conv = conv + dw_bias
        removed = conv - jnp.mean(conv, axis=-1, keepdims=True)
        deviation = lax.rsqrt(jnp.mean(removed * removed, axis=-1, keepdims=True) + EPS)
        xhat = removed * deviation
        normed = (xhat * gain + offset).astype(jnp.bfloat16)
        cot = cot_ref[pl.ds(block * cells, cells), :]
        branch = jnp.zeros((cells, chans), jnp.float32)
        d_normed = jnp.zeros((cells, chans), jnp.float32)
        for piece in range(pieces):
            part = slice(piece * chans, (piece + 1) * chans)
            w_in = w_expand_ref[:, part]
            w_out = w_project_ref[part, :]
            pre = jnp.dot(normed, w_in, preferred_element_type=jnp.float32)
            pre = pre + b_expand_ref[0:1, part].astype(jnp.float32)
            active, slope = gelu_parts(pre)
            hidden = active.astype(jnp.bfloat16)
            branch = branch + jnp.dot(hidden, w_out, preferred_element_type=jnp.float32)
            d_hidden = contract(cot, w_out, 1, 1)
            d_pre_wide = d_hidden * slope
            d_pre = d_pre_wide.astype(jnp.bfloat16)
            project_ref[part, :] += contract(hidden, cot, 0, 0)
            expand_ref[part, :] += contract(normed, d_pre, 0, 0)
            small_ref[53 + piece : 54 + piece] += jnp.sum(
                d_pre.astype(jnp.float32), axis=0, keepdims=True
            )
            d_normed = d_normed + contract(d_pre, w_in, 1, 1)
        plain = fields_ref[pl.ds(block * cells, cells), :].astype(jnp.float32)
        out_ref[pl.ds(block * cells, cells), :] = (plain + (branch + b_project)).astype(jnp.bfloat16)
        small_ref[50:51] += jnp.sum(d_normed * xhat, axis=0, keepdims=True)
        small_ref[51:52] += jnp.sum(d_normed, axis=0, keepdims=True)
        small_ref[52:53] += jnp.sum(cot.astype(jnp.float32), axis=0, keepdims=True)
        scaled = d_normed * gain
        d_conv = deviation * (
            scaled
            - jnp.mean(scaled, axis=-1, keepdims=True)
            - xhat * jnp.mean(scaled * xhat, axis=-1, keepdims=True)
        )
        d_conv = d_conv.astype(jnp.bfloat16)
        dconv_ref[pl.ds(block * cells, cells), :] = d_conv
        d_conv = d_conv.astype(jnp.float32)
        small_ref[49:50] += jnp.sum(d_conv, axis=0, keepdims=True)
        for lane in range(tiles):
            dwide_ref[lane, pl.ds(row, block_rows)] = d_conv[
                :, lane * LANES : (lane + 1) * LANES
            ].reshape(block_rows, cols, LANES)
        return carry

    lax.fori_loop(0, blocks, mlp_block, 0)

    for lane in range(tiles):
        for row_off in range(7):

            def kernel_row(row, totals):
                grads = [slot_rows(dwide_ref, lane, row, slot, slots) for slot in range(slots)]
                loaded = [
                    slot_rows(wide_ref, lane, row + row_off, place, slots)
                    for place in range(slots + 6)
                ]
                return tuple(
                    totals[col_off] + sum(grads[slot] * loaded[slot + col_off] for slot in range(slots))
                    for col_off in range(7)
                )

            zeros = tuple(jnp.zeros((SUBLANES, LANES), jnp.float32) for unused in range(7))
            totals = lax.fori_loop(0, rows, kernel_row, zeros, unroll=4)
            for col_off in range(7):
                tap = row_off * 7 + col_off
                small_ref[tap : tap + 1, lane * LANES : (lane + 1) * LANES] = jnp.sum(
                    totals[col_off], axis=0, keepdims=True
                )
    small_ref[...] = small_ref[...] * scale_factor
    expand_ref[...] = expand_ref[...] * scale_factor
    project_ref[...] = project_ref[...] * scale_factor


def contract(left, right, left_dim, right_dim):
    return lax.dot_general(
        left,
        right,
        (((left_dim,), (right_dim,)), ((), ())),
        preferred_element_type=jnp.float32,
    )


def main_pass(
    padded, fields, cot, dw_kernel, chan_params, b_expand, w_expand, w_project, scale_factor
):
    rows, cols = padded.shape[0] - 6, fields.shape[0] // (padded.shape[0] - 6)
    chans = fields.shape[1]
    hidden_units = w_expand.shape[1]
    tiles = chans // LANES
    cells = rows * cols
    pad_cols = padded.shape[1]
    return pl.pallas_call(
        functools.partial(main_kernel, scale_factor),
        out_shape=[
            jax.ShapeDtypeStruct((cells, chans), jnp.bfloat16),
            jax.ShapeDtypeStruct((cells, chans), jnp.bfloat16),
            jax.ShapeDtypeStruct((hidden_units, chans), jnp.float32),
            jax.ShapeDtypeStruct((hidden_units, chans), jnp.float32),
            jax.ShapeDtypeStruct((64, chans), jnp.float32),
        ],
        in_specs=[pl.BlockSpec(memory_space=pltpu.VMEM)] * 8,
        out_specs=[pl.BlockSpec(memory_space=pltpu.VMEM)] * 5,
        scratch_shapes=[
            pltpu.VMEM((tiles, rows + 6, pad_cols, LANES), jnp.float32),
            pltpu.VMEM((tiles, 49, SUBLANES, LANES), jnp.float32),
            pltpu.VMEM((tiles, rows, cols, LANES), jnp.float32),
            pltpu.VMEM((tiles, rows, cols, LANES), jnp.float32),
        ],
        compiler_params=pltpu.CompilerParams(vmem_limit_bytes=48 << 20),
        cost_estimate=pl.CostEstimate(
            flops=12 * cells * chans * hidden_units,
            bytes_accessed=8 << 20,
            transcendentals=2 * cells * hidden_units,
        ),
        name="block_main",
    )(padded, fields, cot, dw_kernel, chan_params, b_expand, w_expand, w_project)


def adjoint_kernel(
    poles_ref,
    padded_ref,
    cot_ref,
    dw_ref,
    out_ref,
    wide_ref,
    spread_ref,
    edge_ref,
    sum_ref,
):
    tiles = wide_ref.shape[0]
    rows = sum_ref.shape[1]
    cols = sum_ref.shape[2]
    slots = cols // SUBLANES
    spread_weights(dw_ref, spread_ref)
    split_lanes(padded_ref, wide_ref)
    for side in range(2):
        at_pole = poles_ref[side] == 1
        for lane in range(tiles):
            for row_off in range(3):
                near = row_off if side == 0 else 6 - row_off
                for col_off in range(7):
                    plain = spread_ref[lane, (6 - near) * 7 + col_off]
                    turned = spread_ref[lane, near * 7 + col_off]
                    edge_ref[side, lane, row_off * 7 + col_off] = jnp.where(at_pole, turned, plain)

    def block_of(lane, start, first, last):
        totals = [[jnp.zeros((SUBLANES, LANES), jnp.float32)] * slots for unused in range(4)]
        for row in range(10):
            loaded = [
                slot_rows(wide_ref, lane, start + row, place, slots) for place in range(slots + 6)
            ]
            for row_off in range(7):
                to = row - row_off
                if 0 <= to < 4:
                    for col_off in range(7):
                        tap = 6 - col_off
                        if first and row < 3:
                            weight = edge_ref[0, lane, row_off * 7 + tap]
                        elif last and row >= 7:
                            weight = edge_ref[1, lane, (6 - row_off) * 7 + tap]
                        else:
                            weight = spread_ref[lane, (6 - row_off) * 7 + tap]
                        for slot in range(slots):
                            totals[to][slot] = totals[to][slot] + weight * loaded[slot + col_off]
        for to in range(4):
            for slot in range(slots):
                sum_ref[lane, start + to, pl.ds(slot, SUBLANES, stride=slots), :] = totals[to][slot]

    inner = rows // 4 - 2

    def inner_block(at, carry):
        block_of(at // inner, (1 + at % inner) * 4, False, False)
        return carry

    def edge_block(lane, carry):
        block_of(lane, 0, True, False)
        block_of(lane, rows - 4, False, True)
        return carry

    lax.fori_loop(0, tiles * inner, inner_block, 0)
    lax.fori_loop(0, tiles, edge_block, 0)

    def finish(row, carry):
        total = jnp.concatenate([sum_ref[lane, row] for lane in range(tiles)], axis=1)
        out_ref[row] = (cot_ref[row].astype(jnp.float32) + total).astype(jnp.bfloat16)
        return carry

    lax.fori_loop(0, rows, finish, 0)


def adjoint_pass(padded, cot, dw_kernel, poles):
    rows, cols, chans = cot.shape
    tiles = chans // LANES
    return pl.pallas_call(
        adjoint_kernel,
        out_shape=jax.ShapeDtypeStruct(cot.shape, jnp.bfloat16),
        in_specs=[pl.BlockSpec(memory_space=pltpu.SMEM)]
        + [pl.BlockSpec(memory_space=pltpu.VMEM)] * 3,
        out_specs=pl.BlockSpec(memory_space=pltpu.VMEM),
        scratch_shapes=[
            pltpu.VMEM((tiles, rows + 6, padded.shape[1], LANES), jnp.float32),
            pltpu.VMEM((tiles, 49, SUBLANES, LANES), jnp.float32),
            pltpu.VMEM((2, tiles, 21, SUBLANES, LANES), jnp.float32),
            pltpu.VMEM((tiles, rows, cols, LANES), jnp.float32),
        ],
        compiler_params=pltpu.CompilerParams(vmem_limit_bytes=32 << 20),
        cost_estimate=pl.CostEstimate(
            flops=98 * rows * cols * chans, bytes_accessed=3 << 20, transcendentals=0
        ),
        name="block_adjoint",
    )(poles, padded, cot, dw_kernel)


def sphere_pad(field):
    wide = lon_margins(field)
    top, bottom = lat_margins(wide)
    return jnp.concatenate([top, wide, bottom], axis=0)


def local(
    fields,
    cotangent,
    dw_kernel,
    dw_bias,
    norm_gain,
    layer_norm_offset,
    w_expand,
    b_expand,
    w_project,
    b_project,
):
    rows = fields.shape[0]
    cols = fields.shape[1]
    chans = fields.shape[2]
    scale_factor = 1.0 / math.sqrt(rows * cols * lax.axis_size("lat") * lax.axis_size("lon"))
    lat = lax.axis_index("lat")
    poles = jnp.stack([lat == 0, lat == lax.axis_size("lat") - 1]).astype(jnp.int32)
    taps = dw_kernel.reshape(49, chans)
    chan_params = jnp.stack([dw_bias, norm_gain, layer_norm_offset, b_project])
    flat_cot = cotangent.reshape(-1, chans)
    block_out, conv_gradient, grad_exp, grad_proj, small = main_pass(
        sphere_pad(fields),
        fields.reshape(-1, chans),
        flat_cot,
        taps,
        chan_params,
        b_expand.reshape(1, -1),
        w_expand,
        w_project,
        scale_factor,
    )
    block_out = block_out.reshape(fields.shape)
    grad_fields = adjoint_pass(
        sphere_pad(conv_gradient.reshape(fields.shape)), cotangent, taps, poles
    )
    hidden_units = w_expand.shape[1]
    pieces = hidden_units // chans
    first = jnp.concatenate([grad_exp, small], axis=0)
    second = jnp.concatenate([grad_proj, jnp.zeros_like(small)], axis=0)
    core = lax.axis_index("lat") % 2
    keep = jnp.where(core == 0, first, second)
    give = jnp.where(core == 0, second, first).astype(jnp.bfloat16)
    first, second = summed(keep, give)
    first = first.astype(jnp.float32)
    second = second.astype(jnp.float32)
    sum_exp = first[:hidden_units].reshape(pieces, chans, chans).swapaxes(0, 1).reshape(chans, -1)
    sum_proj = second[:hidden_units]
    rest = first[hidden_units:]
    sum_kern = rest[:49].reshape(7, 7, chans)
    sum_dwb, sum_gn, sum_sh, sum_bproj = rest[49], rest[50], rest[51], rest[52]
    sum_bexp = rest[53 : 53 + pieces].reshape(-1)
    return (
        block_out,
        grad_fields,
        sum_kern,
        sum_dwb,
        sum_gn,
        sum_sh,
        sum_exp,
        sum_bexp,
        sum_proj,
        sum_bproj,
    )


def solution(mesh):
    placed = (P("lat", "lon", None), P("lat", "lon", None), P(), P(), P(), P(), P(), P(), P(), P())
    return jax.shard_map(
        local,
        mesh=mesh,
        in_specs=placed,
        out_specs=(
            P("lat", "lon", None),
            P("lat", "lon", None),
            P(),
            P(),
            P(),
            P(),
            P(),
            P(),
            P(),
            P(),
        ),
        check_vma=False,
    )
```

```python
import functools
import math

import jax
import jax.numpy as jnp
from jax import lax
from jax.experimental import pallas as pl
from jax.experimental.pallas import tpu as pltpu
from jax.sharding import PartitionSpec as P

EPS = 1e-06


def flat_pairs(target):
    lons, lats = lax.axis_size("lon"), lax.axis_size("lat")
    pairs = []
    for lon in range(lons):
        for lat in range(lats):
            to_lon, to_lat = target(lon, lat)
            pairs.append((lon * lats + lat, to_lon * lats + to_lat))
    return pairs


def send(value, target):
    return lax.ppermute(value, ("lon", "lat"), flat_pairs(target))


def lon_margins(field):
    lons = lax.axis_size("lon")
    odd = lax.axis_index("lon") % 2 == 1
    first, last = field[:, :3], field[:, -3:]
    outer = send(
        jnp.where(odd, last, first),
        lambda lon, lat: ((lon + 1) % lons if lon % 2 else (lon - 1) % lons, lat),
    )
    inner = send(jnp.where(odd, first, last), lambda lon, lat: (lon ^ 1, lat))
    west = jnp.where(odd, inner, outer)
    east = jnp.where(odd, outer, inner)
    return jnp.concatenate([west, field, east], axis=1)


def lat_margins(wide):
    lons, lats = lax.axis_size("lon"), lax.axis_size("lat")
    lat = lax.axis_index("lat")
    odd = lat % 2 == 1
    pole = (lat == 0) | (lat == lats - 1)
    first, last = wide[:3], wide[-3:]

    def beyond(lon, lat):
        if lat == 0 or lat == lats - 1:
            return ((lon + lons // 2) % lons, lat)
        return (lon, lat + 1 if lat % 2 else lat - 1)

    outgoing = jnp.where(odd, last, first)
    outgoing = jnp.where(pole, outgoing[::-1], outgoing)
    far = send(outgoing, beyond)
    near = send(jnp.where(odd, first, last), lambda lon, lat: (lon, lat ^ 1))
    north = jnp.where(odd, near, far)
    south = jnp.where(odd, far, near)
    return north, south


def axis_bits():
    lon_bits = [("lon", bit) for bit in range((lax.axis_size("lon") - 1).bit_length())]
    lat_bits = [("lat", bit) for bit in range(1, (lax.axis_size("lat") - 1).bit_length())]
    steps = []
    while lon_bits or lat_bits:
        if lon_bits:
            steps.append(lon_bits.pop(0))
        if lat_bits:
            steps.append(lat_bits.pop(0))
    return steps


def flip(place, step):
    lon, lat = place
    axis, bit = step
    return (lon ^ (1 << bit), lat) if axis == "lon" else (lon, lat ^ (1 << bit))


def partner_steps():
    core = lax.axis_index("lat") % 2
    steps = axis_bits()
    other = list(steps)
    for at in range(0, len(steps) - 1, 2):
        other[at], other[at + 1] = other[at + 1], other[at]

    def exchange(value, at):
        return send(value, lambda lon, lat: flip((lon, lat), (other if lat % 2 else steps)[at]))

    def bit_of(at):
        def bit(step):
            return lax.shift_right_logical(lax.axis_index(step[0]), step[1]) & 1

        return jnp.where(core == 1, bit(other[at]), bit(steps[at]))

    return len(steps), exchange, bit_of


def within_pair(value):
    return send(value, lambda lon, lat: (lon, lat ^ 1))


def halves(total, bit):
    half = total.shape[0] // 2
    outgoing = lax.dynamic_slice_in_dim(total, (1 - bit) * half, half, 0)
    mine = lax.dynamic_slice_in_dim(total, bit * half, half, 0)
    return mine, outgoing.astype(jnp.bfloat16)


def rounded_sum(left, right):
    return (left.astype(jnp.float32) + right.astype(jnp.float32)).astype(jnp.bfloat16)


def gelu_parts(values):
    normal_cdf = 0.5 * (1.0 + jax.scipy.special.erf(values * (1.0 / math.sqrt(2.0))))
    density = jnp.exp(-0.5 * values * values) * (1.0 / math.sqrt(2.0 * math.pi))
    return (values * normal_cdf, normal_cdf + values * density)


LANES = 128
SUBLANES = 8


def slot_rows(ref, lane, row, start, count):
    return ref[lane, row, pl.ds(start, SUBLANES, stride=count), :]


def spread_weights(weight_ref, spread_ref):
    for lane in range(spread_ref.shape[0]):
        for tap in range(49):
            row = weight_ref[tap // 7, tap % 7 : tap % 7 + 1, lane * LANES : (lane + 1) * LANES]
            spread_ref[lane, tap] = jnp.broadcast_to(row.astype(jnp.float32), (SUBLANES, LANES))


def split_lanes(source_ref, wide_ref):
    rows = source_ref.shape[0]

    def body(row, carry):
        for lane in range(wide_ref.shape[0]):
            wide_ref[lane, row] = source_ref[row, :, lane * LANES : (lane + 1) * LANES].astype(
                jnp.float32
            )
        return carry

    lax.fori_loop(0, rows, body, 0)


def main_kernel(
    scale_factor,
    core_ref,
    padded_ref,
    fields_ref,
    cot_ref,
    dw_ref,
    dw_bias_ref,
    gain_ref,
    offset_ref,
    b_project_ref,
    b_expand_ref,
    w_expand_ref,
    w_project_ref,
    out_ref,
    dconv_ref,
    keep_ref,
    give_ref,
    small_ref,
    wide_ref,
    spread_ref,
    conv_ref,
    expand_ref,
    project_ref,
):
    tiles = wide_ref.shape[0]
    rows = conv_ref.shape[1]
    cols = conv_ref.shape[2]
    chans = tiles * LANES
    slots = cols // SUBLANES
    hidden_units = w_expand_ref.shape[1]
    pieces = hidden_units // chans
    block_rows = 8
    blocks = rows // block_rows
    cells = block_rows * cols
    spread_weights(dw_ref, spread_ref)
    split_lanes(padded_ref, wide_ref)

    def conv_block(at, carry):
        lane, start = at // (rows // 4), (at % (rows // 4)) * 4
        totals = [[jnp.zeros((SUBLANES, LANES), jnp.float32)] * slots for unused in range(4)]
        for row in range(10):
            loaded = [
                slot_rows(wide_ref, lane, start + row, place, slots) for place in range(slots + 6)
            ]
            for row_off in range(7):
                to = row - row_off
                if 0 <= to < 4:
                    for col_off in range(7):
                        weight = spread_ref[lane, row_off * 7 + col_off]
                        for slot in range(slots):
                            totals[to][slot] = totals[to][slot] + weight * loaded[slot + col_off]
        for to in range(4):
            for slot in range(slots):
                conv_ref[lane, start + to, pl.ds(slot, SUBLANES, stride=slots), :] = totals[to][slot]
        return carry

    lax.fori_loop(0, tiles * (rows // 4), conv_block, 0)

    expand_ref[...] = jnp.zeros_like(expand_ref)
    project_ref[...] = jnp.zeros_like(project_ref)
    small_ref[...] = jnp.zeros_like(small_ref)
    dw_bias, gain, offset, b_project = (
        ref[...].astype(jnp.float32).reshape(1, chans)
        for ref in (dw_bias_ref, gain_ref, offset_ref, b_project_ref)
    )
    b_expand = b_expand_ref[...].astype(jnp.float32).reshape(1, hidden_units)

    def mlp_block(block, carry):
        row = block * block_rows
        conv = jnp.concatenate(
            [conv_ref[lane, pl.ds(row, block_rows)].reshape(cells, LANES) for lane in range(tiles)],
            axis=1,
        )
        conv = conv + dw_bias
        removed = conv - jnp.mean(conv, axis=-1, keepdims=True)
        deviation = lax.rsqrt(jnp.mean(removed * removed, axis=-1, keepdims=True) + EPS)
        xhat = removed * deviation
        normed = (xhat * gain + offset).astype(jnp.bfloat16)
        cot = cot_ref[pl.ds(block * cells, cells), :]
        branch = jnp.zeros((cells, chans), jnp.float32)
        d_normed = jnp.zeros((cells, chans), jnp.float32)
        for piece in range(pieces):
            part = slice(piece * chans, (piece + 1) * chans)
            w_in = w_expand_ref[:, part]
            w_out = w_project_ref[part, :]
            pre = jnp.dot(normed, w_in, preferred_element_type=jnp.float32)
            pre = pre + b_expand[:, part]
            active, slope = gelu_parts(pre)
            hidden = active.astype(jnp.bfloat16)
            branch = branch + jnp.dot(hidden, w_out, preferred_element_type=jnp.float32)
            d_hidden = contract(cot, w_out, 1, 1)
            d_pre_wide = d_hidden * slope
            d_pre = d_pre_wide.astype(jnp.bfloat16)
            project_ref[part, :] += contract(hidden, cot, 0, 0)
            expand_ref[part, :] += contract(normed, d_pre, 0, 0)
            small_ref[8 + piece : 9 + piece] += jnp.sum(
                d_pre.astype(jnp.float32), axis=0, keepdims=True
            )
            d_normed = d_normed + contract(d_pre, w_in, 1, 1)
        plain = fields_ref[pl.ds(block * cells, cells), :].astype(jnp.float32)
        out_ref[pl.ds(block * cells, cells), :] = (plain + (branch + b_project)).astype(jnp.bfloat16)
        small_ref[0:1] += jnp.sum(d_normed * xhat, axis=0, keepdims=True)
        small_ref[1:2] += jnp.sum(d_normed, axis=0, keepdims=True)
        small_ref[2:3] += jnp.sum(cot.astype(jnp.float32), axis=0, keepdims=True)
        scaled = d_normed * gain
        d_conv = deviation * (
            scaled
            - jnp.mean(scaled, axis=-1, keepdims=True)
            - xhat * jnp.mean(scaled * xhat, axis=-1, keepdims=True)
        )
        d_conv = d_conv.astype(jnp.bfloat16)
        dconv_ref[pl.ds(block * cells, cells), :] = d_conv
        return carry

    lax.fori_loop(0, blocks, mlp_block, 0)

    small_ref[...] = small_ref[...] * scale_factor

    def finish(mine, other):
        def body(at, carry):
            part = pl.ds(at * 64, 64)
            keep_ref[part] = mine[part] * scale_factor
            give_ref[part] = (other[part] * scale_factor).astype(jnp.bfloat16)
            return carry

        lax.fori_loop(0, hidden_units // 64, body, 0)

    @pl.when(core_ref[0] == 0)
    def first():
        finish(expand_ref, project_ref)

    @pl.when(core_ref[0] != 0)
    def second():
        finish(project_ref, expand_ref)


def contract(left, right, left_dim, right_dim):
    return lax.dot_general(
        left,
        right,
        (((left_dim,), (right_dim,)), ((), ())),
        preferred_element_type=jnp.float32,
    )


def main_pass(
    core, padded, fields, cot, dw_kernel, vectors, w_expand, w_project, scale_factor
):
    rows, cols = padded.shape[0] - 6, fields.shape[0] // (padded.shape[0] - 6)
    chans = fields.shape[1]
    hidden_units = w_expand.shape[1]
    tiles = chans // LANES
    cells = rows * cols
    pad_cols = padded.shape[1]
    return pl.pallas_call(
        functools.partial(main_kernel, scale_factor),
        out_shape=[
            jax.ShapeDtypeStruct((cells, chans), jnp.bfloat16),
            jax.ShapeDtypeStruct((cells, chans), jnp.bfloat16),
            jax.ShapeDtypeStruct((hidden_units, chans), jnp.float32),
            jax.ShapeDtypeStruct((hidden_units, chans), jnp.bfloat16),
            jax.ShapeDtypeStruct((8 + hidden_units // chans, chans), jnp.float32),
        ],
        in_specs=[pl.BlockSpec(memory_space=pltpu.SMEM)]
        + [pl.BlockSpec(memory_space=pltpu.VMEM)] * 11,
        out_specs=[pl.BlockSpec(memory_space=pltpu.VMEM)] * 5,
        scratch_shapes=[
            pltpu.VMEM((tiles, rows + 6, pad_cols, LANES), jnp.float32),
            pltpu.VMEM((tiles, 49, SUBLANES, LANES), jnp.float32),
            pltpu.VMEM((tiles, rows, cols, LANES), jnp.float32),
            pltpu.VMEM((hidden_units, chans), jnp.float32),
            pltpu.VMEM((hidden_units, chans), jnp.float32),
        ],
        compiler_params=pltpu.CompilerParams(vmem_limit_bytes=14 << 20),
        cost_estimate=pl.CostEstimate(
            flops=12 * cells * chans * hidden_units,
            bytes_accessed=8 << 20,
            transcendentals=2 * cells * hidden_units,
        ),
        name="block_main",
    )(core, padded, fields, cot, dw_kernel, *vectors, w_expand, w_project)


def taps_kernel(scale_factor, padded_ref, dconv_ref, small_ref, out_ref, wide_ref, dwide_ref, sums_ref):
    tiles, rows, cols = dwide_ref.shape[0], dwide_ref.shape[1], dwide_ref.shape[2]
    slots = cols // SUBLANES
    split_lanes(padded_ref, wide_ref)
    split_lanes(dconv_ref, dwide_ref)
    sums_ref[...] = jnp.zeros_like(sums_ref)
    for lane in range(tiles):
        lanes = slice(lane * LANES, (lane + 1) * LANES)
        for row_off in range(7):

            def kernel_row(row, totals):
                grads = [slot_rows(dwide_ref, lane, row, slot, slots) for slot in range(slots)]
                loaded = [
                    slot_rows(wide_ref, lane, row + row_off, place, slots)
                    for place in range(slots + 6)
                ]
                sums = [
                    totals[col_off] + sum(grads[slot] * loaded[slot + col_off] for slot in range(slots))
                    for col_off in range(7)
                ]
                if row_off == 0:
                    sums.append(totals[7] + sum(grads))
                return tuple(sums)

            count = 8 if row_off == 0 else 7
            zeros = tuple(jnp.zeros((SUBLANES, LANES), jnp.float32) for unused in range(count))
            totals = lax.fori_loop(0, rows, kernel_row, zeros, unroll=4)
            for col_off in range(count):
                tap = row_off * 7 + col_off if col_off < 7 else 49
                sums_ref[tap : tap + 1, lanes] = jnp.sum(totals[col_off], axis=0, keepdims=True)
    sums_ref[...] = sums_ref[...] * scale_factor
    pieces = small_ref.shape[0] - 8
    sums_ref[50:53] = small_ref[0:3]
    sums_ref[53 : 53 + pieces] = small_ref[8 : 8 + pieces]
    out_ref[...] = sums_ref[...].astype(jnp.bfloat16)


def taps_pass(padded, conv_gradient, small, scale_factor):
    rows, cols, chans = conv_gradient.shape
    tiles = chans // LANES
    height = -(-(45 + small.shape[0]) // 32) * 32
    return pl.pallas_call(
        functools.partial(taps_kernel, scale_factor),
        out_shape=jax.ShapeDtypeStruct((height, chans), jnp.bfloat16),
        in_specs=[pl.BlockSpec(memory_space=pltpu.VMEM)] * 3,
        out_specs=pl.BlockSpec(memory_space=pltpu.VMEM),
        scratch_shapes=[
            pltpu.VMEM((tiles,) + padded.shape[:2] + (LANES,), jnp.float32),
            pltpu.VMEM((tiles, rows, cols, LANES), jnp.float32),
            pltpu.VMEM((height, chans), jnp.float32),
        ],
        compiler_params=pltpu.CompilerParams(vmem_limit_bytes=6 << 20),
        cost_estimate=pl.CostEstimate(
            flops=98 * rows * cols * chans, bytes_accessed=3 << 20, transcendentals=0
        ),
        name="block_taps",
    )(padded, conv_gradient, small)


def finish_kernel(
    core_ref,
    mine_ref,
    got_ref,
    kern_ref,
    dwb_ref,
    gain_ref,
    shift_ref,
    expand_ref,
    b_expand_ref,
    project_ref,
    b_project_ref,
    sums_ref,
):
    hidden_units, chans = project_ref.shape
    pieces = hidden_units // chans
    small = slice(hidden_units, mine_ref.shape[0])
    sums_ref[...] = mine_ref[small].astype(jnp.float32) + got_ref[small].astype(jnp.float32)
    for row_off in range(7):
        kern_ref[row_off] = sums_ref[row_off * 7 : row_off * 7 + 7]
    dwb_ref[...] = sums_ref[49]
    gain_ref[...] = sums_ref[50]
    shift_ref[...] = sums_ref[51]
    b_project_ref[...] = sums_ref[52]
    for piece in range(pieces):
        b_expand_ref[piece * chans : (piece + 1) * chans] = sums_ref[53 + piece]

    def write(first_ref, second_ref):
        for piece in range(pieces):
            part = slice(piece * chans, (piece + 1) * chans)
            expand_ref[:, part] = first_ref[part].astype(jnp.float32)
            project_ref[part] = second_ref[part].astype(jnp.float32)

    @pl.when(core_ref[0] == 0)
    def first():
        write(mine_ref, got_ref)

    @pl.when(core_ref[0] != 0)
    def second():
        write(got_ref, mine_ref)


def finish_pass(core, mine, got, hidden_units):
    chans = mine.shape[1]
    one = jax.ShapeDtypeStruct((chans,), jnp.float32)
    return pl.pallas_call(
        finish_kernel,
        out_shape=[
            jax.ShapeDtypeStruct((7, 7, chans), jnp.float32),
            one,
            one,
            one,
            jax.ShapeDtypeStruct((chans, hidden_units), jnp.float32),
            jax.ShapeDtypeStruct((hidden_units,), jnp.float32),
            jax.ShapeDtypeStruct((hidden_units, chans), jnp.float32),
            one,
        ],
        in_specs=[pl.BlockSpec(memory_space=pltpu.SMEM)]
        + [pl.BlockSpec(memory_space=pltpu.VMEM)] * 2,
        out_specs=[pl.BlockSpec(memory_space=pltpu.VMEM)] * 8,
        scratch_shapes=[pltpu.VMEM((mine.shape[0] - hidden_units, chans), jnp.float32)],
        compiler_params=pltpu.CompilerParams(vmem_limit_bytes=8 << 20),
        name="block_finish",
    )(core, mine, got)


def adjoint_kernel(
    poles_ref,
    padded_ref,
    cot_ref,
    dw_ref,
    out_ref,
    wide_ref,
    spread_ref,
    edge_ref,
    sum_ref,
):
    tiles = wide_ref.shape[0]
    rows = sum_ref.shape[1]
    cols = sum_ref.shape[2]
    slots = cols // SUBLANES
    spread_weights(dw_ref, spread_ref)
    split_lanes(padded_ref, wide_ref)
    for side in range(2):
        at_pole = poles_ref[side] == 1
        for lane in range(tiles):
            for row_off in range(3):
                near = row_off if side == 0 else 6 - row_off
                for col_off in range(7):
                    plain = spread_ref[lane, (6 - near) * 7 + col_off]
                    turned = spread_ref[lane, near * 7 + col_off]
                    edge_ref[side, lane, row_off * 7 + col_off] = jnp.where(at_pole, turned, plain)

    def block_of(lane, start, first, last):
        totals = [[jnp.zeros((SUBLANES, LANES), jnp.float32)] * slots for unused in range(4)]
        for row in range(10):
            loaded = [
                slot_rows(wide_ref, lane, start + row, place, slots) for place in range(slots + 6)
            ]
            for row_off in range(7):
                to = row - row_off
                if 0 <= to < 4:
                    for col_off in range(7):
                        tap = 6 - col_off
                        if first and row < 3:
                            weight = edge_ref[0, lane, row_off * 7 + tap]
                        elif last and row >= 7:
                            weight = edge_ref[1, lane, (6 - row_off) * 7 + tap]
                        else:
                            weight = spread_ref[lane, (6 - row_off) * 7 + tap]
                        for slot in range(slots):
                            totals[to][slot] = totals[to][slot] + weight * loaded[slot + col_off]
        for to in range(4):
            for slot in range(slots):
                sum_ref[lane, start + to, pl.ds(slot, SUBLANES, stride=slots), :] = totals[to][slot]

    inner = rows // 4 - 2

    def inner_block(at, carry):
        block_of(at // inner, (1 + at % inner) * 4, False, False)
        return carry

    def edge_block(lane, carry):
        block_of(lane, 0, True, False)
        block_of(lane, rows - 4, False, True)
        return carry

    lax.fori_loop(0, tiles * inner, inner_block, 0)
    lax.fori_loop(0, tiles, edge_block, 0)

    def finish(row, carry):
        total = jnp.concatenate([sum_ref[lane, row] for lane in range(tiles)], axis=1)
        out_ref[row] = (cot_ref[row].astype(jnp.float32) + total).astype(jnp.bfloat16)
        return carry

    lax.fori_loop(0, rows, finish, 0)


def adjoint_pass(padded, cot, dw_kernel, poles):
    rows, cols, chans = cot.shape
    tiles = chans // LANES
    return pl.pallas_call(
        adjoint_kernel,
        out_shape=jax.ShapeDtypeStruct(cot.shape, jnp.bfloat16),
        in_specs=[pl.BlockSpec(memory_space=pltpu.SMEM)]
        + [pl.BlockSpec(memory_space=pltpu.VMEM)] * 3,
        out_specs=pl.BlockSpec(memory_space=pltpu.VMEM),
        scratch_shapes=[
            pltpu.VMEM((tiles, rows + 6, padded.shape[1], LANES), jnp.float32),
            pltpu.VMEM((tiles, 49, SUBLANES, LANES), jnp.float32),
            pltpu.VMEM((2, tiles, 21, SUBLANES, LANES), jnp.float32),
            pltpu.VMEM((tiles, rows, cols, LANES), jnp.float32),
        ],
        compiler_params=pltpu.CompilerParams(vmem_limit_bytes=6 << 20),
        cost_estimate=pl.CostEstimate(
            flops=98 * rows * cols * chans, bytes_accessed=3 << 20, transcendentals=0
        ),
        name="block_adjoint",
    )(poles, padded, cot, dw_kernel)


def sphere_pad(field):
    wide = lon_margins(field)
    top, bottom = lat_margins(wide)
    return jnp.concatenate([top, wide, bottom], axis=0)


def local(
    fields,
    cotangent,
    dw_kernel,
    dw_bias,
    norm_gain,
    layer_norm_offset,
    w_expand,
    b_expand,
    w_project,
    b_project,
):
    rows = fields.shape[0]
    cols = fields.shape[1]
    chans = fields.shape[2]
    scale_factor = 1.0 / math.sqrt(rows * cols * lax.axis_size("lat") * lax.axis_size("lon"))
    hidden_units = w_expand.shape[1]
    lat = lax.axis_index("lat")
    poles = jnp.stack([lat == 0, lat == lax.axis_size("lat") - 1]).astype(jnp.int32)
    core = (lat % 2).reshape(1)
    padded = sphere_pad(fields)
    block_out, conv_gradient, keep, give, small = main_pass(
        core,
        padded,
        fields.reshape(-1, chans),
        cotangent.reshape(-1, chans),
        dw_kernel,
        (dw_bias, norm_gain, layer_norm_offset, b_project, b_expand),
        w_expand,
        w_project,
        scale_factor,
    )
    block_out = block_out.reshape(fields.shape)
    conv_gradient = conv_gradient.reshape(fields.shape)
    barrier = lax.optimization_barrier
    count, exchange, bit_of = partner_steps()
    total = keep + within_pair(give).astype(jnp.float32)
    mine, outgoing = halves(total, bit_of(0))
    outgoing, taps_in = barrier((outgoing, conv_gradient))
    got = exchange(outgoing, 0)
    small = taps_pass(padded, taps_in, small, scale_factor)
    got, small, conv_gradient = barrier((got, small, conv_gradient))
    mine, outgoing = halves(mine + got.astype(jnp.float32), bit_of(1))
    outgoing, conv_gradient = barrier((outgoing, conv_gradient))
    got = exchange(outgoing, 1)
    wide = lon_margins(conv_gradient)
    payload = (mine + got.astype(jnp.float32)).astype(jnp.bfloat16)
    payload = jnp.concatenate([payload, small], axis=0)
    for at in range(2, count):
        got = exchange(payload, at)
        if at == 2:
            got, wide = barrier((got, wide))
            top, bottom = lat_margins(wide)
        payload = rounded_sum(payload, got)
    if count > 2:
        payload, top, bottom = barrier((payload, top, bottom))
    else:
        top, bottom = lat_margins(wide)
    padded_gradient = jnp.concatenate([top, wide, bottom], axis=0)
    for at in (1, 0):
        if at == 0:
            payload, padded_gradient = barrier((payload, padded_gradient))
            grad_fields = adjoint_pass(padded_gradient, cotangent, dw_kernel, poles)
        got = exchange(payload, at)
        if at == 0:
            got, grad_fields = barrier((got, grad_fields))
        own = payload.shape[0] - small.shape[0]
        low = bit_of(at) == 0
        here, there = payload[:own], got[:own]
        payload = jnp.concatenate(
            [
                jnp.where(low, here, there),
                jnp.where(low, there, here),
                rounded_sum(payload[own:], got[own:]),
            ],
            axis=0,
        )
    sum_kern, sum_dwb, sum_gn, sum_sh, sum_exp, sum_bexp, sum_proj, sum_bproj = finish_pass(
        core, payload, within_pair(payload), hidden_units
    )
    return (
        block_out,
        grad_fields,
        sum_kern,
        sum_dwb,
        sum_gn,
        sum_sh,
        sum_exp,
        sum_bexp,
        sum_proj,
        sum_bproj,
    )


def solution(mesh):
    placed = (P("lat", "lon", None), P("lat", "lon", None), P(), P(), P(), P(), P(), P(), P(), P())
    return jax.shard_map(
        local,
        mesh=mesh,
        in_specs=placed,
        out_specs=(
            P("lat", "lon", None),
            P("lat", "lon", None),
            P(),
            P(),
            P(),
            P(),
            P(),
            P(),
            P(),
            P(),
        ),
        check_vma=False,
    )
```

```python
import functools
import math

import jax
import jax.numpy as jnp
from jax import lax
from jax.experimental import pallas as pl
from jax.experimental.pallas import tpu as pltpu
from jax.sharding import PartitionSpec as P

EPS = 1e-06


def flat_pairs(target):
    lons, lats = lax.axis_size("lon"), lax.axis_size("lat")
    pairs = []
    for lon in range(lons):
        for lat in range(lats):
            to_lon, to_lat = target(lon, lat)
            pairs.append((lon * lats + lat, to_lon * lats + to_lat))
    return pairs


def send(value, target):
    return lax.ppermute(value, ("lon", "lat"), flat_pairs(target))


def lon_margins(field):
    lons = lax.axis_size("lon")
    odd = lax.axis_index("lon") % 2 == 1
    first, last = field[:, :3], field[:, -3:]
    outer = send(
        jnp.where(odd, last, first),
        lambda lon, lat: ((lon + 1) % lons if lon % 2 else (lon - 1) % lons, lat),
    )
    inner = send(jnp.where(odd, first, last), lambda lon, lat: (lon ^ 1, lat))
    west = jnp.where(odd, inner, outer)
    east = jnp.where(odd, outer, inner)
    return jnp.concatenate([west, field, east], axis=1)


def lat_margins(wide):
    lons, lats = lax.axis_size("lon"), lax.axis_size("lat")
    lat = lax.axis_index("lat")
    odd = lat % 2 == 1
    pole = (lat == 0) | (lat == lats - 1)
    first, last = wide[:3], wide[-3:]

    def beyond(lon, lat):
        if lat == 0 or lat == lats - 1:
            return ((lon + lons // 2) % lons, lat)
        return (lon, lat + 1 if lat % 2 else lat - 1)

    outgoing = jnp.where(odd, last, first)
    outgoing = jnp.where(pole, outgoing[::-1], outgoing)
    far = send(outgoing, beyond)
    near = send(jnp.where(odd, first, last), lambda lon, lat: (lon, lat ^ 1))
    north = jnp.where(odd, near, far)
    south = jnp.where(odd, far, near)
    return north, south


def axis_bits():
    lon_bits = [("lon", bit) for bit in range((lax.axis_size("lon") - 1).bit_length())]
    lat_bits = [("lat", bit) for bit in range(1, (lax.axis_size("lat") - 1).bit_length())]
    steps = []
    while lon_bits or lat_bits:
        if lon_bits:
            steps.append(lon_bits.pop(0))
        if lat_bits:
            steps.append(lat_bits.pop(0))
    return steps


def flip(place, step):
    lon, lat = place
    axis, bit = step
    return (lon ^ (1 << bit), lat) if axis == "lon" else (lon, lat ^ (1 << bit))


def partner_steps():
    core = lax.axis_index("lat") % 2
    steps = axis_bits()
    other = list(steps)
    for at in range(0, len(steps) - 1, 2):
        other[at], other[at + 1] = other[at + 1], other[at]

    def exchange(value, at):
        return send(value, lambda lon, lat: flip((lon, lat), (other if lat % 2 else steps)[at]))

    def order(first):
        high, low = (
            lax.shift_right_logical(lax.axis_index(axis), bit) & 1 for axis, bit in first[:2]
        )
        return 2 * high + low

    own, pair = order(steps), order(other)
    place = jnp.stack([core, jnp.where(core == 0, own, pair), jnp.where(core == 0, pair, own)])
    return len(steps), exchange, place.astype(jnp.int32)


def within_pair(value):
    return send(value, lambda lon, lat: (lon, lat ^ 1))


def halves(held, got):
    half = held.shape[0] // 2
    mine = held[:half] + got[:half].astype(jnp.float32)
    return mine, (held[half:] + got[half:].astype(jnp.float32)).astype(jnp.bfloat16)


def rounded_sum(left, right):
    return (left.astype(jnp.float32) + right.astype(jnp.float32)).astype(jnp.bfloat16)


def gelu_parts(values):
    normal_cdf = 0.5 * (1.0 + jax.scipy.special.erf(values * (1.0 / math.sqrt(2.0))))
    density = jnp.exp(-0.5 * values * values) * (1.0 / math.sqrt(2.0 * math.pi))
    return (values * normal_cdf, normal_cdf + values * density)


LANES = 128
SUBLANES = 8


def slot_rows(ref, lane, row, start, count):
    return ref[lane, row, pl.ds(start, SUBLANES, stride=count), :]


def spread_weights(weight_ref, spread_ref):
    for lane in range(spread_ref.shape[0]):
        for tap in range(49):
            row = weight_ref[tap // 7, tap % 7 : tap % 7 + 1, lane * LANES : (lane + 1) * LANES]
            spread_ref[lane, tap] = jnp.broadcast_to(row.astype(jnp.float32), (SUBLANES, LANES))


def split_lanes(source_ref, wide_ref, start=0, to=0, count=None):
    count = source_ref.shape[0] if count is None else count

    def body(row, carry):
        for lane in range(wide_ref.shape[0]):
            wide_ref[lane, to + row] = source_ref[
                start + row, :, lane * LANES : (lane + 1) * LANES
            ].astype(jnp.float32)
        return carry

    lax.fori_loop(0, count, body, 0)


def split_padded(top_ref, wide_ref, bottom_ref, out_ref):
    split_lanes(top_ref, out_ref)
    split_lanes(wide_ref, out_ref, to=3)
    split_lanes(bottom_ref, out_ref, to=3 + wide_ref.shape[0])


def window_sums(source_ref, lane, start, weight_of):
    slots = (source_ref.shape[2] - 6) // SUBLANES
    totals = [[jnp.zeros((SUBLANES, LANES), jnp.float32)] * slots for unused in range(4)]
    for row in range(10):
        loaded = [
            slot_rows(source_ref, lane, start + row, place, slots) for place in range(slots + 6)
        ]
        for row_off in range(7):
            to = row - row_off
            if 0 <= to < 4:
                for col_off in range(7):
                    weight = weight_of(row, row_off, col_off)
                    for slot in range(slots):
                        totals[to][slot] = totals[to][slot] + weight * loaded[slot + col_off]
    return totals


def store_sums(totals, out_ref, lane, start):
    slots = len(totals[0])
    for to in range(4):
        for slot in range(slots):
            out_ref[lane, start + to, pl.ds(slot, SUBLANES, stride=slots), :] = totals[to][slot]


def inner_conv_kernel(wide_ref, dw_ref, out_ref, split_ref, spread_ref):
    tiles, rows = out_ref.shape[0], out_ref.shape[1]
    spread_weights(dw_ref, spread_ref)
    split_lanes(wide_ref, split_ref)

    def body(at, carry):
        lane, start = at // (rows // 4), (at % (rows // 4)) * 4
        totals = window_sums(
            split_ref, lane, start + 1, lambda row, row_off, col_off: spread_ref[lane, row_off * 7 + col_off]
        )
        store_sums(totals, out_ref, lane, start)
        return carry

    lax.fori_loop(0, tiles * (rows // 4), body, 0)


def inner_conv(wide, dw_kernel):
    rows, chans = wide.shape[0], wide.shape[2]
    cols = wide.shape[1] - 6
    tiles = chans // LANES
    return pl.pallas_call(
        inner_conv_kernel,
        out_shape=jax.ShapeDtypeStruct((tiles, rows - 8, cols, LANES), jnp.float32),
        in_specs=[pl.BlockSpec(memory_space=pltpu.VMEM)] * 2,
        out_specs=pl.BlockSpec(memory_space=pltpu.VMEM),
        scratch_shapes=[
            pltpu.VMEM((tiles,) + wide.shape[:2] + (LANES,), jnp.float32),
            pltpu.VMEM((tiles, 49, SUBLANES, LANES), jnp.float32),
        ],
        compiler_params=pltpu.CompilerParams(vmem_limit_bytes=6 << 20),
        cost_estimate=pl.CostEstimate(
            flops=98 * rows * cols * chans, bytes_accessed=2 << 20, transcendentals=0
        ),
        name="block_inner_conv",
    )(wide, dw_kernel)


def main_kernel(
    scale_factor,
    place_ref,
    top_ref,
    wide_ref,
    bottom_ref,
    inner_ref,
    fields_ref,
    cot_ref,
    dw_ref,
    dw_bias_ref,
    gain_ref,
    offset_ref,
    b_project_ref,
    b_expand_ref,
    w_expand_ref,
    w_project_ref,
    out_ref,
    dconv_ref,
    keep_ref,
    give_ref,
    small_ref,
    split_ref,
    spread_ref,
    edge_ref,
    expand_ref,
    project_ref,
):
    tiles, inner_rows, cols = inner_ref.shape[:3]
    rows = inner_rows + 8
    chans = tiles * LANES
    hidden_units = w_expand_ref.shape[1]
    pieces = hidden_units // chans
    spread_weights(dw_ref, spread_ref)
    split_lanes(top_ref, split_ref)
    split_lanes(wide_ref, split_ref, to=3, count=7)
    split_lanes(wide_ref, split_ref, start=rows - 7, to=10, count=7)
    split_lanes(bottom_ref, split_ref, to=17)

    def conv_edge(at, carry):
        lane, side = at // 2, at % 2
        totals = window_sums(
            split_ref,
            lane,
            side * 10,
            lambda row, row_off, col_off: spread_ref[lane, row_off * 7 + col_off],
        )
        store_sums(totals, edge_ref, lane, side * 4)
        return carry

    lax.fori_loop(0, tiles * 2, conv_edge, 0)
    small_ref[...] = jnp.zeros_like(small_ref)
    dw_bias, gain, offset, b_project = (
        ref[...].astype(jnp.float32).reshape(1, chans)
        for ref in (dw_bias_ref, gain_ref, offset_ref, b_project_ref)
    )
    b_expand = b_expand_ref[...].astype(jnp.float32).reshape(1, hidden_units)

    conv = jnp.concatenate(
        [
            jnp.concatenate(
                [edge_ref[lane, :4], inner_ref[lane], edge_ref[lane, 4:]], axis=0
            ).reshape(rows * cols, LANES)
            for lane in range(tiles)
        ],
        axis=1,
    )
    conv = conv + dw_bias
    removed = conv - jnp.mean(conv, axis=-1, keepdims=True)
    deviation = lax.rsqrt(jnp.mean(removed * removed, axis=-1, keepdims=True) + EPS)
    xhat = removed * deviation
    normed = (xhat * gain + offset).astype(jnp.bfloat16)
    cot = cot_ref[...]
    branch = jnp.zeros((rows * cols, chans), jnp.float32)
    d_normed = jnp.zeros((rows * cols, chans), jnp.float32)
    for piece in range(pieces):
        part = slice(piece * chans, (piece + 1) * chans)
        w_in = w_expand_ref[:, part]
        w_out = w_project_ref[part, :]
        pre = jnp.dot(normed, w_in, preferred_element_type=jnp.float32)
        pre = pre + b_expand[:, part]
        active, slope = gelu_parts(pre)
        hidden = active.astype(jnp.bfloat16)
        branch = branch + jnp.dot(hidden, w_out, preferred_element_type=jnp.float32)
        d_hidden = contract(cot, w_out, 1, 1)
        d_pre_wide = d_hidden * slope
        d_pre = d_pre_wide.astype(jnp.bfloat16)
        project_ref[part, :] = contract(hidden, cot, 0, 0)
        expand_ref[part, :] = contract(normed, d_pre, 0, 0)
        small_ref[8 + piece : 9 + piece] = jnp.sum(
            d_pre.astype(jnp.float32), axis=0, keepdims=True
        )
        d_normed = d_normed + contract(d_pre, w_in, 1, 1)
    plain = fields_ref[...].astype(jnp.float32)
    out_ref[...] = (plain + (branch + b_project)).astype(jnp.bfloat16)
    small_ref[0:1] = jnp.sum(d_normed * xhat, axis=0, keepdims=True)
    small_ref[1:2] = jnp.sum(d_normed, axis=0, keepdims=True)
    small_ref[2:3] = jnp.sum(cot.astype(jnp.float32), axis=0, keepdims=True)
    scaled = d_normed * gain
    d_conv = deviation * (
        scaled
        - jnp.mean(scaled, axis=-1, keepdims=True)
        - xhat * jnp.mean(scaled * xhat, axis=-1, keepdims=True)
    )
    d_conv = d_conv.astype(jnp.bfloat16)
    dconv_ref[...] = d_conv
    small_ref[...] = small_ref[...] * scale_factor
    quarter = hidden_units // 4

    def finish(mine, other):
        for at in range(4):
            part = slice(at * quarter, (at + 1) * quarter)
            here = pl.multiple_of((at ^ place_ref[1]) * quarter, quarter)
            there = pl.multiple_of((at ^ place_ref[2]) * quarter, quarter)
            keep_ref[pl.ds(here, quarter)] = mine[part] * scale_factor
            give_ref[pl.ds(there, quarter)] = (other[part] * scale_factor).astype(jnp.bfloat16)

    @pl.when(place_ref[0] == 0)
    def first():
        finish(expand_ref, project_ref)

    @pl.when(place_ref[0] != 0)
    def second():
        finish(project_ref, expand_ref)


def contract(left, right, left_dim, right_dim):
    return lax.dot_general(
        left,
        right,
        (((left_dim,), (right_dim,)), ((), ())),
        preferred_element_type=jnp.float32,
    )


def main_pass(
    place, top, wide, bottom, inner, fields, cot, dw_kernel, vectors, w_expand, w_project, scale_factor
):
    rows, cols = wide.shape[0], wide.shape[1] - 6
    chans = fields.shape[1]
    hidden_units = w_expand.shape[1]
    tiles = chans // LANES
    cells = rows * cols
    return pl.pallas_call(
        functools.partial(main_kernel, scale_factor),
        out_shape=[
            jax.ShapeDtypeStruct((cells, chans), jnp.bfloat16),
            jax.ShapeDtypeStruct((cells, chans), jnp.bfloat16),
            jax.ShapeDtypeStruct((hidden_units, chans), jnp.float32),
            jax.ShapeDtypeStruct((hidden_units, chans), jnp.bfloat16),
            jax.ShapeDtypeStruct((8 + hidden_units // chans, chans), jnp.float32),
        ],
        in_specs=[pl.BlockSpec(memory_space=pltpu.SMEM)]
        + [pl.BlockSpec(memory_space=pltpu.VMEM)] * 14,
        out_specs=[pl.BlockSpec(memory_space=pltpu.VMEM)] * 5,
        scratch_shapes=[
            pltpu.VMEM((tiles, 20, wide.shape[1], LANES), jnp.float32),
            pltpu.VMEM((tiles, 49, SUBLANES, LANES), jnp.float32),
            pltpu.VMEM((tiles, 8, cols, LANES), jnp.float32),
            pltpu.VMEM((hidden_units, chans), jnp.float32),
            pltpu.VMEM((hidden_units, chans), jnp.float32),
        ],
        compiler_params=pltpu.CompilerParams(vmem_limit_bytes=28 << 20),
        cost_estimate=pl.CostEstimate(
            flops=12 * cells * chans * hidden_units,
            bytes_accessed=8 << 20,
            transcendentals=2 * cells * hidden_units,
        ),
        name="block_main",
    )(place, top, wide, bottom, inner, fields, cot, dw_kernel, *vectors, w_expand, w_project)


def taps_kernel(
    scale_factor,
    top_ref,
    band_ref,
    bottom_ref,
    dconv_ref,
    small_ref,
    out_ref,
    wide_ref,
    dwide_ref,
    sums_ref,
):
    tiles, rows, cols = dwide_ref.shape[0], dwide_ref.shape[1], dwide_ref.shape[2]
    slots = cols // SUBLANES
    split_padded(top_ref, band_ref, bottom_ref, wide_ref)
    split_lanes(dconv_ref, dwide_ref)
    sums_ref[...] = jnp.zeros_like(sums_ref)
    for lane in range(tiles):
        lanes = slice(lane * LANES, (lane + 1) * LANES)
        for row_off in range(7):

            def kernel_row(row, totals):
                grads = [slot_rows(dwide_ref, lane, row, slot, slots) for slot in range(slots)]
                loaded = [
                    slot_rows(wide_ref, lane, row + row_off, place, slots)
                    for place in range(slots + 6)
                ]
                sums = [
                    totals[col_off] + sum(grads[slot] * loaded[slot + col_off] for slot in range(slots))
                    for col_off in range(7)
                ]
                if row_off == 0:
                    sums.append(totals[7] + sum(grads))
                return tuple(sums)

            count = 8 if row_off == 0 else 7
            zeros = tuple(jnp.zeros((SUBLANES, LANES), jnp.float32) for unused in range(count))
            totals = lax.fori_loop(0, rows, kernel_row, zeros, unroll=4)
            for col_off in range(count):
                tap = row_off * 7 + col_off if col_off < 7 else 49
                sums_ref[tap : tap + 1, lanes] = jnp.sum(totals[col_off], axis=0, keepdims=True)
    sums_ref[...] = sums_ref[...] * scale_factor
    pieces = small_ref.shape[0] - 8
    sums_ref[50:53] = small_ref[0:3]
    sums_ref[53 : 53 + pieces] = small_ref[8 : 8 + pieces]
    out_ref[...] = sums_ref[...].astype(jnp.bfloat16)


def taps_pass(top, wide, bottom, conv_gradient, small, scale_factor):
    rows, cols, chans = conv_gradient.shape
    tiles = chans // LANES
    height = -(-(45 + small.shape[0]) // 32) * 32
    return pl.pallas_call(
        functools.partial(taps_kernel, scale_factor),
        out_shape=jax.ShapeDtypeStruct((height, chans), jnp.bfloat16),
        in_specs=[pl.BlockSpec(memory_space=pltpu.VMEM)] * 5,
        out_specs=pl.BlockSpec(memory_space=pltpu.VMEM),
        scratch_shapes=[
            pltpu.VMEM((tiles, rows + 6, cols + 6, LANES), jnp.float32),
            pltpu.VMEM((tiles, rows, cols, LANES), jnp.float32),
            pltpu.VMEM((height, chans), jnp.float32),
        ],
        compiler_params=pltpu.CompilerParams(vmem_limit_bytes=6 << 20),
        cost_estimate=pl.CostEstimate(
            flops=98 * rows * cols * chans, bytes_accessed=3 << 20, transcendentals=0
        ),
        name="block_taps",
    )(top, wide, bottom, conv_gradient, small)


def finish_kernel(
    place_ref,
    mine_ref,
    got_ref,
    kern_ref,
    dwb_ref,
    gain_ref,
    shift_ref,
    expand_ref,
    b_expand_ref,
    project_ref,
    b_project_ref,
    sums_ref,
):
    hidden_units, chans = project_ref.shape
    pieces = hidden_units // chans
    small = slice(hidden_units, mine_ref.shape[0])
    sums_ref[...] = mine_ref[small].astype(jnp.float32) + got_ref[small].astype(jnp.float32)
    for row_off in range(7):
        kern_ref[row_off] = sums_ref[row_off * 7 : row_off * 7 + 7]
    dwb_ref[...] = sums_ref[49]
    gain_ref[...] = sums_ref[50]
    shift_ref[...] = sums_ref[51]
    b_project_ref[...] = sums_ref[52]
    for piece in range(pieces):
        b_expand_ref[piece * chans : (piece + 1) * chans] = sums_ref[53 + piece]

    def write(first_ref, first_order, second_ref, second_order):
        for at in range(pieces):
            part = slice(at * chans, (at + 1) * chans)
            columns = pl.multiple_of((at ^ first_order) * chans, chans)
            expand_ref[:, pl.ds(columns, chans)] = first_ref[part].astype(jnp.float32)
            to = pl.multiple_of((at ^ second_order) * chans, chans)
            project_ref[pl.ds(to, chans)] = second_ref[part].astype(jnp.float32)

    @pl.when(place_ref[0] == 0)
    def first():
        write(mine_ref, place_ref[1], got_ref, place_ref[2])

    @pl.when(place_ref[0] != 0)
    def second():
        write(got_ref, place_ref[2], mine_ref, place_ref[1])


def finish_pass(place, mine, got, hidden_units):
    chans = mine.shape[1]
    one = jax.ShapeDtypeStruct((chans,), jnp.float32)
    return pl.pallas_call(
        finish_kernel,
        out_shape=[
            jax.ShapeDtypeStruct((7, 7, chans), jnp.float32),
            one,
            one,
            one,
            jax.ShapeDtypeStruct((chans, hidden_units), jnp.float32),
            jax.ShapeDtypeStruct((hidden_units,), jnp.float32),
            jax.ShapeDtypeStruct((hidden_units, chans), jnp.float32),
            one,
        ],
        in_specs=[pl.BlockSpec(memory_space=pltpu.SMEM)]
        + [pl.BlockSpec(memory_space=pltpu.VMEM)] * 2,
        out_specs=[pl.BlockSpec(memory_space=pltpu.VMEM)] * 8,
        scratch_shapes=[pltpu.VMEM((mine.shape[0] - hidden_units, chans), jnp.float32)],
        compiler_params=pltpu.CompilerParams(vmem_limit_bytes=8 << 20),
        name="block_finish",
    )(place, mine, got)


def adjoint_kernel(
    poles_ref,
    top_ref,
    band_ref,
    bottom_ref,
    cot_ref,
    dw_ref,
    out_ref,
    wide_ref,
    spread_ref,
    edge_ref,
    sum_ref,
):
    tiles = wide_ref.shape[0]
    rows = sum_ref.shape[1]
    spread_weights(dw_ref, spread_ref)
    split_padded(top_ref, band_ref, bottom_ref, wide_ref)
    for side in range(2):
        at_pole = poles_ref[side] == 1
        for lane in range(tiles):
            for row_off in range(3):
                near = row_off if side == 0 else 6 - row_off
                for col_off in range(7):
                    plain = spread_ref[lane, (6 - near) * 7 + col_off]
                    turned = spread_ref[lane, near * 7 + col_off]
                    edge_ref[side, lane, row_off * 7 + col_off] = jnp.where(at_pole, turned, plain)

    def block_of(lane, start, first, last):
        def weight_of(row, row_off, col_off):
            if first and row < 3:
                return edge_ref[0, lane, row_off * 7 + 6 - col_off]
            if last and row >= 7:
                return edge_ref[1, lane, (6 - row_off) * 7 + 6 - col_off]
            return spread_ref[lane, (6 - row_off) * 7 + 6 - col_off]

        store_sums(window_sums(wide_ref, lane, start, weight_of), sum_ref, lane, start)

    inner = rows // 4 - 2

    def inner_block(at, carry):
        block_of(at // inner, (1 + at % inner) * 4, False, False)
        return carry

    def edge_block(lane, carry):
        block_of(lane, 0, True, False)
        block_of(lane, rows - 4, False, True)
        return carry

    lax.fori_loop(0, tiles * inner, inner_block, 0)
    lax.fori_loop(0, tiles, edge_block, 0)

    def finish(row, carry):
        total = jnp.concatenate([sum_ref[lane, row] for lane in range(tiles)], axis=1)
        out_ref[row] = (cot_ref[row].astype(jnp.float32) + total).astype(jnp.bfloat16)
        return carry

    lax.fori_loop(0, rows, finish, 0)


def adjoint_pass(top, wide, bottom, cot, dw_kernel, poles):
    rows, cols, chans = cot.shape
    tiles = chans // LANES
    return pl.pallas_call(
        adjoint_kernel,
        out_shape=jax.ShapeDtypeStruct(cot.shape, jnp.bfloat16),
        in_specs=[pl.BlockSpec(memory_space=pltpu.SMEM)]
        + [pl.BlockSpec(memory_space=pltpu.VMEM)] * 5,
        out_specs=pl.BlockSpec(memory_space=pltpu.VMEM),
        scratch_shapes=[
            pltpu.VMEM((tiles, rows + 6, cols + 6, LANES), jnp.float32),
            pltpu.VMEM((tiles, 49, SUBLANES, LANES), jnp.float32),
            pltpu.VMEM((2, tiles, 21, SUBLANES, LANES), jnp.float32),
            pltpu.VMEM((tiles, rows, cols, LANES), jnp.float32),
        ],
        compiler_params=pltpu.CompilerParams(vmem_limit_bytes=6 << 20),
        cost_estimate=pl.CostEstimate(
            flops=98 * rows * cols * chans, bytes_accessed=3 << 20, transcendentals=0
        ),
        name="block_adjoint",
    )(poles, top, wide, bottom, cot, dw_kernel)


def local(
    fields,
    cotangent,
    dw_kernel,
    dw_bias,
    norm_gain,
    layer_norm_offset,
    w_expand,
    b_expand,
    w_project,
    b_project,
):
    rows = fields.shape[0]
    cols = fields.shape[1]
    chans = fields.shape[2]
    scale_factor = 1.0 / math.sqrt(rows * cols * lax.axis_size("lat") * lax.axis_size("lon"))
    hidden_units = w_expand.shape[1]
    lat = lax.axis_index("lat")
    poles = jnp.stack([lat == 0, lat == lax.axis_size("lat") - 1]).astype(jnp.int32)
    count, exchange, place = partner_steps()
    wide = lon_margins(fields)
    inner = inner_conv(wide, dw_kernel)
    edges = lat_margins(wide)
    block_out, conv_gradient, keep, give, small = main_pass(
        place,
        edges[0],
        wide,
        edges[1],
        inner,
        fields.reshape(-1, chans),
        cotangent.reshape(-1, chans),
        dw_kernel,
        (dw_bias, norm_gain, layer_norm_offset, b_project, b_expand),
        w_expand,
        w_project,
        scale_factor,
    )
    block_out = block_out.reshape(fields.shape)
    conv_gradient = conv_gradient.reshape(fields.shape)
    barrier = lax.optimization_barrier
    mine, outgoing = halves(keep, within_pair(give))
    outgoing, taps_in = barrier((outgoing, conv_gradient))
    got = exchange(outgoing, 0)
    small = taps_pass(edges[0], wide, edges[1], taps_in, small, scale_factor)
    got, small, conv_gradient = barrier((got, small, conv_gradient))
    mine, outgoing = halves(mine, got)
    outgoing, conv_gradient = barrier((outgoing, conv_gradient))
    got = exchange(outgoing, 1)
    wide = lon_margins(conv_gradient)
    payload = (mine + got.astype(jnp.float32)).astype(jnp.bfloat16)
    payload = jnp.concatenate([payload, small], axis=0)
    for at in range(2, count):
        got = exchange(payload, at)
        if at == 2:
            got, wide = barrier((got, wide))
            top, bottom = lat_margins(wide)
        payload = rounded_sum(payload, got)
    if count > 2:
        payload, top, bottom = barrier((payload, top, bottom))
    else:
        top, bottom = lat_margins(wide)
    for at in (1, 0):
        if at == 0:
            payload, top, wide, bottom = barrier((payload, top, wide, bottom))
            grad_fields = adjoint_pass(top, wide, bottom, cotangent, dw_kernel, poles)
        got = exchange(payload, at)
        if at == 0:
            got, grad_fields = barrier((got, grad_fields))
        own = payload.shape[0] - small.shape[0]
        payload = jnp.concatenate(
            [payload[:own], got[:own], rounded_sum(payload[own:], got[own:])], axis=0
        )
    sum_kern, sum_dwb, sum_gn, sum_sh, sum_exp, sum_bexp, sum_proj, sum_bproj = finish_pass(
        place, payload, within_pair(payload), hidden_units
    )
    return (
        block_out,
        grad_fields,
        sum_kern,
        sum_dwb,
        sum_gn,
        sum_sh,
        sum_exp,
        sum_bexp,
        sum_proj,
        sum_bproj,
    )


def solution(mesh):
    placed = (P("lat", "lon", None), P("lat", "lon", None), P(), P(), P(), P(), P(), P(), P(), P())
    return jax.shard_map(
        local,
        mesh=mesh,
        in_specs=placed,
        out_specs=(
            P("lat", "lon", None),
            P("lat", "lon", None),
            P(),
            P(),
            P(),
            P(),
            P(),
            P(),
            P(),
            P(),
        ),
        check_vma=False,
    )
```

```python
import functools
import math

import jax
import jax.numpy as jnp
from jax import lax
from jax.experimental import pallas as pl
from jax.experimental.pallas import tpu as pltpu
from jax.sharding import PartitionSpec as P

EPS = 1e-06


def flat_pairs(target):
    lons, lats = lax.axis_size("lon"), lax.axis_size("lat")
    pairs = []
    for lon in range(lons):
        for lat in range(lats):
            to_lon, to_lat = target(lon, lat)
            pairs.append((lon * lats + lat, to_lon * lats + to_lat))
    return pairs


def send(value, target):
    return lax.ppermute(value, ("lon", "lat"), flat_pairs(target))


def lon_margins(field):
    lons = lax.axis_size("lon")
    odd = lax.axis_index("lon") % 2 == 1
    first, last = field[:, :3], field[:, -3:]
    outer = send(
        jnp.where(odd, last, first),
        lambda lon, lat: ((lon + 1) % lons if lon % 2 else (lon - 1) % lons, lat),
    )
    inner = send(jnp.where(odd, first, last), lambda lon, lat: (lon ^ 1, lat))
    west = jnp.where(odd, inner, outer)
    east = jnp.where(odd, outer, inner)
    return west, field, east


def lat_margins(band):
    lons, lats = lax.axis_size("lon"), lax.axis_size("lat")
    lat = lax.axis_index("lat")
    odd = lat % 2 == 1
    pole = (lat == 0) | (lat == lats - 1)
    first = jnp.concatenate([part[:3] for part in band], axis=1)
    last = jnp.concatenate([part[-3:] for part in band], axis=1)

    def beyond(lon, lat):
        if lat == 0 or lat == lats - 1:
            return ((lon + lons // 2) % lons, lat)
        return (lon, lat + 1 if lat % 2 else lat - 1)

    outgoing = jnp.where(odd, last, first)
    outgoing = jnp.where(pole, outgoing[::-1], outgoing)
    far = send(outgoing, beyond)
    near = send(jnp.where(odd, first, last), lambda lon, lat: (lon, lat ^ 1))
    north = jnp.where(odd, near, far)
    south = jnp.where(odd, far, near)
    return north, south


def axis_bits():
    lon_bits = [("lon", bit) for bit in range((lax.axis_size("lon") - 1).bit_length())]
    lat_bits = [("lat", bit) for bit in range(1, (lax.axis_size("lat") - 1).bit_length())]
    steps = []
    while lon_bits or lat_bits:
        if lon_bits:
            steps.append(lon_bits.pop(0))
        if lat_bits:
            steps.append(lat_bits.pop(0))
    return steps


def flip(place, step):
    lon, lat = place
    axis, bit = step
    return (lon ^ (1 << bit), lat) if axis == "lon" else (lon, lat ^ (1 << bit))


def partner_steps():
    core = lax.axis_index("lat") % 2
    steps = axis_bits()
    other = list(steps)
    for at in range(0, len(steps) - 1, 2):
        other[at], other[at + 1] = other[at + 1], other[at]

    def exchange(value, at):
        return send(value, lambda lon, lat: flip((lon, lat), (other if lat % 2 else steps)[at]))

    def order(first):
        high, low = (
            lax.shift_right_logical(lax.axis_index(axis), bit) & 1 for axis, bit in first[:2]
        )
        return 2 * high + low

    own, pair = order(steps), order(other)
    place = jnp.stack([core, jnp.where(core == 0, own, pair), jnp.where(core == 0, pair, own)])
    return len(steps), exchange, place.astype(jnp.int32)


def within_pair(value):
    return send(value, lambda lon, lat: (lon, lat ^ 1))


def widened_sum(*terms):
    total = terms[0].astype(jnp.float32)
    for term in terms[1:]:
        total = total + term.astype(jnp.float32)
    return total


def rounded_sum(left, right):
    return (left.astype(jnp.float32) + right.astype(jnp.float32)).astype(jnp.bfloat16)


def gelu_parts(values):
    normal_cdf = 0.5 * (1.0 + jax.scipy.special.erf(values * (1.0 / math.sqrt(2.0))))
    density = jnp.exp(-0.5 * values * values) * (1.0 / math.sqrt(2.0 * math.pi))
    return (values * normal_cdf, normal_cdf + values * density)


LANES = 128
SUBLANES = 8


def slot_rows(ref, lane, row, start, count):
    return ref[lane, row, pl.ds(start, SUBLANES, stride=count), :]


def spread_weights(weight_ref, spread_ref):
    for lane in range(spread_ref.shape[0]):
        for tap in range(49):
            row = weight_ref[tap // 7, tap % 7 : tap % 7 + 1, lane * LANES : (lane + 1) * LANES]
            spread_ref[lane, tap] = jnp.broadcast_to(row.astype(jnp.float32), (SUBLANES, LANES))


def split_lanes(source_ref, wide_ref, start=0, to=0, count=None):
    count = source_ref.shape[0] if count is None else count

    def body(row, carry):
        for lane in range(wide_ref.shape[0]):
            wide_ref[lane, to + row] = source_ref[
                start + row, :, lane * LANES : (lane + 1) * LANES
            ].astype(jnp.float32)
        return carry

    lax.fori_loop(0, count, body, 0)


def split_band(band_refs, out_ref, start=0, to=0, count=None):
    count = band_refs[1].shape[0] if count is None else count

    def body(row, carry):
        for lane in range(out_ref.shape[0]):
            column = 0
            for ref in band_refs:
                part = ref[start + row, :, lane * LANES : (lane + 1) * LANES]
                out_ref[lane, to + row, column : column + ref.shape[1]] = part.astype(jnp.float32)
                column += ref.shape[1]
        return carry

    lax.fori_loop(0, count, body, 0)


def split_padded(top_ref, band_refs, bottom_ref, out_ref):
    split_lanes(top_ref, out_ref)
    split_band(band_refs, out_ref, to=3)
    split_lanes(bottom_ref, out_ref, to=3 + band_refs[1].shape[0])


def window_sums(source_ref, lane, start, weight_of):
    slots = (source_ref.shape[2] - 6) // SUBLANES
    totals = [[jnp.zeros((SUBLANES, LANES), jnp.float32)] * slots for unused in range(4)]
    for row in range(10):
        loaded = [
            slot_rows(source_ref, lane, start + row, place, slots) for place in range(slots + 6)
        ]
        for row_off in range(7):
            to = row - row_off
            if 0 <= to < 4:
                for col_off in range(7):
                    weight = weight_of(row, row_off, col_off)
                    for slot in range(slots):
                        totals[to][slot] = totals[to][slot] + weight * loaded[slot + col_off]
    return totals


def store_sums(totals, out_ref, lane, start):
    slots = len(totals[0])
    for to in range(4):
        for slot in range(slots):
            out_ref[lane, start + to, pl.ds(slot, SUBLANES, stride=slots), :] = totals[to][slot]


def inner_conv_kernel(
    flipped, west_ref, field_ref, east_ref, dw_ref, out_ref, split_ref, spread_ref
):
    tiles, rows = out_ref.shape[0], out_ref.shape[1]
    spread_weights(dw_ref, spread_ref)
    split_band((west_ref, field_ref, east_ref), split_ref)

    def body(at, carry):
        lane, start = at // (rows // 4), (at % (rows // 4)) * 4

        def weight_of(row, row_off, col_off):
            tap = row_off * 7 + col_off
            return spread_ref[lane, 48 - tap if flipped else tap]

        store_sums(window_sums(split_ref, lane, start + 1, weight_of), out_ref, lane, start)
        return carry

    lax.fori_loop(0, tiles * (rows // 4), body, 0)


def inner_conv(band, dw_kernel, flipped):
    rows, cols, chans = band[1].shape
    tiles = chans // LANES
    return pl.pallas_call(
        functools.partial(inner_conv_kernel, flipped),
        out_shape=jax.ShapeDtypeStruct((tiles, rows - 8, cols, LANES), jnp.float32),
        in_specs=[pl.BlockSpec(memory_space=pltpu.VMEM)] * 4,
        out_specs=pl.BlockSpec(memory_space=pltpu.VMEM),
        scratch_shapes=[
            pltpu.VMEM((tiles, rows, cols + 6, LANES), jnp.float32),
            pltpu.VMEM((tiles, 49, SUBLANES, LANES), jnp.float32),
        ],
        compiler_params=pltpu.CompilerParams(vmem_limit_bytes=6 << 20),
        cost_estimate=pl.CostEstimate(
            flops=98 * rows * cols * chans, bytes_accessed=2 << 20, transcendentals=0
        ),
        name="block_inner_conv",
    )(*band, dw_kernel)


def main_kernel(
    scale_factor,
    place_ref,
    top_ref,
    west_ref,
    fields_ref,
    east_ref,
    bottom_ref,
    inner_ref,
    cot_ref,
    dw_ref,
    dw_bias_ref,
    gain_ref,
    offset_ref,
    b_project_ref,
    b_expand_ref,
    w_expand_ref,
    w_project_ref,
    out_ref,
    dconv_ref,
    keep_ref,
    give_ref,
    small_ref,
    split_ref,
    spread_ref,
    edge_ref,
    expand_ref,
    project_ref,
):
    tiles, inner_rows, cols = inner_ref.shape[:3]
    rows = inner_rows + 8
    chans = tiles * LANES
    hidden_units = w_expand_ref.shape[1]
    pieces = hidden_units // chans
    spread_weights(dw_ref, spread_ref)
    split_lanes(top_ref, split_ref)
    band_refs = (west_ref, fields_ref, east_ref)
    split_band(band_refs, split_ref, to=3, count=7)
    split_band(band_refs, split_ref, start=rows - 7, to=10, count=7)
    split_lanes(bottom_ref, split_ref, to=17)

    def conv_edge(at, carry):
        lane, side = at // 2, at % 2
        totals = window_sums(
            split_ref,
            lane,
            side * 10,
            lambda row, row_off, col_off: spread_ref[lane, row_off * 7 + col_off],
        )
        store_sums(totals, edge_ref, lane, side * 4)
        return carry

    lax.fori_loop(0, tiles * 2, conv_edge, 0)
    small_ref[...] = jnp.zeros_like(small_ref)
    dw_bias, gain, offset, b_project = (
        ref[...].astype(jnp.float32).reshape(1, chans)
        for ref in (dw_bias_ref, gain_ref, offset_ref, b_project_ref)
    )
    b_expand = b_expand_ref[...].astype(jnp.float32).reshape(1, hidden_units)

    conv = jnp.concatenate(
        [
            jnp.concatenate(
                [edge_ref[lane, :4], inner_ref[lane], edge_ref[lane, 4:]], axis=0
            ).reshape(rows * cols, LANES)
            for lane in range(tiles)
        ],
        axis=1,
    )
    conv = conv + dw_bias
    removed = conv - jnp.mean(conv, axis=-1, keepdims=True)
    deviation = lax.rsqrt(jnp.mean(removed * removed, axis=-1, keepdims=True) + EPS)
    xhat = removed * deviation
    normed = (xhat * gain + offset).astype(jnp.bfloat16)
    cot = cot_ref[...]
    branch = jnp.zeros((rows * cols, chans), jnp.float32)
    d_normed = jnp.zeros((rows * cols, chans), jnp.float32)
    for piece in range(pieces):
        part = slice(piece * chans, (piece + 1) * chans)
        w_in = w_expand_ref[:, part]
        w_out = w_project_ref[part, :]
        pre = jnp.dot(normed, w_in, preferred_element_type=jnp.float32)
        pre = pre + b_expand[:, part]
        active, slope = gelu_parts(pre)
        hidden = active.astype(jnp.bfloat16)
        branch = branch + jnp.dot(hidden, w_out, preferred_element_type=jnp.float32)
        d_hidden = contract(cot, w_out, 1, 1)
        d_pre_wide = d_hidden * slope
        d_pre = d_pre_wide.astype(jnp.bfloat16)
        project_ref[part, :] = contract(hidden, cot, 0, 0)
        expand_ref[part, :] = contract(normed, d_pre, 0, 0)
        small_ref[8 + piece : 9 + piece] = jnp.sum(
            d_pre.astype(jnp.float32), axis=0, keepdims=True
        )
        d_normed = d_normed + contract(d_pre, w_in, 1, 1)
    plain = fields_ref[...].reshape(rows * cols, chans).astype(jnp.float32)
    out_ref[...] = (plain + (branch + b_project)).astype(jnp.bfloat16)
    small_ref[0:1] = jnp.sum(d_normed * xhat, axis=0, keepdims=True)
    small_ref[1:2] = jnp.sum(d_normed, axis=0, keepdims=True)
    small_ref[2:3] = jnp.sum(cot.astype(jnp.float32), axis=0, keepdims=True)
    scaled = d_normed * gain
    d_conv = deviation * (
        scaled
        - jnp.mean(scaled, axis=-1, keepdims=True)
        - xhat * jnp.mean(scaled * xhat, axis=-1, keepdims=True)
    )
    d_conv = d_conv.astype(jnp.bfloat16)
    dconv_ref[...] = d_conv
    small_ref[...] = small_ref[...] * scale_factor
    quarter = hidden_units // 4

    def finish(mine, other):
        for at in range(4):
            part = slice(at * quarter, (at + 1) * quarter)
            here = pl.multiple_of((at ^ place_ref[1]) * quarter, quarter)
            there = pl.multiple_of((at ^ place_ref[2]) * quarter, quarter)
            keep_ref[pl.ds(here, quarter)] = mine[part] * scale_factor
            give_ref[pl.ds(there, quarter)] = (other[part] * scale_factor).astype(jnp.bfloat16)

    @pl.when(place_ref[0] == 0)
    def first():
        finish(expand_ref, project_ref)

    @pl.when(place_ref[0] != 0)
    def second():
        finish(project_ref, expand_ref)


def contract(left, right, left_dim, right_dim):
    return lax.dot_general(
        left,
        right,
        (((left_dim,), (right_dim,)), ((), ())),
        preferred_element_type=jnp.float32,
    )


def main_pass(
    place, top, band, bottom, inner, cot, dw_kernel, vectors, w_expand, w_project, scale_factor
):
    rows, cols, chans = band[1].shape
    hidden_units = w_expand.shape[1]
    tiles = chans // LANES
    cells = rows * cols
    return pl.pallas_call(
        functools.partial(main_kernel, scale_factor),
        out_shape=[
            jax.ShapeDtypeStruct((cells, chans), jnp.bfloat16),
            jax.ShapeDtypeStruct((cells, chans), jnp.bfloat16),
            jax.ShapeDtypeStruct((hidden_units, chans), jnp.float32),
            jax.ShapeDtypeStruct((hidden_units, chans), jnp.bfloat16),
            jax.ShapeDtypeStruct((8 + hidden_units // chans, chans), jnp.float32),
        ],
        in_specs=[pl.BlockSpec(memory_space=pltpu.SMEM)]
        + [pl.BlockSpec(memory_space=pltpu.VMEM)] * 15,
        out_specs=[pl.BlockSpec(memory_space=pltpu.VMEM)] * 5,
        scratch_shapes=[
            pltpu.VMEM((tiles, 20, cols + 6, LANES), jnp.float32),
            pltpu.VMEM((tiles, 49, SUBLANES, LANES), jnp.float32),
            pltpu.VMEM((tiles, 8, cols, LANES), jnp.float32),
            pltpu.VMEM((hidden_units, chans), jnp.float32),
            pltpu.VMEM((hidden_units, chans), jnp.float32),
        ],
        compiler_params=pltpu.CompilerParams(vmem_limit_bytes=28 << 20),
        cost_estimate=pl.CostEstimate(
            flops=12 * cells * chans * hidden_units,
            bytes_accessed=8 << 20,
            transcendentals=2 * cells * hidden_units,
        ),
        name="block_main",
    )(place, top, *band, bottom, inner, cot, dw_kernel, *vectors, w_expand, w_project)


def taps_kernel(
    scale_factor,
    top_ref,
    west_ref,
    field_ref,
    east_ref,
    bottom_ref,
    dconv_ref,
    small_ref,
    out_ref,
    wide_ref,
    dwide_ref,
    sums_ref,
):
    tiles, rows, cols = dwide_ref.shape[0], dwide_ref.shape[1], dwide_ref.shape[2]
    slots = cols // SUBLANES
    split_padded(top_ref, (west_ref, field_ref, east_ref), bottom_ref, wide_ref)
    split_lanes(dconv_ref, dwide_ref)
    sums_ref[...] = jnp.zeros_like(sums_ref)
    for lane in range(tiles):
        lanes = slice(lane * LANES, (lane + 1) * LANES)
        for row_off in range(7):

            def kernel_row(row, totals):
                grads = [slot_rows(dwide_ref, lane, row, slot, slots) for slot in range(slots)]
                loaded = [
                    slot_rows(wide_ref, lane, row + row_off, place, slots)
                    for place in range(slots + 6)
                ]
                sums = [
                    totals[col_off] + sum(grads[slot] * loaded[slot + col_off] for slot in range(slots))
                    for col_off in range(7)
                ]
                if row_off == 0:
                    sums.append(totals[7] + sum(grads))
                return tuple(sums)

            count = 8 if row_off == 0 else 7
            zeros = tuple(jnp.zeros((SUBLANES, LANES), jnp.float32) for unused in range(count))
            totals = lax.fori_loop(0, rows, kernel_row, zeros, unroll=4)
            for col_off in range(count):
                tap = row_off * 7 + col_off if col_off < 7 else 49
                sums_ref[tap : tap + 1, lanes] = jnp.sum(totals[col_off], axis=0, keepdims=True)
    sums_ref[...] = sums_ref[...] * scale_factor
    pieces = small_ref.shape[0] - 8
    sums_ref[50:53] = small_ref[0:3]
    sums_ref[53 : 53 + pieces] = small_ref[8 : 8 + pieces]
    out_ref[...] = sums_ref[...].astype(jnp.bfloat16)


def taps_pass(top, band, bottom, conv_gradient, small, scale_factor):
    rows, cols, chans = conv_gradient.shape
    tiles = chans // LANES
    height = -(-(45 + small.shape[0]) // 32) * 32
    return pl.pallas_call(
        functools.partial(taps_kernel, scale_factor),
        out_shape=jax.ShapeDtypeStruct((height, chans), jnp.bfloat16),
        in_specs=[pl.BlockSpec(memory_space=pltpu.VMEM)] * 7,
        out_specs=pl.BlockSpec(memory_space=pltpu.VMEM),
        scratch_shapes=[
            pltpu.VMEM((tiles, rows + 6, cols + 6, LANES), jnp.float32),
            pltpu.VMEM((tiles, rows, cols, LANES), jnp.float32),
            pltpu.VMEM((height, chans), jnp.float32),
        ],
        compiler_params=pltpu.CompilerParams(vmem_limit_bytes=6 << 20),
        cost_estimate=pl.CostEstimate(
            flops=98 * rows * cols * chans, bytes_accessed=3 << 20, transcendentals=0
        ),
        name="block_taps",
    )(top, *band, bottom, conv_gradient, small)


def finish_kernel(
    place_ref,
    mine_ref,
    last_ref,
    pair_ref,
    pair_last_ref,
    kern_ref,
    dwb_ref,
    gain_ref,
    shift_ref,
    expand_ref,
    b_expand_ref,
    project_ref,
    b_project_ref,
    sums_ref,
):
    hidden_units, chans = project_ref.shape
    pieces = hidden_units // chans
    early = mine_ref.shape[0] // chans
    small = slice(hidden_units - early * chans, last_ref.shape[0])
    sums_ref[...] = last_ref[small].astype(jnp.float32) + pair_last_ref[small].astype(jnp.float32)
    for row_off in range(7):
        kern_ref[row_off] = sums_ref[row_off * 7 : row_off * 7 + 7]
    dwb_ref[...] = sums_ref[49]
    gain_ref[...] = sums_ref[50]
    shift_ref[...] = sums_ref[51]
    b_project_ref[...] = sums_ref[52]
    for piece in range(pieces):
        b_expand_ref[piece * chans : (piece + 1) * chans] = sums_ref[53 + piece]

    def write(first_refs, first_order, second_refs, second_order):
        for at in range(pieces):
            late = at >= early
            part = pl.ds((at - early if late else at) * chans, chans)
            columns = pl.multiple_of((at ^ first_order) * chans, chans)
            expand_ref[:, pl.ds(columns, chans)] = first_refs[late][part].astype(jnp.float32)
            to = pl.multiple_of((at ^ second_order) * chans, chans)
            project_ref[pl.ds(to, chans)] = second_refs[late][part].astype(jnp.float32)

    mine_refs, pair_refs = (mine_ref, last_ref), (pair_ref, pair_last_ref)

    @pl.when(place_ref[0] == 0)
    def first():
        write(mine_refs, place_ref[1], pair_refs, place_ref[2])

    @pl.when(place_ref[0] != 0)
    def second():
        write(pair_refs, place_ref[2], mine_refs, place_ref[1])


def finish_pass(place, mine, last, pair, pair_last, hidden_units):
    chans = mine.shape[1]
    one = jax.ShapeDtypeStruct((chans,), jnp.float32)
    return pl.pallas_call(
        finish_kernel,
        out_shape=[
            jax.ShapeDtypeStruct((7, 7, chans), jnp.float32),
            one,
            one,
            one,
            jax.ShapeDtypeStruct((chans, hidden_units), jnp.float32),
            jax.ShapeDtypeStruct((hidden_units,), jnp.float32),
            jax.ShapeDtypeStruct((hidden_units, chans), jnp.float32),
            one,
        ],
        in_specs=[pl.BlockSpec(memory_space=pltpu.SMEM)]
        + [pl.BlockSpec(memory_space=pltpu.VMEM)] * 4,
        out_specs=[pl.BlockSpec(memory_space=pltpu.VMEM)] * 8,
        scratch_shapes=[pltpu.VMEM((mine.shape[0] + last.shape[0] - hidden_units, chans), jnp.float32)],
        compiler_params=pltpu.CompilerParams(vmem_limit_bytes=8 << 20),
        name="block_finish",
    )(place, mine, last, pair, pair_last)


def adjoint_kernel(
    poles_ref,
    top_ref,
    west_ref,
    field_ref,
    east_ref,
    bottom_ref,
    inner_ref,
    cot_ref,
    dw_ref,
    out_ref,
    split_ref,
    spread_ref,
    edge_ref,
    sum_ref,
):
    tiles = split_ref.shape[0]
    rows = cot_ref.shape[0]
    spread_weights(dw_ref, spread_ref)
    band_refs = (west_ref, field_ref, east_ref)
    split_lanes(top_ref, split_ref)
    split_band(band_refs, split_ref, to=3, count=7)
    split_band(band_refs, split_ref, start=rows - 7, to=10, count=7)
    split_lanes(bottom_ref, split_ref, to=17)
    for side in range(2):
        at_pole = poles_ref[side] == 1
        for lane in range(tiles):
            for row_off in range(3):
                near = row_off if side == 0 else 6 - row_off
                for col_off in range(7):
                    plain = spread_ref[lane, (6 - near) * 7 + col_off]
                    turned = spread_ref[lane, near * 7 + col_off]
                    edge_ref[side, lane, row_off * 7 + col_off] = jnp.where(at_pole, turned, plain)

    def edge_block(lane, carry):
        for side in range(2):

            def weight_of(row, row_off, col_off):
                if side == 0 and row < 3:
                    return edge_ref[0, lane, row_off * 7 + 6 - col_off]
                if side == 1 and row >= 7:
                    return edge_ref[1, lane, (6 - row_off) * 7 + 6 - col_off]
                return spread_ref[lane, 48 - (row_off * 7 + col_off)]

            totals = window_sums(split_ref, lane, side * 10, weight_of)
            store_sums(totals, sum_ref, lane, side * 4)
        return carry

    lax.fori_loop(0, tiles, edge_block, 0)

    def write(ref, start, to, count):
        def body(row, carry):
            total = jnp.concatenate([ref[lane, start + row] for lane in range(tiles)], axis=1)
            out_ref[to + row] = (cot_ref[to + row].astype(jnp.float32) + total).astype(jnp.bfloat16)
            return carry

        lax.fori_loop(0, count, body, 0)

    write(sum_ref, 0, 0, 4)
    write(inner_ref, 0, 4, rows - 8)
    write(sum_ref, 4, rows - 4, 4)


def adjoint_pass(top, band, bottom, inner, cot, dw_kernel, poles):
    rows, cols, chans = cot.shape
    tiles = chans // LANES
    return pl.pallas_call(
        adjoint_kernel,
        out_shape=jax.ShapeDtypeStruct(cot.shape, jnp.bfloat16),
        in_specs=[pl.BlockSpec(memory_space=pltpu.SMEM)]
        + [pl.BlockSpec(memory_space=pltpu.VMEM)] * 8,
        out_specs=pl.BlockSpec(memory_space=pltpu.VMEM),
        scratch_shapes=[
            pltpu.VMEM((tiles, 20, cols + 6, LANES), jnp.float32),
            pltpu.VMEM((tiles, 49, SUBLANES, LANES), jnp.float32),
            pltpu.VMEM((2, tiles, 21, SUBLANES, LANES), jnp.float32),
            pltpu.VMEM((tiles, 8, cols, LANES), jnp.float32),
        ],
        compiler_params=pltpu.CompilerParams(vmem_limit_bytes=6 << 20),
        cost_estimate=pl.CostEstimate(
            flops=25 * rows * cols * chans, bytes_accessed=3 << 20, transcendentals=0
        ),
        name="block_adjoint",
    )(poles, top, *band, bottom, inner, cot, dw_kernel)


def local(
    fields,
    cotangent,
    dw_kernel,
    dw_bias,
    norm_gain,
    layer_norm_offset,
    w_expand,
    b_expand,
    w_project,
    b_project,
):
    rows = fields.shape[0]
    cols = fields.shape[1]
    chans = fields.shape[2]
    scale_factor = 1.0 / math.sqrt(rows * cols * lax.axis_size("lat") * lax.axis_size("lon"))
    hidden_units = w_expand.shape[1]
    lat = lax.axis_index("lat")
    poles = jnp.stack([lat == 0, lat == lax.axis_size("lat") - 1]).astype(jnp.int32)
    count, exchange, place = partner_steps()
    band = lon_margins(fields)
    inner = inner_conv(band, dw_kernel, False)
    edges = lat_margins(band)
    block_out, conv_gradient, keep, give, small = main_pass(
        place,
        edges[0],
        band,
        edges[1],
        inner,
        cotangent.reshape(-1, chans),
        dw_kernel,
        (dw_bias, norm_gain, layer_norm_offset, b_project, b_expand),
        w_expand,
        w_project,
        scale_factor,
    )
    block_out = block_out.reshape(fields.shape)
    conv_gradient = conv_gradient.reshape(fields.shape)
    barrier = lax.optimization_barrier
    half = hidden_units // 2
    quarter = half // 2
    got_far = within_pair(give[half:])
    got_near = within_pair(give[:half])
    outgoing = widened_sum(keep[half:], got_far).astype(jnp.bfloat16)
    outgoing, taps_in = barrier((outgoing, conv_gradient))
    got = exchange(outgoing[quarter:], 0)
    kept = exchange(outgoing[:quarter], 0)
    small = taps_pass(edges[0], band, edges[1], taps_in, small, scale_factor)
    got, small, conv_gradient = barrier((got, small, conv_gradient))
    outgoing = widened_sum(keep[quarter:half], got_near[quarter:], got).astype(jnp.bfloat16)
    outgoing, conv_gradient = barrier((outgoing, conv_gradient))
    got = exchange(outgoing, 1)
    band = lon_margins(conv_gradient)
    payload = widened_sum(keep[:quarter], got_near[:quarter], kept, got).astype(jnp.bfloat16)
    payload = jnp.concatenate([payload, small], axis=0)
    for at in range(2, count):
        got = exchange(payload, at)
        if at == 2:
            got, band = barrier((got, band))
        payload = rounded_sum(payload, got)
    payload, band = barrier((payload, band))
    top, bottom = lat_margins(band)
    got = exchange(payload, 1)
    inner = inner_conv(band, dw_kernel, True)
    got, inner = barrier((got, inner))
    across = exchange(payload[:quarter], 0)
    beside, small = got[:quarter], rounded_sum(payload[quarter:], got[quarter:])
    sent = jnp.concatenate([beside, small], axis=0)
    sent, band = barrier((sent, band))
    got = exchange(sent, 0)
    grad_fields = adjoint_pass(top, band, bottom, inner, cotangent, dw_kernel, poles)
    mine = jnp.concatenate([payload[:quarter], beside, across], axis=0)
    pair = within_pair(mine)
    got, grad_fields = barrier((got, grad_fields))
    last = jnp.concatenate([got[:quarter], rounded_sum(small, got[quarter:])], axis=0)
    pair_last = within_pair(last)
    sum_kern, sum_dwb, sum_gn, sum_sh, sum_exp, sum_bexp, sum_proj, sum_bproj = finish_pass(
        place, mine, last, pair, pair_last, hidden_units
    )
    return (
        block_out,
        grad_fields,
        sum_kern,
        sum_dwb,
        sum_gn,
        sum_sh,
        sum_exp,
        sum_bexp,
        sum_proj,
        sum_bproj,
    )


def solution(mesh):
    placed = (P("lat", "lon", None), P("lat", "lon", None), P(), P(), P(), P(), P(), P(), P(), P())
    return jax.shard_map(
        local,
        mesh=mesh,
        in_specs=placed,
        out_specs=(
            P("lat", "lon", None),
            P("lat", "lon", None),
            P(),
            P(),
            P(),
            P(),
            P(),
            P(),
            P(),
            P(),
        ),
        check_vma=False,
    )
```

```python
import functools
import math

import jax
import jax.numpy as jnp
from jax import lax
from jax.experimental import pallas as pl
from jax.experimental.pallas import tpu as pltpu
from jax.sharding import PartitionSpec as P

EPS = 1e-06


def flat_pairs(target):
    lons, lats = lax.axis_size("lon"), lax.axis_size("lat")
    pairs = []
    for lon in range(lons):
        for lat in range(lats):
            to_lon, to_lat = target(lon, lat)
            pairs.append((lon * lats + lat, to_lon * lats + to_lat))
    return pairs


def send(value, target):
    return lax.ppermute(value, ("lon", "lat"), flat_pairs(target))


def lon_margins(field):
    lons = lax.axis_size("lon")
    odd = lax.axis_index("lon") % 2 == 1
    first, last = field[:, :3], field[:, -3:]
    outer = send(
        jnp.where(odd, last, first),
        lambda lon, lat: ((lon + 1) % lons if lon % 2 else (lon - 1) % lons, lat),
    )
    inner = send(jnp.where(odd, first, last), lambda lon, lat: (lon ^ 1, lat))
    west = jnp.where(odd, inner, outer)
    east = jnp.where(odd, outer, inner)
    return west, field, east


def lat_margins(band):
    lons, lats = lax.axis_size("lon"), lax.axis_size("lat")
    lat = lax.axis_index("lat")
    odd = lat % 2 == 1
    pole = (lat == 0) | (lat == lats - 1)
    first = jnp.concatenate([part[:3] for part in band], axis=1)
    last = jnp.concatenate([part[-3:] for part in band], axis=1)

    def beyond(lon, lat):
        if lat == 0 or lat == lats - 1:
            return ((lon + lons // 2) % lons, lat)
        return (lon, lat + 1 if lat % 2 else lat - 1)

    outgoing = jnp.where(odd, last, first)
    outgoing = jnp.where(pole, outgoing[::-1], outgoing)
    far = send(outgoing, beyond)
    near = send(jnp.where(odd, first, last), lambda lon, lat: (lon, lat ^ 1))
    north = jnp.where(odd, near, far)
    south = jnp.where(odd, far, near)
    return north, south


def axis_bits():
    lon_bits = [("lon", bit) for bit in range((lax.axis_size("lon") - 1).bit_length())]
    lat_bits = [("lat", bit) for bit in range(1, (lax.axis_size("lat") - 1).bit_length())]
    steps = []
    while lon_bits or lat_bits:
        if lon_bits:
            steps.append(lon_bits.pop(0))
        if lat_bits:
            steps.append(lat_bits.pop(0))
    return steps


def flip(place, step):
    lon, lat = place
    axis, bit = step
    return (lon ^ (1 << bit), lat) if axis == "lon" else (lon, lat ^ (1 << bit))


def partner_steps():
    steps = axis_bits()
    other = list(steps)
    for at in range(0, len(steps) - 1, 2):
        other[at], other[at + 1] = other[at + 1], other[at]

    def exchange(value, at):
        return send(value, lambda lon, lat: flip((lon, lat), (other if lat % 2 else steps)[at]))

    return len(steps), exchange


def places():
    def order(first):
        high, low = (
            lax.shift_right_logical(lax.axis_index(axis), bit) & 1 for axis, bit in first
        )
        return 2 * high + low

    core = lax.axis_index("lat") & 1
    steps = axis_bits()[:2]
    plain, turned = order(steps), order(steps[::-1])
    return core, jnp.where(core == 0, plain, turned), jnp.where(core == 0, turned, plain)


def within_pair(value):
    return send(value, lambda lon, lat: (lon, lat ^ 1))


def widened_sum(*terms):
    total = terms[0].astype(jnp.float32)
    for term in terms[1:]:
        total = total + term.astype(jnp.float32)
    return total


def rounded_sum(left, right):
    return (left.astype(jnp.float32) + right.astype(jnp.float32)).astype(jnp.bfloat16)


def gelu_parts(values):
    normal_cdf = 0.5 * (1.0 + jax.scipy.special.erf(values * (1.0 / math.sqrt(2.0))))
    density = jnp.exp(-0.5 * values * values) * (1.0 / math.sqrt(2.0 * math.pi))
    return (values * normal_cdf, normal_cdf + values * density)


LANES = 128
SUBLANES = 8


def slot_rows(ref, lane, row, start, count):
    return ref[lane, row, pl.ds(start, SUBLANES, stride=count), :]


def spread_weights(weight_ref, spread_ref):
    for lane in range(spread_ref.shape[0]):
        for tap in range(49):
            row = weight_ref[tap // 7, tap % 7 : tap % 7 + 1, lane * LANES : (lane + 1) * LANES]
            spread_ref[lane, tap] = jnp.broadcast_to(row.astype(jnp.float32), (SUBLANES, LANES))


def split_lanes(source_ref, wide_ref, start=0, to=0, count=None):
    count = source_ref.shape[0] if count is None else count

    def body(row, carry):
        for lane in range(wide_ref.shape[0]):
            wide_ref[lane, to + row] = source_ref[
                start + row, :, lane * LANES : (lane + 1) * LANES
            ].astype(jnp.float32)
        return carry

    lax.fori_loop(0, count, body, 0)


def split_band(band_refs, out_ref, start=0, to=0, count=None):
    count = band_refs[1].shape[0] if count is None else count

    def body(row, carry):
        for lane in range(out_ref.shape[0]):
            column = 0
            for ref in band_refs:
                part = ref[start + row, :, lane * LANES : (lane + 1) * LANES]
                out_ref[lane, to + row, column : column + ref.shape[1]] = part.astype(jnp.float32)
                column += ref.shape[1]
        return carry

    lax.fori_loop(0, count, body, 0)


def split_padded(top_ref, band_refs, bottom_ref, out_ref):
    split_lanes(top_ref, out_ref)
    split_band(band_refs, out_ref, to=3)
    split_lanes(bottom_ref, out_ref, to=3 + band_refs[1].shape[0])


def window_sums(source_ref, lane, start, weight_of):
    slots = (source_ref.shape[2] - 6) // SUBLANES
    totals = [[jnp.zeros((SUBLANES, LANES), jnp.float32)] * slots for unused in range(4)]
    for row in range(10):
        loaded = [
            slot_rows(source_ref, lane, start + row, place, slots) for place in range(slots + 6)
        ]
        for row_off in range(7):
            to = row - row_off
            if 0 <= to < 4:
                for col_off in range(7):
                    weight = weight_of(row, row_off, col_off)
                    for slot in range(slots):
                        totals[to][slot] = totals[to][slot] + weight * loaded[slot + col_off]
    return totals


def store_sums(totals, out_ref, lane, start):
    slots = len(totals[0])
    for to in range(4):
        for slot in range(slots):
            out_ref[lane, start + to, pl.ds(slot, SUBLANES, stride=slots), :] = totals[to][slot]


def inner_conv_kernel(
    flipped, west_ref, field_ref, east_ref, dw_ref, out_ref, split_ref, spread_ref
):
    tiles, rows = out_ref.shape[0], out_ref.shape[1]
    spread_weights(dw_ref, spread_ref)
    split_band((west_ref, field_ref, east_ref), split_ref)

    def body(at, carry):
        lane, start = at // (rows // 4), (at % (rows // 4)) * 4

        def weight_of(row, row_off, col_off):
            tap = row_off * 7 + col_off
            return spread_ref[lane, 48 - tap if flipped else tap]

        store_sums(window_sums(split_ref, lane, start + 1, weight_of), out_ref, lane, start)
        return carry

    lax.fori_loop(0, tiles * (rows // 4), body, 0)


def inner_conv(band, dw_kernel, flipped):
    rows, cols, chans = band[1].shape
    tiles = chans // LANES
    return pl.pallas_call(
        functools.partial(inner_conv_kernel, flipped),
        out_shape=jax.ShapeDtypeStruct((tiles, rows - 8, cols, LANES), jnp.float32),
        in_specs=[pl.BlockSpec(memory_space=pltpu.VMEM)] * 4,
        out_specs=pl.BlockSpec(memory_space=pltpu.VMEM),
        scratch_shapes=[
            pltpu.VMEM((tiles, rows, cols + 6, LANES), jnp.float32),
            pltpu.VMEM((tiles, 49, SUBLANES, LANES), jnp.float32),
        ],
        compiler_params=pltpu.CompilerParams(vmem_limit_bytes=6 << 20),
        cost_estimate=pl.CostEstimate(
            flops=98 * rows * cols * chans, bytes_accessed=2 << 20, transcendentals=0
        ),
        name="block_inner_conv",
    )(*band, dw_kernel)


def pack_kernel(*refs):
    for at, ref in enumerate(refs[:-1]):
        refs[-1][at : at + 1, : ref.shape[0]] = ref[...].astype(jnp.float32).reshape(1, -1)


def packed(vectors):
    width = max(vector.shape[0] for vector in vectors)
    return pl.pallas_call(
        pack_kernel,
        out_shape=jax.ShapeDtypeStruct((8, width), jnp.float32),
        in_specs=[pl.BlockSpec(memory_space=pltpu.VMEM)] * len(vectors),
        out_specs=pl.BlockSpec(memory_space=pltpu.VMEM),
        compiler_params=pltpu.CompilerParams(vmem_limit_bytes=1 << 20),
        name="block_pack",
    )(*vectors)


def main_kernel(
    scale_factor,
    top_ref,
    west_ref,
    fields_ref,
    east_ref,
    bottom_ref,
    inner_ref,
    cot_ref,
    dw_ref,
    vectors_ref,
    w_expand_ref,
    w_project_ref,
    out_ref,
    dconv_ref,
    keep_ref,
    give_ref,
    small_ref,
    split_ref,
    spread_ref,
    edge_ref,
    expand_ref,
    project_ref,
):
    tiles, inner_rows, cols = inner_ref.shape[:3]
    rows = inner_rows + 8
    chans = tiles * LANES
    hidden_units = w_expand_ref.shape[1]
    pieces = hidden_units // chans
    spread_weights(dw_ref, spread_ref)
    split_lanes(top_ref, split_ref)
    band_refs = (west_ref, fields_ref, east_ref)
    split_band(band_refs, split_ref, to=3, count=7)
    split_band(band_refs, split_ref, start=rows - 7, to=10, count=7)
    split_lanes(bottom_ref, split_ref, to=17)

    def conv_edge(at, carry):
        lane, side = at // 2, at % 2
        totals = window_sums(
            split_ref,
            lane,
            side * 10,
            lambda row, row_off, col_off: spread_ref[lane, row_off * 7 + col_off],
        )
        store_sums(totals, edge_ref, lane, side * 4)
        return carry

    lax.fori_loop(0, tiles * 2, conv_edge, 0)
    small_ref[...] = jnp.zeros_like(small_ref)
    dw_bias, gain, offset, b_project = (vectors_ref[at : at + 1, :chans] for at in range(4))
    b_expand = vectors_ref[4:5]

    conv = jnp.concatenate(
        [
            jnp.concatenate(
                [edge_ref[lane, :4], inner_ref[lane], edge_ref[lane, 4:]], axis=0
            ).reshape(rows * cols, LANES)
            for lane in range(tiles)
        ],
        axis=1,
    )
    conv = conv + dw_bias
    removed = conv - jnp.mean(conv, axis=-1, keepdims=True)
    deviation = lax.rsqrt(jnp.mean(removed * removed, axis=-1, keepdims=True) + EPS)
    xhat = removed * deviation
    normed = (xhat * gain + offset).astype(jnp.bfloat16)
    cot = cot_ref[...]
    branch = jnp.zeros((rows * cols, chans), jnp.float32)
    d_normed = jnp.zeros((rows * cols, chans), jnp.float32)
    for piece in range(pieces):
        part = slice(piece * chans, (piece + 1) * chans)
        w_in = w_expand_ref[:, part]
        w_out = w_project_ref[part, :]
        pre = jnp.dot(normed, w_in, preferred_element_type=jnp.float32)
        pre = pre + b_expand[:, part]
        active, slope = gelu_parts(pre)
        hidden = active.astype(jnp.bfloat16)
        branch = branch + jnp.dot(hidden, w_out, preferred_element_type=jnp.float32)
        d_hidden = contract(cot, w_out, 1, 1)
        d_pre_wide = d_hidden * slope
        d_pre = d_pre_wide.astype(jnp.bfloat16)
        project_ref[part, :] = contract(hidden, cot, 0, 0)
        expand_ref[part, :] = contract(normed, d_pre, 0, 0)
        small_ref[8 + piece : 9 + piece] = jnp.sum(
            d_pre.astype(jnp.float32), axis=0, keepdims=True
        )
        d_normed = d_normed + contract(d_pre, w_in, 1, 1)
    plain = fields_ref[...].reshape(rows * cols, chans).astype(jnp.float32)
    out_ref[...] = (plain + (branch + b_project)).astype(jnp.bfloat16)
    small_ref[0:1] = jnp.sum(d_normed * xhat, axis=0, keepdims=True)
    small_ref[1:2] = jnp.sum(d_normed, axis=0, keepdims=True)
    small_ref[2:3] = jnp.sum(cot.astype(jnp.float32), axis=0, keepdims=True)
    scaled = d_normed * gain
    d_conv = deviation * (
        scaled
        - jnp.mean(scaled, axis=-1, keepdims=True)
        - xhat * jnp.mean(scaled * xhat, axis=-1, keepdims=True)
    )
    d_conv = d_conv.astype(jnp.bfloat16)
    dconv_ref[...] = d_conv
    small_ref[...] = small_ref[...] * scale_factor
    quarter = hidden_units // 4
    place = places()

    def finish(mine, other):
        for at in range(4):
            part = slice(at * quarter, (at + 1) * quarter)
            here = pl.multiple_of((at ^ place[1]) * quarter, quarter)
            there = pl.multiple_of((at ^ place[2]) * quarter, quarter)
            keep_ref[pl.ds(here, quarter)] = mine[part] * scale_factor
            give_ref[pl.ds(there, quarter)] = (other[part] * scale_factor).astype(jnp.bfloat16)

    @pl.when(place[0] == 0)
    def first():
        finish(expand_ref, project_ref)

    @pl.when(place[0] != 0)
    def second():
        finish(project_ref, expand_ref)


def contract(left, right, left_dim, right_dim):
    return lax.dot_general(
        left,
        right,
        (((left_dim,), (right_dim,)), ((), ())),
        preferred_element_type=jnp.float32,
    )


def main_pass(
    top, band, bottom, inner, cot, dw_kernel, vectors, w_expand, w_project, scale_factor
):
    rows, cols, chans = band[1].shape
    hidden_units = w_expand.shape[1]
    tiles = chans // LANES
    cells = rows * cols
    return pl.pallas_call(
        functools.partial(main_kernel, scale_factor),
        out_shape=[
            jax.ShapeDtypeStruct((cells, chans), jnp.bfloat16),
            jax.ShapeDtypeStruct((cells, chans), jnp.bfloat16),
            jax.ShapeDtypeStruct((hidden_units, chans), jnp.float32),
            jax.ShapeDtypeStruct((hidden_units, chans), jnp.bfloat16),
            jax.ShapeDtypeStruct((8 + hidden_units // chans, chans), jnp.float32),
        ],
        in_specs=[pl.BlockSpec(memory_space=pltpu.VMEM)] * 11,
        out_specs=[pl.BlockSpec(memory_space=pltpu.VMEM)] * 5,
        scratch_shapes=[
            pltpu.VMEM((tiles, 20, cols + 6, LANES), jnp.float32),
            pltpu.VMEM((tiles, 49, SUBLANES, LANES), jnp.float32),
            pltpu.VMEM((tiles, 8, cols, LANES), jnp.float32),
            pltpu.VMEM((hidden_units, chans), jnp.float32),
            pltpu.VMEM((hidden_units, chans), jnp.float32),
        ],
        compiler_params=pltpu.CompilerParams(vmem_limit_bytes=28 << 20),
        cost_estimate=pl.CostEstimate(
            flops=12 * cells * chans * hidden_units,
            bytes_accessed=8 << 20,
            transcendentals=2 * cells * hidden_units,
        ),
        name="block_main",
    )(top, *band, bottom, inner, cot, dw_kernel, vectors, w_expand, w_project)


def taps_kernel(
    scale_factor,
    top_ref,
    west_ref,
    field_ref,
    east_ref,
    bottom_ref,
    dconv_ref,
    small_ref,
    out_ref,
    wide_ref,
    dwide_ref,
    sums_ref,
):
    tiles, rows, cols = dwide_ref.shape[0], dwide_ref.shape[1], dwide_ref.shape[2]
    slots = cols // SUBLANES
    split_padded(top_ref, (west_ref, field_ref, east_ref), bottom_ref, wide_ref)
    split_lanes(dconv_ref, dwide_ref)
    sums_ref[...] = jnp.zeros_like(sums_ref)
    for lane in range(tiles):
        lanes = slice(lane * LANES, (lane + 1) * LANES)
        for row_off in range(7):

            def kernel_row(row, totals):
                grads = [slot_rows(dwide_ref, lane, row, slot, slots) for slot in range(slots)]
                loaded = [
                    slot_rows(wide_ref, lane, row + row_off, place, slots)
                    for place in range(slots + 6)
                ]
                sums = [
                    totals[col_off] + sum(grads[slot] * loaded[slot + col_off] for slot in range(slots))
                    for col_off in range(7)
                ]
                if row_off == 0:
                    sums.append(totals[7] + sum(grads))
                return tuple(sums)

            count = 8 if row_off == 0 else 7
            zeros = tuple(jnp.zeros((SUBLANES, LANES), jnp.float32) for unused in range(count))
            totals = lax.fori_loop(0, rows, kernel_row, zeros, unroll=4)
            for col_off in range(count):
                tap = row_off * 7 + col_off if col_off < 7 else 49
                sums_ref[tap : tap + 1, lanes] = jnp.sum(totals[col_off], axis=0, keepdims=True)
    sums_ref[...] = sums_ref[...] * scale_factor
    pieces = small_ref.shape[0] - 8
    sums_ref[50:53] = small_ref[0:3]
    sums_ref[53 : 53 + pieces] = small_ref[8 : 8 + pieces]
    out_ref[...] = sums_ref[...].astype(jnp.bfloat16)


def taps_pass(top, band, bottom, conv_gradient, small, scale_factor):
    rows, cols, chans = conv_gradient.shape
    tiles = chans // LANES
    height = -(-(45 + small.shape[0]) // 32) * 32
    return pl.pallas_call(
        functools.partial(taps_kernel, scale_factor),
        out_shape=jax.ShapeDtypeStruct((height, chans), jnp.bfloat16),
        in_specs=[pl.BlockSpec(memory_space=pltpu.VMEM)] * 7,
        out_specs=pl.BlockSpec(memory_space=pltpu.VMEM),
        scratch_shapes=[
            pltpu.VMEM((tiles, rows + 6, cols + 6, LANES), jnp.float32),
            pltpu.VMEM((tiles, rows, cols, LANES), jnp.float32),
            pltpu.VMEM((height, chans), jnp.float32),
        ],
        compiler_params=pltpu.CompilerParams(vmem_limit_bytes=6 << 20),
        cost_estimate=pl.CostEstimate(
            flops=98 * rows * cols * chans, bytes_accessed=3 << 20, transcendentals=0
        ),
        name="block_taps",
    )(top, *band, bottom, conv_gradient, small)


def write_pieces(
    mine_ref, pair_ref, first, count, expand_ref, project_ref, held_ref, sems
):
    chans = project_ref.shape[1]
    place = places()

    def write(columns_ref, columns_order, rows_ref, rows_order):
        copies = []
        for at in range(count):
            part = slice(at * chans, (at + 1) * chans)
            column = pl.multiple_of(((first + at) ^ columns_order) * chans, chans)
            row = pl.multiple_of(((first + at) ^ rows_order) * chans, chans)
            held_ref[2 * at] = columns_ref[part].astype(jnp.float32)
            copies.append(
                pltpu.make_async_copy(
                    held_ref.at[2 * at], expand_ref.at[:, pl.ds(column, chans)], sems.at[2 * at]
                )
            )
            copies[-1].start()
            held_ref[2 * at + 1] = rows_ref[part].astype(jnp.float32)
            copies.append(
                pltpu.make_async_copy(
                    held_ref.at[2 * at + 1], project_ref.at[pl.ds(row, chans)], sems.at[2 * at + 1]
                )
            )
            copies[-1].start()
        for copy in copies:
            copy.wait()

    @pl.when(place[0] == 0)
    def even():
        write(mine_ref, place[1], pair_ref, place[2])

    @pl.when(place[0] != 0)
    def odd():
        write(pair_ref, place[2], mine_ref, place[1])


def early_kernel(mine_ref, pair_ref, expand_ref, project_ref, held_ref, sems):
    count = mine_ref.shape[0] // project_ref.shape[1]
    write_pieces(mine_ref, pair_ref, 0, count, expand_ref, project_ref, held_ref, sems)


def early_pass(mine, pair, hidden_units):
    chans = mine.shape[1]
    count = mine.shape[0] // chans
    return pl.pallas_call(
        early_kernel,
        out_shape=[
            jax.ShapeDtypeStruct((chans, hidden_units), jnp.float32),
            jax.ShapeDtypeStruct((hidden_units, chans), jnp.float32),
        ],
        in_specs=[pl.BlockSpec(memory_space=pltpu.VMEM)] * 2,
        out_specs=[pl.BlockSpec(memory_space=pl.ANY)] * 2,
        scratch_shapes=[
            pltpu.VMEM((2 * count, chans, chans), jnp.float32),
            pltpu.SemaphoreType.DMA((2 * count,)),
        ],
        compiler_params=pltpu.CompilerParams(vmem_limit_bytes=6 << 20),
        cost_estimate=pl.CostEstimate(flops=0, bytes_accessed=4 << 20, transcendentals=0),
        name="block_early",
    )(mine, pair)


def finish_kernel(
    last_ref,
    pair_last_ref,
    expand_in_ref,
    project_in_ref,
    kern_ref,
    dwb_ref,
    gain_ref,
    shift_ref,
    expand_ref,
    b_expand_ref,
    project_ref,
    b_project_ref,
    sums_ref,
    held_ref,
    sems,
):
    hidden_units, chans = project_ref.shape
    pieces = hidden_units // chans
    count = held_ref.shape[0] // 2
    small = slice(count * chans, last_ref.shape[0])
    sums_ref[...] = last_ref[small].astype(jnp.float32) + pair_last_ref[small].astype(jnp.float32)
    for row_off in range(7):
        kern_ref[row_off] = sums_ref[row_off * 7 : row_off * 7 + 7]
    dwb_ref[...] = sums_ref[49]
    gain_ref[...] = sums_ref[50]
    shift_ref[...] = sums_ref[51]
    b_project_ref[...] = sums_ref[52]
    for piece in range(pieces):
        b_expand_ref[piece * chans : (piece + 1) * chans] = sums_ref[53 + piece]
    write_pieces(
        last_ref,
        pair_last_ref,
        pieces - count,
        count,
        expand_ref,
        project_ref,
        held_ref,
        sems,
    )


def finish_pass(last, pair_last, expand, project, early):
    hidden_units, chans = project.shape
    count = (hidden_units - early) // chans
    one = jax.ShapeDtypeStruct((chans,), jnp.float32)
    whole = pl.BlockSpec(memory_space=pltpu.VMEM)
    left = pl.BlockSpec(memory_space=pl.ANY)
    return pl.pallas_call(
        finish_kernel,
        out_shape=[
            jax.ShapeDtypeStruct((7, 7, chans), jnp.float32),
            one,
            one,
            one,
            jax.ShapeDtypeStruct((chans, hidden_units), jnp.float32),
            jax.ShapeDtypeStruct((hidden_units,), jnp.float32),
            jax.ShapeDtypeStruct((hidden_units, chans), jnp.float32),
            one,
        ],
        in_specs=[whole, whole, left, left],
        out_specs=[whole, whole, whole, whole, left, whole, left, whole],
        scratch_shapes=[
            pltpu.VMEM((last.shape[0] - count * chans, chans), jnp.float32),
            pltpu.VMEM((2 * count, chans, chans), jnp.float32),
            pltpu.SemaphoreType.DMA((2 * count,)),
        ],
        input_output_aliases={2: 4, 3: 6},
        compiler_params=pltpu.CompilerParams(vmem_limit_bytes=6 << 20),
        name="block_finish",
    )(last, pair_last, expand, project)


def adjoint_kernel(
    top_ref,
    west_ref,
    field_ref,
    east_ref,
    bottom_ref,
    inner_ref,
    cot_ref,
    dw_ref,
    out_ref,
    split_ref,
    spread_ref,
    edge_ref,
    sum_ref,
):
    tiles = split_ref.shape[0]
    rows = cot_ref.shape[0]
    spread_weights(dw_ref, spread_ref)
    band_refs = (west_ref, field_ref, east_ref)
    split_lanes(top_ref, split_ref)
    split_band(band_refs, split_ref, to=3, count=7)
    split_band(band_refs, split_ref, start=rows - 7, to=10, count=7)
    split_lanes(bottom_ref, split_ref, to=17)
    for side in range(2):
        at_pole = lax.axis_index("lat") == (0 if side == 0 else lax.axis_size("lat") - 1)
        for lane in range(tiles):
            for row_off in range(3):
                near = row_off if side == 0 else 6 - row_off
                for col_off in range(7):
                    plain = spread_ref[lane, (6 - near) * 7 + col_off]
                    turned = spread_ref[lane, near * 7 + col_off]
                    edge_ref[side, lane, row_off * 7 + col_off] = jnp.where(at_pole, turned, plain)

    def edge_block(lane, carry):
        for side in range(2):

            def weight_of(row, row_off, col_off):
                if side == 0 and row < 3:
                    return edge_ref[0, lane, row_off * 7 + 6 - col_off]
                if side == 1 and row >= 7:
                    return edge_ref[1, lane, (6 - row_off) * 7 + 6 - col_off]
                return spread_ref[lane, 48 - (row_off * 7 + col_off)]

            totals = window_sums(split_ref, lane, side * 10, weight_of)
            store_sums(totals, sum_ref, lane, side * 4)
        return carry

    lax.fori_loop(0, tiles, edge_block, 0)

    def write(ref, start, to, count):
        def body(row, carry):
            total = jnp.concatenate([ref[lane, start + row] for lane in range(tiles)], axis=1)
            out_ref[to + row] = (cot_ref[to + row].astype(jnp.float32) + total).astype(jnp.bfloat16)
            return carry

        lax.fori_loop(0, count, body, 0)

    write(sum_ref, 0, 0, 4)
    write(inner_ref, 0, 4, rows - 8)
    write(sum_ref, 4, rows - 4, 4)


def adjoint_pass(top, band, bottom, inner, cot, dw_kernel):
    rows, cols, chans = cot.shape
    tiles = chans // LANES
    return pl.pallas_call(
        adjoint_kernel,
        out_shape=jax.ShapeDtypeStruct(cot.shape, jnp.bfloat16),
        in_specs=[pl.BlockSpec(memory_space=pltpu.VMEM)] * 8,
        out_specs=pl.BlockSpec(memory_space=pltpu.VMEM),
        scratch_shapes=[
            pltpu.VMEM((tiles, 20, cols + 6, LANES), jnp.float32),
            pltpu.VMEM((tiles, 49, SUBLANES, LANES), jnp.float32),
            pltpu.VMEM((2, tiles, 21, SUBLANES, LANES), jnp.float32),
            pltpu.VMEM((tiles, 8, cols, LANES), jnp.float32),
        ],
        compiler_params=pltpu.CompilerParams(vmem_limit_bytes=6 << 20),
        cost_estimate=pl.CostEstimate(
            flops=25 * rows * cols * chans, bytes_accessed=3 << 20, transcendentals=0
        ),
        name="block_adjoint",
    )(top, *band, bottom, inner, cot, dw_kernel)


def local(
    fields,
    cotangent,
    dw_kernel,
    dw_bias,
    norm_gain,
    layer_norm_offset,
    w_expand,
    b_expand,
    w_project,
    b_project,
):
    rows = fields.shape[0]
    cols = fields.shape[1]
    chans = fields.shape[2]
    scale_factor = 1.0 / math.sqrt(rows * cols * lax.axis_size("lat") * lax.axis_size("lon"))
    hidden_units = w_expand.shape[1]
    count, exchange = partner_steps()
    barrier = lax.optimization_barrier
    band = lon_margins(fields)
    vectors = packed((dw_bias, norm_gain, layer_norm_offset, b_project, b_expand))
    band, vectors = barrier((band, vectors))
    inner = inner_conv(band, dw_kernel, False)
    edges = lat_margins(band)
    block_out, conv_gradient, keep, give, small = main_pass(
        edges[0],
        band,
        edges[1],
        inner,
        cotangent.reshape(-1, chans),
        dw_kernel,
        vectors,
        w_expand,
        w_project,
        scale_factor,
    )
    block_out = block_out.reshape(fields.shape)
    conv_gradient = conv_gradient.reshape(fields.shape)
    half = hidden_units // 2
    quarter = half // 2
    got_far = within_pair(give[half:])
    got_near = within_pair(give[:half])
    outgoing = widened_sum(keep[half:], got_far).astype(jnp.bfloat16)
    outgoing, taps_in = barrier((outgoing, conv_gradient))
    got = exchange(outgoing[quarter:], 0)
    kept = exchange(outgoing[:quarter], 0)
    small = taps_pass(edges[0], band, edges[1], taps_in, small, scale_factor)
    got, small, conv_gradient = barrier((got, small, conv_gradient))
    outgoing = widened_sum(keep[quarter:half], got_near[quarter:], got).astype(jnp.bfloat16)
    outgoing, conv_gradient = barrier((outgoing, conv_gradient))
    got = exchange(outgoing, 1)
    band = lon_margins(conv_gradient)
    payload = widened_sum(keep[:quarter], got_near[:quarter], kept, got).astype(jnp.bfloat16)
    payload = jnp.concatenate([payload, small], axis=0)
    for at in range(2, count):
        got = exchange(payload, at)
        if at == 2:
            got, band = barrier((got, band))
        payload = rounded_sum(payload, got)
    payload, band = barrier((payload, band))
    top, bottom = lat_margins(band)
    got = exchange(payload, 1)
    inner = inner_conv(band, dw_kernel, True)
    got, inner = barrier((got, inner))
    across = exchange(payload[:quarter], 0)
    beside, small = got[:quarter], rounded_sum(payload[quarter:], got[quarter:])
    sent = jnp.concatenate([beside, small], axis=0)
    sent, band = barrier((sent, band))
    got = exchange(sent, 0)
    grad_fields = adjoint_pass(top, band, bottom, inner, cotangent, dw_kernel)
    mine = jnp.concatenate([payload[:quarter], beside, across], axis=0)
    pair = within_pair(mine)
    written = early_pass(mine, pair, hidden_units)
    got, grad_fields, written = barrier((got, grad_fields, written))
    last = jnp.concatenate([got[:quarter], rounded_sum(small, got[quarter:])], axis=0)
    pair_last = within_pair(last)
    sum_kern, sum_dwb, sum_gn, sum_sh, sum_exp, sum_bexp, sum_proj, sum_bproj = finish_pass(
        last, pair_last, *written, mine.shape[0]
    )
    return (
        block_out,
        grad_fields,
        sum_kern,
        sum_dwb,
        sum_gn,
        sum_sh,
        sum_exp,
        sum_bexp,
        sum_proj,
        sum_bproj,
    )


def solution(mesh):
    placed = (P("lat", "lon", None), P("lat", "lon", None), P(), P(), P(), P(), P(), P(), P(), P())
    return jax.shard_map(
        local,
        mesh=mesh,
        in_specs=placed,
        out_specs=(
            P("lat", "lon", None),
            P("lat", "lon", None),
            P(),
            P(),
            P(),
            P(),
            P(),
            P(),
            P(),
            P(),
        ),
        check_vma=False,
    )
```

```python
import functools
import math

import jax
import jax.numpy as jnp
from jax import lax
from jax.experimental import pallas as pl
from jax.experimental.pallas import tpu as pltpu
from jax.sharding import PartitionSpec as P

EPS = 1e-06


def flat_pairs(target):
    lons, lats = lax.axis_size("lon"), lax.axis_size("lat")
    pairs = []
    for lon in range(lons):
        for lat in range(lats):
            to_lon, to_lat = target(lon, lat)
            pairs.append((lon * lats + lat, to_lon * lats + to_lat))
    return pairs


def send(value, target):
    return lax.ppermute(value, ("lon", "lat"), flat_pairs(target))


def lon_margins(field):
    lons = lax.axis_size("lon")
    odd = lax.axis_index("lon") % 2 == 1
    first, last = field[:, :3], field[:, -3:]
    outer = send(
        jnp.where(odd, last, first),
        lambda lon, lat: ((lon + 1) % lons if lon % 2 else (lon - 1) % lons, lat),
    )
    inner = send(jnp.where(odd, first, last), lambda lon, lat: (lon ^ 1, lat))
    west = jnp.where(odd, inner, outer)
    east = jnp.where(odd, outer, inner)
    return west, field, east


def lat_margins(band):
    lons, lats = lax.axis_size("lon"), lax.axis_size("lat")
    lat = lax.axis_index("lat")
    odd = lat % 2 == 1
    pole = (lat == 0) | (lat == lats - 1)
    first = jnp.concatenate([part[:3] for part in band], axis=1)
    last = jnp.concatenate([part[-3:] for part in band], axis=1)

    def beyond(lon, lat):
        if lat == 0 or lat == lats - 1:
            return ((lon + lons // 2) % lons, lat)
        return (lon, lat + 1 if lat % 2 else lat - 1)

    outgoing = jnp.where(odd, last, first)
    outgoing = jnp.where(pole, outgoing[::-1], outgoing)
    far = send(outgoing, beyond)
    near = send(jnp.where(odd, first, last), lambda lon, lat: (lon, lat ^ 1))
    north = jnp.where(odd, near, far)
    south = jnp.where(odd, far, near)
    return north, south


def axis_bits():
    lon_bits = [("lon", bit) for bit in range((lax.axis_size("lon") - 1).bit_length())]
    lat_bits = [("lat", bit) for bit in range(1, (lax.axis_size("lat") - 1).bit_length())]
    steps = []
    while lon_bits or lat_bits:
        if lon_bits:
            steps.append(lon_bits.pop(0))
        if lat_bits:
            steps.append(lat_bits.pop(0))
    return steps


def flip(place, step):
    lon, lat = place
    axis, bit = step
    return (lon ^ (1 << bit), lat) if axis == "lon" else (lon, lat ^ (1 << bit))


def partner_steps():
    steps = axis_bits()
    other = list(steps)
    for at in range(0, len(steps) - 1, 2):
        other[at], other[at + 1] = other[at + 1], other[at]

    def exchange(value, at):
        return send(value, lambda lon, lat: flip((lon, lat), (other if lat % 2 else steps)[at]))

    return len(steps), exchange


def places():
    def order(first):
        high, low = (
            lax.shift_right_logical(lax.axis_index(axis), bit) & 1 for axis, bit in first
        )
        return 2 * high + low

    core = lax.axis_index("lat") & 1
    steps = axis_bits()[:2]
    plain, turned = order(steps), order(steps[::-1])
    return core, jnp.where(core == 0, plain, turned), jnp.where(core == 0, turned, plain)


def within_pair(value):
    return send(value, lambda lon, lat: (lon, lat ^ 1))


def widened_sum(*terms):
    total = terms[0].astype(jnp.float32)
    for term in terms[1:]:
        total = total + term.astype(jnp.float32)
    return total


def rounded_sum(left, right):
    return (left.astype(jnp.float32) + right.astype(jnp.float32)).astype(jnp.bfloat16)


def gelu_parts(values):
    normal_cdf = 0.5 * (1.0 + jax.scipy.special.erf(values * (1.0 / math.sqrt(2.0))))
    density = jnp.exp(-0.5 * values * values) * (1.0 / math.sqrt(2.0 * math.pi))
    return (values * normal_cdf, normal_cdf + values * density)


LANES = 128
SUBLANES = 8


def slot_rows(ref, lane, row, start, count):
    return ref[lane, row, pl.ds(start, SUBLANES, stride=count), :]


def spread_weights(weight_ref, spread_ref):
    for lane in range(spread_ref.shape[0]):
        for tap in range(49):
            row = weight_ref[tap // 7, tap % 7 : tap % 7 + 1, lane * LANES : (lane + 1) * LANES]
            spread_ref[lane, tap] = jnp.broadcast_to(row.astype(jnp.float32), (SUBLANES, LANES))


def split_lanes(source_ref, wide_ref, start=0, to=0, count=None):
    count = source_ref.shape[0] if count is None else count

    def body(row, carry):
        for lane in range(wide_ref.shape[0]):
            wide_ref[lane, to + row] = source_ref[
                start + row, :, lane * LANES : (lane + 1) * LANES
            ].astype(jnp.float32)
        return carry

    lax.fori_loop(0, count, body, 0)


def split_band(band_refs, out_ref, start=0, to=0, count=None):
    count = band_refs[1].shape[0] if count is None else count

    def body(row, carry):
        for lane in range(out_ref.shape[0]):
            column = 0
            for ref in band_refs:
                part = ref[start + row, :, lane * LANES : (lane + 1) * LANES]
                out_ref[lane, to + row, column : column + ref.shape[1]] = part.astype(jnp.float32)
                column += ref.shape[1]
        return carry

    lax.fori_loop(0, count, body, 0)


def split_padded(top_ref, band_refs, bottom_ref, out_ref):
    split_lanes(top_ref, out_ref)
    split_band(band_refs, out_ref, to=3)
    split_lanes(bottom_ref, out_ref, to=3 + band_refs[1].shape[0])


def window_sums(source_ref, lane, start, weight_of):
    slots = (source_ref.shape[2] - 6) // SUBLANES
    totals = [[jnp.zeros((SUBLANES, LANES), jnp.float32)] * slots for unused in range(4)]
    for row in range(10):
        loaded = [
            slot_rows(source_ref, lane, start + row, place, slots) for place in range(slots + 6)
        ]
        for row_off in range(7):
            to = row - row_off
            if 0 <= to < 4:
                for col_off in range(7):
                    weight = weight_of(row, row_off, col_off)
                    for slot in range(slots):
                        totals[to][slot] = totals[to][slot] + weight * loaded[slot + col_off]
    return totals


def store_sums(totals, out_ref, lane, start):
    slots = len(totals[0])
    for to in range(4):
        for slot in range(slots):
            out_ref[lane, start + to, pl.ds(slot, SUBLANES, stride=slots), :] = totals[to][slot]


def inner_conv_kernel(
    flipped, west_ref, field_ref, east_ref, dw_ref, out_ref, split_ref, spread_ref
):
    tiles, rows = out_ref.shape[0], out_ref.shape[1]
    spread_weights(dw_ref, spread_ref)
    split_band((west_ref, field_ref, east_ref), split_ref)

    def body(at, carry):
        lane, start = at // (rows // 4), (at % (rows // 4)) * 4

        def weight_of(row, row_off, col_off):
            tap = row_off * 7 + col_off
            return spread_ref[lane, 48 - tap if flipped else tap]

        store_sums(window_sums(split_ref, lane, start + 1, weight_of), out_ref, lane, start)
        return carry

    lax.fori_loop(0, tiles * (rows // 4), body, 0)


def inner_conv(band, dw_kernel, flipped):
    rows, cols, chans = band[1].shape
    tiles = chans // LANES
    return pl.pallas_call(
        functools.partial(inner_conv_kernel, flipped),
        out_shape=jax.ShapeDtypeStruct((tiles, rows - 8, cols, LANES), jnp.float32),
        in_specs=[pl.BlockSpec(memory_space=pltpu.VMEM)] * 4,
        out_specs=pl.BlockSpec(memory_space=pltpu.VMEM),
        scratch_shapes=[
            pltpu.VMEM((tiles, rows, cols + 6, LANES), jnp.float32),
            pltpu.VMEM((tiles, 49, SUBLANES, LANES), jnp.float32),
        ],
        compiler_params=pltpu.CompilerParams(vmem_limit_bytes=6 << 20),
        cost_estimate=pl.CostEstimate(
            flops=98 * rows * cols * chans, bytes_accessed=2 << 20, transcendentals=0
        ),
        name="block_inner_conv",
    )(*band, dw_kernel)


def pack_kernel(*refs):
    for at, ref in enumerate(refs[:-1]):
        refs[-1][at : at + 1, : ref.shape[0]] = ref[...].astype(jnp.float32).reshape(1, -1)


def packed(vectors):
    width = max(vector.shape[0] for vector in vectors)
    return pl.pallas_call(
        pack_kernel,
        out_shape=jax.ShapeDtypeStruct((8, width), jnp.float32),
        in_specs=[pl.BlockSpec(memory_space=pltpu.VMEM)] * len(vectors),
        out_specs=pl.BlockSpec(memory_space=pltpu.VMEM),
        compiler_params=pltpu.CompilerParams(vmem_limit_bytes=1 << 20),
        name="block_pack",
    )(*vectors)


def main_kernel(
    scale_factor,
    top_ref,
    west_ref,
    fields_ref,
    east_ref,
    bottom_ref,
    inner_ref,
    cot_ref,
    dw_ref,
    vectors_ref,
    w_expand_ref,
    w_project_ref,
    out_ref,
    dconv_ref,
    keep_ref,
    give_ref,
    small_ref,
    split_ref,
    spread_ref,
    edge_ref,
    expand_ref,
    project_ref,
):
    tiles, inner_rows, cols = inner_ref.shape[:3]
    rows = inner_rows + 8
    chans = tiles * LANES
    hidden_units = w_expand_ref.shape[1]
    pieces = hidden_units // chans
    spread_weights(dw_ref, spread_ref)
    split_lanes(top_ref, split_ref)
    band_refs = (west_ref, fields_ref, east_ref)
    split_band(band_refs, split_ref, to=3, count=7)
    split_band(band_refs, split_ref, start=rows - 7, to=10, count=7)
    split_lanes(bottom_ref, split_ref, to=17)

    def conv_edge(at, carry):
        lane, side = at // 2, at % 2
        totals = window_sums(
            split_ref,
            lane,
            side * 10,
            lambda row, row_off, col_off: spread_ref[lane, row_off * 7 + col_off],
        )
        store_sums(totals, edge_ref, lane, side * 4)
        return carry

    lax.fori_loop(0, tiles * 2, conv_edge, 0)
    small_ref[...] = jnp.zeros_like(small_ref)
    dw_bias, gain, offset, b_project = (vectors_ref[at : at + 1, :chans] for at in range(4))
    b_expand = vectors_ref[4:5]

    conv = jnp.concatenate(
        [
            jnp.concatenate(
                [edge_ref[lane, :4], inner_ref[lane], edge_ref[lane, 4:]], axis=0
            ).reshape(rows * cols, LANES)
            for lane in range(tiles)
        ],
        axis=1,
    )
    conv = conv + dw_bias
    removed = conv - jnp.mean(conv, axis=-1, keepdims=True)
    deviation = lax.rsqrt(jnp.mean(removed * removed, axis=-1, keepdims=True) + EPS)
    xhat = removed * deviation
    normed = (xhat * gain + offset).astype(jnp.bfloat16)
    cot = cot_ref[...]
    branch = jnp.zeros((rows * cols, chans), jnp.float32)
    d_normed = jnp.zeros((rows * cols, chans), jnp.float32)
    for piece in range(pieces):
        part = slice(piece * chans, (piece + 1) * chans)
        w_in = w_expand_ref[:, part]
        w_out = w_project_ref[part, :]
        pre = jnp.dot(normed, w_in, preferred_element_type=jnp.float32)
        pre = pre + b_expand[:, part]
        active, slope = gelu_parts(pre)
        hidden = active.astype(jnp.bfloat16)
        branch = branch + jnp.dot(hidden, w_out, preferred_element_type=jnp.float32)
        d_hidden = contract(cot, w_out, 1, 1)
        d_pre_wide = d_hidden * slope
        d_pre = d_pre_wide.astype(jnp.bfloat16)
        project_ref[part, :] = contract(hidden, cot, 0, 0)
        expand_ref[part, :] = contract(normed, d_pre, 0, 0)
        small_ref[8 + piece : 9 + piece] = jnp.sum(
            d_pre.astype(jnp.float32), axis=0, keepdims=True
        )
        d_normed = d_normed + contract(d_pre, w_in, 1, 1)
    plain = fields_ref[...].reshape(rows * cols, chans).astype(jnp.float32)
    out_ref[...] = (plain + (branch + b_project)).astype(jnp.bfloat16)
    small_ref[0:1] = jnp.sum(d_normed * xhat, axis=0, keepdims=True)
    small_ref[1:2] = jnp.sum(d_normed, axis=0, keepdims=True)
    small_ref[2:3] = jnp.sum(cot.astype(jnp.float32), axis=0, keepdims=True)
    scaled = d_normed * gain
    d_conv = deviation * (
        scaled
        - jnp.mean(scaled, axis=-1, keepdims=True)
        - xhat * jnp.mean(scaled * xhat, axis=-1, keepdims=True)
    )
    d_conv = d_conv.astype(jnp.bfloat16)
    dconv_ref[...] = d_conv
    small_ref[...] = small_ref[...] * scale_factor
    quarter = hidden_units // 4
    place = places()

    def finish(mine, other):
        for at in range(4):
            part = slice(at * quarter, (at + 1) * quarter)
            here = pl.multiple_of((at ^ place[1]) * quarter, quarter)
            there = pl.multiple_of((at ^ place[2]) * quarter, quarter)
            keep_ref[pl.ds(here, quarter)] = mine[part] * scale_factor
            give_ref[pl.ds(there, quarter)] = (other[part] * scale_factor).astype(jnp.bfloat16)

    @pl.when(place[0] == 0)
    def first():
        finish(expand_ref, project_ref)

    @pl.when(place[0] != 0)
    def second():
        finish(project_ref, expand_ref)


def contract(left, right, left_dim, right_dim):
    return lax.dot_general(
        left,
        right,
        (((left_dim,), (right_dim,)), ((), ())),
        preferred_element_type=jnp.float32,
    )


def main_pass(
    top, band, bottom, inner, cot, dw_kernel, vectors, w_expand, w_project, scale_factor
):
    rows, cols, chans = band[1].shape
    hidden_units = w_expand.shape[1]
    tiles = chans // LANES
    cells = rows * cols
    return pl.pallas_call(
        functools.partial(main_kernel, scale_factor),
        out_shape=[
            jax.ShapeDtypeStruct((cells, chans), jnp.bfloat16),
            jax.ShapeDtypeStruct((cells, chans), jnp.bfloat16),
            jax.ShapeDtypeStruct((hidden_units, chans), jnp.float32),
            jax.ShapeDtypeStruct((hidden_units, chans), jnp.bfloat16),
            jax.ShapeDtypeStruct((8 + hidden_units // chans, chans), jnp.float32),
        ],
        in_specs=[pl.BlockSpec(memory_space=pltpu.VMEM)] * 11,
        out_specs=[pl.BlockSpec(memory_space=pltpu.VMEM)] * 5,
        scratch_shapes=[
            pltpu.VMEM((tiles, 20, cols + 6, LANES), jnp.float32),
            pltpu.VMEM((tiles, 49, SUBLANES, LANES), jnp.float32),
            pltpu.VMEM((tiles, 8, cols, LANES), jnp.float32),
            pltpu.VMEM((hidden_units, chans), jnp.float32),
            pltpu.VMEM((hidden_units, chans), jnp.float32),
        ],
        compiler_params=pltpu.CompilerParams(vmem_limit_bytes=28 << 20),
        cost_estimate=pl.CostEstimate(
            flops=12 * cells * chans * hidden_units,
            bytes_accessed=8 << 20,
            transcendentals=2 * cells * hidden_units,
        ),
        name="block_main",
    )(top, *band, bottom, inner, cot, dw_kernel, vectors, w_expand, w_project)


def taps_kernel(
    scale_factor,
    top_ref,
    west_ref,
    field_ref,
    east_ref,
    bottom_ref,
    dconv_ref,
    small_ref,
    out_ref,
    wide_ref,
    dwide_ref,
    sums_ref,
):
    tiles, rows, cols = dwide_ref.shape[0], dwide_ref.shape[1], dwide_ref.shape[2]
    slots = cols // SUBLANES
    split_padded(top_ref, (west_ref, field_ref, east_ref), bottom_ref, wide_ref)
    split_lanes(dconv_ref, dwide_ref)
    sums_ref[...] = jnp.zeros_like(sums_ref)
    for lane in range(tiles):
        lanes = slice(lane * LANES, (lane + 1) * LANES)
        for row_off in (0, 2, 4, 6):
            both = row_off < 6

            def padded_row(row):
                return tuple(slot_rows(wide_ref, lane, row, place, slots) for place in range(slots + 6))

            def kernel_row(row, carry):
                totals, low = carry
                grads = [slot_rows(dwide_ref, lane, row, slot, slots) for slot in range(slots)]
                high = padded_row(row + row_off + 1) if both else low
                low = low if both else padded_row(row + row_off)
                sums = []
                for at, loaded in enumerate((low, high) if both else (low,)):
                    for col_off in range(7):
                        product = sum(grads[slot] * loaded[slot + col_off] for slot in range(slots))
                        sums.append(totals[at * 7 + col_off] + product)
                if row_off == 6:
                    sums.append(totals[7] + sum(grads))
                return tuple(sums), (high if both else ())

            count = 14 if both else 8
            zeros = tuple(jnp.zeros((SUBLANES, LANES), jnp.float32) for unused in range(count))
            start = padded_row(row_off) if both else ()
            totals, unused = lax.fori_loop(0, rows, kernel_row, (zeros, start), unroll=8)
            for at in range(count):
                tap = row_off * 7 + at
                sums_ref[tap : tap + 1, lanes] = jnp.sum(totals[at], axis=0, keepdims=True)
    sums_ref[...] = sums_ref[...] * scale_factor
    pieces = small_ref.shape[0] - 8
    sums_ref[50:53] = small_ref[0:3]
    sums_ref[53 : 53 + pieces] = small_ref[8 : 8 + pieces]
    out_ref[...] = sums_ref[...].astype(jnp.bfloat16)


def taps_pass(top, band, bottom, conv_gradient, small, scale_factor):
    rows, cols, chans = conv_gradient.shape
    tiles = chans // LANES
    height = -(-(45 + small.shape[0]) // 32) * 32
    return pl.pallas_call(
        functools.partial(taps_kernel, scale_factor),
        out_shape=jax.ShapeDtypeStruct((height, chans), jnp.bfloat16),
        in_specs=[pl.BlockSpec(memory_space=pltpu.VMEM)] * 7,
        out_specs=pl.BlockSpec(memory_space=pltpu.VMEM),
        scratch_shapes=[
            pltpu.VMEM((tiles, rows + 6, cols + 6, LANES), jnp.float32),
            pltpu.VMEM((tiles, rows, cols, LANES), jnp.float32),
            pltpu.VMEM((height, chans), jnp.float32),
        ],
        compiler_params=pltpu.CompilerParams(vmem_limit_bytes=6 << 20),
        cost_estimate=pl.CostEstimate(
            flops=98 * rows * cols * chans, bytes_accessed=3 << 20, transcendentals=0
        ),
        name="block_taps",
    )(top, *band, bottom, conv_gradient, small)


def write_pieces(
    mine_ref, pair_ref, first, count, expand_ref, project_ref, held_ref, sems
):
    chans = project_ref.shape[1]
    place = places()

    def write(columns_ref, columns_order, rows_ref, rows_order):
        copies = []
        for at in range(count):
            part = slice(at * chans, (at + 1) * chans)
            column = pl.multiple_of(((first + at) ^ columns_order) * chans, chans)
            row = pl.multiple_of(((first + at) ^ rows_order) * chans, chans)
            held_ref[2 * at] = columns_ref[part].astype(jnp.float32)
            copies.append(
                pltpu.make_async_copy(
                    held_ref.at[2 * at], expand_ref.at[:, pl.ds(column, chans)], sems.at[2 * at]
                )
            )
            copies[-1].start()
            held_ref[2 * at + 1] = rows_ref[part].astype(jnp.float32)
            copies.append(
                pltpu.make_async_copy(
                    held_ref.at[2 * at + 1], project_ref.at[pl.ds(row, chans)], sems.at[2 * at + 1]
                )
            )
            copies[-1].start()
        for copy in copies:
            copy.wait()

    @pl.when(place[0] == 0)
    def even():
        write(mine_ref, place[1], pair_ref, place[2])

    @pl.when(place[0] != 0)
    def odd():
        write(pair_ref, place[2], mine_ref, place[1])


def early_kernel(mine_ref, pair_ref, expand_ref, project_ref, held_ref, sems):
    count = mine_ref.shape[0] // project_ref.shape[1]
    write_pieces(mine_ref, pair_ref, 0, count, expand_ref, project_ref, held_ref, sems)


def early_pass(mine, pair, hidden_units):
    chans = mine.shape[1]
    count = mine.shape[0] // chans
    return pl.pallas_call(
        early_kernel,
        out_shape=[
            jax.ShapeDtypeStruct((chans, hidden_units), jnp.float32),
            jax.ShapeDtypeStruct((hidden_units, chans), jnp.float32),
        ],
        in_specs=[pl.BlockSpec(memory_space=pltpu.VMEM)] * 2,
        out_specs=[pl.BlockSpec(memory_space=pl.ANY)] * 2,
        scratch_shapes=[
            pltpu.VMEM((2 * count, chans, chans), jnp.float32),
            pltpu.SemaphoreType.DMA((2 * count,)),
        ],
        compiler_params=pltpu.CompilerParams(vmem_limit_bytes=6 << 20),
        cost_estimate=pl.CostEstimate(flops=0, bytes_accessed=4 << 20, transcendentals=0),
        name="block_early",
    )(mine, pair)


def finish_kernel(
    last_ref,
    pair_last_ref,
    expand_in_ref,
    project_in_ref,
    kern_ref,
    dwb_ref,
    gain_ref,
    shift_ref,
    expand_ref,
    b_expand_ref,
    project_ref,
    b_project_ref,
    sums_ref,
    held_ref,
    sems,
):
    hidden_units, chans = project_ref.shape
    pieces = hidden_units // chans
    count = held_ref.shape[0] // 2
    small = slice(count * chans, last_ref.shape[0])
    sums_ref[...] = last_ref[small].astype(jnp.float32) + pair_last_ref[small].astype(jnp.float32)
    for row_off in range(7):
        kern_ref[row_off] = sums_ref[row_off * 7 : row_off * 7 + 7]
    dwb_ref[...] = sums_ref[49]
    gain_ref[...] = sums_ref[50]
    shift_ref[...] = sums_ref[51]
    b_project_ref[...] = sums_ref[52]
    for piece in range(pieces):
        b_expand_ref[piece * chans : (piece + 1) * chans] = sums_ref[53 + piece]
    write_pieces(
        last_ref,
        pair_last_ref,
        pieces - count,
        count,
        expand_ref,
        project_ref,
        held_ref,
        sems,
    )


def finish_pass(last, pair_last, expand, project, early):
    hidden_units, chans = project.shape
    count = (hidden_units - early) // chans
    one = jax.ShapeDtypeStruct((chans,), jnp.float32)
    whole = pl.BlockSpec(memory_space=pltpu.VMEM)
    left = pl.BlockSpec(memory_space=pl.ANY)
    return pl.pallas_call(
        finish_kernel,
        out_shape=[
            jax.ShapeDtypeStruct((7, 7, chans), jnp.float32),
            one,
            one,
            one,
            jax.ShapeDtypeStruct((chans, hidden_units), jnp.float32),
            jax.ShapeDtypeStruct((hidden_units,), jnp.float32),
            jax.ShapeDtypeStruct((hidden_units, chans), jnp.float32),
            one,
        ],
        in_specs=[whole, whole, left, left],
        out_specs=[whole, whole, whole, whole, left, whole, left, whole],
        scratch_shapes=[
            pltpu.VMEM((last.shape[0] - count * chans, chans), jnp.float32),
            pltpu.VMEM((2 * count, chans, chans), jnp.float32),
            pltpu.SemaphoreType.DMA((2 * count,)),
        ],
        input_output_aliases={2: 4, 3: 6},
        compiler_params=pltpu.CompilerParams(vmem_limit_bytes=6 << 20),
        name="block_finish",
    )(last, pair_last, expand, project)


def adjoint_kernel(
    top_ref,
    west_ref,
    field_ref,
    east_ref,
    bottom_ref,
    inner_ref,
    cot_ref,
    dw_ref,
    out_ref,
    split_ref,
    spread_ref,
    edge_ref,
    sum_ref,
):
    tiles = split_ref.shape[0]
    rows = cot_ref.shape[0]
    spread_weights(dw_ref, spread_ref)
    band_refs = (west_ref, field_ref, east_ref)
    split_lanes(top_ref, split_ref)
    split_band(band_refs, split_ref, to=3, count=7)
    split_band(band_refs, split_ref, start=rows - 7, to=10, count=7)
    split_lanes(bottom_ref, split_ref, to=17)
    for side in range(2):
        at_pole = lax.axis_index("lat") == (0 if side == 0 else lax.axis_size("lat") - 1)
        for lane in range(tiles):
            for row_off in range(3):
                near = row_off if side == 0 else 6 - row_off
                for col_off in range(7):
                    plain = spread_ref[lane, (6 - near) * 7 + col_off]
                    turned = spread_ref[lane, near * 7 + col_off]
                    edge_ref[side, lane, row_off * 7 + col_off] = jnp.where(at_pole, turned, plain)

    def edge_block(lane, carry):
        for side in range(2):

            def weight_of(row, row_off, col_off):
                if side == 0 and row < 3:
                    return edge_ref[0, lane, row_off * 7 + 6 - col_off]
                if side == 1 and row >= 7:
                    return edge_ref[1, lane, (6 - row_off) * 7 + 6 - col_off]
                return spread_ref[lane, 48 - (row_off * 7 + col_off)]

            totals = window_sums(split_ref, lane, side * 10, weight_of)
            store_sums(totals, sum_ref, lane, side * 4)
        return carry

    lax.fori_loop(0, tiles, edge_block, 0)

    def write(ref, start, to, count):
        def body(row, carry):
            total = jnp.concatenate([ref[lane, start + row] for lane in range(tiles)], axis=1)
            out_ref[to + row] = (cot_ref[to + row].astype(jnp.float32) + total).astype(jnp.bfloat16)
            return carry

        lax.fori_loop(0, count, body, 0)

    write(sum_ref, 0, 0, 4)
    write(inner_ref, 0, 4, rows - 8)
    write(sum_ref, 4, rows - 4, 4)


def adjoint_pass(top, band, bottom, inner, cot, dw_kernel):
    rows, cols, chans = cot.shape
    tiles = chans // LANES
    return pl.pallas_call(
        adjoint_kernel,
        out_shape=jax.ShapeDtypeStruct(cot.shape, jnp.bfloat16),
        in_specs=[pl.BlockSpec(memory_space=pltpu.VMEM)] * 8,
        out_specs=pl.BlockSpec(memory_space=pltpu.VMEM),
        scratch_shapes=[
            pltpu.VMEM((tiles, 20, cols + 6, LANES), jnp.float32),
            pltpu.VMEM((tiles, 49, SUBLANES, LANES), jnp.float32),
            pltpu.VMEM((2, tiles, 21, SUBLANES, LANES), jnp.float32),
            pltpu.VMEM((tiles, 8, cols, LANES), jnp.float32),
        ],
        compiler_params=pltpu.CompilerParams(vmem_limit_bytes=6 << 20),
        cost_estimate=pl.CostEstimate(
            flops=25 * rows * cols * chans, bytes_accessed=3 << 20, transcendentals=0
        ),
        name="block_adjoint",
    )(top, *band, bottom, inner, cot, dw_kernel)


def local(
    fields,
    cotangent,
    dw_kernel,
    dw_bias,
    norm_gain,
    layer_norm_offset,
    w_expand,
    b_expand,
    w_project,
    b_project,
):
    rows = fields.shape[0]
    cols = fields.shape[1]
    chans = fields.shape[2]
    scale_factor = 1.0 / math.sqrt(rows * cols * lax.axis_size("lat") * lax.axis_size("lon"))
    hidden_units = w_expand.shape[1]
    count, exchange = partner_steps()
    barrier = lax.optimization_barrier
    band = lon_margins(fields)
    vectors = packed((dw_bias, norm_gain, layer_norm_offset, b_project, b_expand))
    band, vectors = barrier((band, vectors))
    inner = inner_conv(band, dw_kernel, False)
    edges = lat_margins(band)
    block_out, conv_gradient, keep, give, small = main_pass(
        edges[0],
        band,
        edges[1],
        inner,
        cotangent.reshape(-1, chans),
        dw_kernel,
        vectors,
        w_expand,
        w_project,
        scale_factor,
    )
    block_out = block_out.reshape(fields.shape)
    conv_gradient = conv_gradient.reshape(fields.shape)
    half = hidden_units // 2
    quarter = half // 2
    got_far = within_pair(give[half:])
    got_near = within_pair(give[:half])
    outgoing = widened_sum(keep[half:], got_far).astype(jnp.bfloat16)
    outgoing, taps_in = barrier((outgoing, conv_gradient))
    got = exchange(outgoing[quarter:], 0)
    kept = exchange(outgoing[:quarter], 0)
    small = taps_pass(edges[0], band, edges[1], taps_in, small, scale_factor)
    got, small, conv_gradient = barrier((got, small, conv_gradient))
    outgoing = widened_sum(keep[quarter:half], got_near[quarter:], got).astype(jnp.bfloat16)
    outgoing, conv_gradient = barrier((outgoing, conv_gradient))
    got = exchange(outgoing, 1)
    band = lon_margins(conv_gradient)
    payload = widened_sum(keep[:quarter], got_near[:quarter], kept, got).astype(jnp.bfloat16)
    payload = jnp.concatenate([payload, small], axis=0)
    for at in range(2, count):
        got = exchange(payload, at)
        if at == 2:
            got, band = barrier((got, band))
        payload = rounded_sum(payload, got)
    payload, band = barrier((payload, band))
    top, bottom = lat_margins(band)
    got = exchange(payload, 1)
    inner = inner_conv(band, dw_kernel, True)
    got, inner = barrier((got, inner))
    across = exchange(payload[:quarter], 0)
    beside, small = got[:quarter], rounded_sum(payload[quarter:], got[quarter:])
    sent = jnp.concatenate([beside, small], axis=0)
    sent, band = barrier((sent, band))
    got = exchange(sent, 0)
    grad_fields = adjoint_pass(top, band, bottom, inner, cotangent, dw_kernel)
    mine = jnp.concatenate([payload[:quarter], beside, across], axis=0)
    pair = within_pair(mine)
    written = early_pass(mine, pair, hidden_units)
    got, grad_fields, written = barrier((got, grad_fields, written))
    last = jnp.concatenate([got[:quarter], rounded_sum(small, got[quarter:])], axis=0)
    pair_last = within_pair(last)
    sum_kern, sum_dwb, sum_gn, sum_sh, sum_exp, sum_bexp, sum_proj, sum_bproj = finish_pass(
        last, pair_last, *written, mine.shape[0]
    )
    return (
        block_out,
        grad_fields,
        sum_kern,
        sum_dwb,
        sum_gn,
        sum_sh,
        sum_exp,
        sum_bexp,
        sum_proj,
        sum_bproj,
    )


def solution(mesh):
    placed = (P("lat", "lon", None), P("lat", "lon", None), P(), P(), P(), P(), P(), P(), P(), P())
    return jax.shard_map(
        local,
        mesh=mesh,
        in_specs=placed,
        out_specs=(
            P("lat", "lon", None),
            P("lat", "lon", None),
            P(),
            P(),
            P(),
            P(),
            P(),
            P(),
            P(),
            P(),
        ),
        check_vma=False,
    )
```

```python
import functools
import math

import jax
import jax.numpy as jnp
from jax import lax
from jax.experimental import pallas as pl
from jax.experimental.pallas import tpu as pltpu
from jax.sharding import PartitionSpec as P

EPS = 1e-06


def flat_pairs(target):
    lons, lats = lax.axis_size("lon"), lax.axis_size("lat")
    pairs = []
    for lon in range(lons):
        for lat in range(lats):
            to_lon, to_lat = target(lon, lat)
            pairs.append((lon * lats + lat, to_lon * lats + to_lat))
    return pairs


def send(value, target):
    return lax.ppermute(value, ("lon", "lat"), flat_pairs(target))


def lon_margins(field):
    lons = lax.axis_size("lon")
    odd = lax.axis_index("lon") % 2 == 1
    first, last = field[:, :3], field[:, -3:]
    outer = send(
        jnp.where(odd, last, first),
        lambda lon, lat: ((lon + 1) % lons if lon % 2 else (lon - 1) % lons, lat),
    )
    inner = send(jnp.where(odd, first, last), lambda lon, lat: (lon ^ 1, lat))
    west = jnp.where(odd, inner, outer)
    east = jnp.where(odd, outer, inner)
    return west, field, east


def lat_margins(band):
    lons, lats = lax.axis_size("lon"), lax.axis_size("lat")
    lat = lax.axis_index("lat")
    odd = lat % 2 == 1
    pole = (lat == 0) | (lat == lats - 1)
    first = jnp.concatenate([part[:3] for part in band], axis=1)
    last = jnp.concatenate([part[-3:] for part in band], axis=1)

    def beyond(lon, lat):
        if lat == 0 or lat == lats - 1:
            return ((lon + lons // 2) % lons, lat)
        return (lon, lat + 1 if lat % 2 else lat - 1)

    outgoing = jnp.where(odd, last, first)
    outgoing = jnp.where(pole, outgoing[::-1], outgoing)
    far = send(outgoing, beyond)
    near = send(jnp.where(odd, first, last), lambda lon, lat: (lon, lat ^ 1))
    north = jnp.where(odd, near, far)
    south = jnp.where(odd, far, near)
    return north, south


def axis_bits():
    lon_bits = [("lon", bit) for bit in range((lax.axis_size("lon") - 1).bit_length())]
    lat_bits = [("lat", bit) for bit in range(1, (lax.axis_size("lat") - 1).bit_length())]
    steps = []
    while lon_bits or lat_bits:
        if lon_bits:
            steps.append(lon_bits.pop(0))
        if lat_bits:
            steps.append(lat_bits.pop(0))
    return steps


def flip(place, step):
    lon, lat = place
    axis, bit = step
    return (lon ^ (1 << bit), lat) if axis == "lon" else (lon, lat ^ (1 << bit))


def partner_steps():
    steps = axis_bits()
    other = list(steps)
    for at in range(0, len(steps) - 1, 2):
        other[at], other[at + 1] = other[at + 1], other[at]

    def exchange(value, at):
        return send(value, lambda lon, lat: flip((lon, lat), (other if lat % 2 else steps)[at]))

    return len(steps), exchange


def places():
    def order(first):
        high, low = (
            lax.shift_right_logical(lax.axis_index(axis), bit) & 1 for axis, bit in first
        )
        return 2 * high + low

    core = lax.axis_index("lat") & 1
    steps = axis_bits()[:2]
    plain, turned = order(steps), order(steps[::-1])
    return core, jnp.where(core == 0, plain, turned), jnp.where(core == 0, turned, plain)


def within_pair(value):
    return send(value, lambda lon, lat: (lon, lat ^ 1))


def widened_sum(*terms):
    total = terms[0].astype(jnp.float32)
    for term in terms[1:]:
        total = total + term.astype(jnp.float32)
    return total


def rounded_sum(left, right):
    return (left.astype(jnp.float32) + right.astype(jnp.float32)).astype(jnp.bfloat16)


def gelu_parts(values):
    normal_cdf = 0.5 * (1.0 + jax.scipy.special.erf(values * (1.0 / math.sqrt(2.0))))
    density = jnp.exp(-0.5 * values * values) * (1.0 / math.sqrt(2.0 * math.pi))
    return (values * normal_cdf, normal_cdf + values * density)


LANES = 128
SUBLANES = 8


def slot_rows(ref, lane, row, start, count):
    return ref[lane, row, pl.ds(start, SUBLANES, stride=count), :]


def spread_weights(weight_ref, spread_ref):
    for lane in range(spread_ref.shape[0]):
        for tap in range(49):
            row = weight_ref[tap // 7, tap % 7 : tap % 7 + 1, lane * LANES : (lane + 1) * LANES]
            spread_ref[lane, tap] = jnp.broadcast_to(row.astype(jnp.float32), (SUBLANES, LANES))


def split_lanes(source_ref, wide_ref, start=0, to=0, count=None):
    count = source_ref.shape[0] if count is None else count

    def body(row, carry):
        for lane in range(wide_ref.shape[0]):
            wide_ref[lane, to + row] = source_ref[
                start + row, :, lane * LANES : (lane + 1) * LANES
            ].astype(jnp.float32)
        return carry

    lax.fori_loop(0, count, body, 0)


def split_band(band_refs, out_ref, start=0, to=0, count=None):
    count = band_refs[1].shape[0] if count is None else count

    def body(row, carry):
        for lane in range(out_ref.shape[0]):
            column = 0
            for ref in band_refs:
                part = ref[start + row, :, lane * LANES : (lane + 1) * LANES]
                out_ref[lane, to + row, column : column + ref.shape[1]] = part.astype(jnp.float32)
                column += ref.shape[1]
        return carry

    lax.fori_loop(0, count, body, 0)


def split_padded(top_ref, band_refs, bottom_ref, out_ref):
    split_lanes(top_ref, out_ref)
    split_band(band_refs, out_ref, to=3)
    split_lanes(bottom_ref, out_ref, to=3 + band_refs[1].shape[0])


def window_sums(source_ref, lane, start, weight_of, height=4):
    slots = (source_ref.shape[2] - 6) // SUBLANES
    totals = [[jnp.zeros((SUBLANES, LANES), jnp.float32)] * slots for unused in range(height)]
    for row in range(height + 6):
        loaded = [
            slot_rows(source_ref, lane, start + row, place, slots) for place in range(slots + 6)
        ]
        for row_off in range(7):
            to = row - row_off
            if 0 <= to < height:
                for col_off in range(7):
                    weight = weight_of(row, row_off, col_off)
                    for slot in range(slots):
                        totals[to][slot] = totals[to][slot] + weight * loaded[slot + col_off]
    return totals


def store_sums(totals, out_ref, lane, start):
    slots = len(totals[0])
    for to in range(len(totals)):
        for slot in range(slots):
            out_ref[lane, start + to, pl.ds(slot, SUBLANES, stride=slots), :] = totals[to][slot]


def inner_conv_kernel(
    flipped, west_ref, field_ref, east_ref, dw_ref, out_ref, split_ref, spread_ref
):
    tiles, rows = out_ref.shape[0], out_ref.shape[1]
    spread_weights(dw_ref, spread_ref)
    split_band((west_ref, field_ref, east_ref), split_ref)

    def body(at, carry):
        lane, start = at // (rows // 8), (at % (rows // 8)) * 8

        def weight_of(row, row_off, col_off):
            tap = row_off * 7 + col_off
            return spread_ref[lane, 48 - tap if flipped else tap]

        store_sums(window_sums(split_ref, lane, start + 1, weight_of, 8), out_ref, lane, start)
        return carry

    lax.fori_loop(0, tiles * (rows // 8), body, 0)


def inner_conv(band, dw_kernel, flipped):
    rows, cols, chans = band[1].shape
    tiles = chans // LANES
    return pl.pallas_call(
        functools.partial(inner_conv_kernel, flipped),
        out_shape=jax.ShapeDtypeStruct((tiles, rows - 8, cols, LANES), jnp.float32),
        in_specs=[pl.BlockSpec(memory_space=pltpu.VMEM)] * 4,
        out_specs=pl.BlockSpec(memory_space=pltpu.VMEM),
        scratch_shapes=[
            pltpu.VMEM((tiles, rows, cols + 6, LANES), jnp.float32),
            pltpu.VMEM((tiles, 49, SUBLANES, LANES), jnp.float32),
        ],
        compiler_params=pltpu.CompilerParams(vmem_limit_bytes=6 << 20),
        cost_estimate=pl.CostEstimate(
            flops=98 * rows * cols * chans, bytes_accessed=2 << 20, transcendentals=0
        ),
        name="block_inner_conv",
    )(*band, dw_kernel)


def pack_kernel(*refs):
    for at, ref in enumerate(refs[:-1]):
        refs[-1][at : at + 1, : ref.shape[0]] = ref[...].astype(jnp.float32).reshape(1, -1)


def packed(vectors):
    width = max(vector.shape[0] for vector in vectors)
    return pl.pallas_call(
        pack_kernel,
        out_shape=jax.ShapeDtypeStruct((8, width), jnp.float32),
        in_specs=[pl.BlockSpec(memory_space=pltpu.VMEM)] * len(vectors),
        out_specs=pl.BlockSpec(memory_space=pltpu.VMEM),
        compiler_params=pltpu.CompilerParams(vmem_limit_bytes=1 << 20),
        name="block_pack",
    )(*vectors)


def main_kernel(
    scale_factor,
    top_ref,
    west_ref,
    fields_ref,
    east_ref,
    bottom_ref,
    inner_ref,
    cot_ref,
    dw_ref,
    vectors_ref,
    w_expand_ref,
    w_project_ref,
    out_ref,
    dconv_ref,
    keep_ref,
    give_ref,
    small_ref,
    split_ref,
    spread_ref,
    edge_ref,
    expand_ref,
    project_ref,
):
    tiles, inner_rows, cols = inner_ref.shape[:3]
    rows = inner_rows + 8
    chans = tiles * LANES
    hidden_units = w_expand_ref.shape[1]
    pieces = hidden_units // chans
    spread_weights(dw_ref, spread_ref)
    split_lanes(top_ref, split_ref)
    band_refs = (west_ref, fields_ref, east_ref)
    split_band(band_refs, split_ref, to=3, count=7)
    split_band(band_refs, split_ref, start=rows - 7, to=10, count=7)
    split_lanes(bottom_ref, split_ref, to=17)

    def conv_edge(at, carry):
        lane, side = at // 2, at % 2
        totals = window_sums(
            split_ref,
            lane,
            side * 10,
            lambda row, row_off, col_off: spread_ref[lane, row_off * 7 + col_off],
        )
        store_sums(totals, edge_ref, lane, side * 4)
        return carry

    lax.fori_loop(0, tiles * 2, conv_edge, 0)
    small_ref[...] = jnp.zeros_like(small_ref)
    dw_bias, gain, offset, b_project = (vectors_ref[at : at + 1, :chans] for at in range(4))
    b_expand = vectors_ref[4:5]

    conv = jnp.concatenate(
        [
            jnp.concatenate(
                [edge_ref[lane, :4], inner_ref[lane], edge_ref[lane, 4:]], axis=0
            ).reshape(rows * cols, LANES)
            for lane in range(tiles)
        ],
        axis=1,
    )
    conv = conv + dw_bias
    removed = conv - jnp.mean(conv, axis=-1, keepdims=True)
    deviation = lax.rsqrt(jnp.mean(removed * removed, axis=-1, keepdims=True) + EPS)
    xhat = removed * deviation
    normed = (xhat * gain + offset).astype(jnp.bfloat16)
    cot = cot_ref[...]
    branch = jnp.zeros((rows * cols, chans), jnp.float32)
    d_normed = jnp.zeros((rows * cols, chans), jnp.float32)
    for piece in range(pieces):
        part = slice(piece * chans, (piece + 1) * chans)
        w_in = w_expand_ref[:, part]
        w_out = w_project_ref[part, :]
        pre = jnp.dot(normed, w_in, preferred_element_type=jnp.float32)
        pre = pre + b_expand[:, part]
        active, slope = gelu_parts(pre)
        hidden = active.astype(jnp.bfloat16)
        branch = branch + jnp.dot(hidden, w_out, preferred_element_type=jnp.float32)
        d_hidden = contract(cot, w_out, 1, 1)
        d_pre_wide = d_hidden * slope
        d_pre = d_pre_wide.astype(jnp.bfloat16)
        project_ref[part, :] = contract(hidden, cot, 0, 0)
        expand_ref[part, :] = contract(normed, d_pre, 0, 0)
        small_ref[8 + piece : 9 + piece] = jnp.sum(
            d_pre.astype(jnp.float32), axis=0, keepdims=True
        )
        d_normed = d_normed + contract(d_pre, w_in, 1, 1)
    plain = fields_ref[...].reshape(rows * cols, chans).astype(jnp.float32)
    out_ref[...] = (plain + (branch + b_project)).astype(jnp.bfloat16)
    small_ref[0:1] = jnp.sum(d_normed * xhat, axis=0, keepdims=True)
    small_ref[1:2] = jnp.sum(d_normed, axis=0, keepdims=True)
    small_ref[2:3] = jnp.sum(cot.astype(jnp.float32), axis=0, keepdims=True)
    scaled = d_normed * gain
    d_conv = deviation * (
        scaled
        - jnp.mean(scaled, axis=-1, keepdims=True)
        - xhat * jnp.mean(scaled * xhat, axis=-1, keepdims=True)
    )
    d_conv = d_conv.astype(jnp.bfloat16)
    dconv_ref[...] = d_conv
    small_ref[...] = small_ref[...] * scale_factor
    quarter = hidden_units // 4
    place = places()

    def finish(mine, other):
        for at in range(4):
            part = slice(at * quarter, (at + 1) * quarter)
            here = pl.multiple_of((at ^ place[1]) * quarter, quarter)
            there = pl.multiple_of((at ^ place[2]) * quarter, quarter)
            keep_ref[pl.ds(here, quarter)] = mine[part] * scale_factor
            give_ref[pl.ds(there, quarter)] = (other[part] * scale_factor).astype(jnp.bfloat16)

    @pl.when(place[0] == 0)
    def first():
        finish(expand_ref, project_ref)

    @pl.when(place[0] != 0)
    def second():
        finish(project_ref, expand_ref)


def contract(left, right, left_dim, right_dim):
    return lax.dot_general(
        left,
        right,
        (((left_dim,), (right_dim,)), ((), ())),
        preferred_element_type=jnp.float32,
    )


def main_pass(
    top, band, bottom, inner, cot, dw_kernel, vectors, w_expand, w_project, scale_factor
):
    rows, cols, chans = band[1].shape
    hidden_units = w_expand.shape[1]
    tiles = chans // LANES
    cells = rows * cols
    return pl.pallas_call(
        functools.partial(main_kernel, scale_factor),
        out_shape=[
            jax.ShapeDtypeStruct((cells, chans), jnp.bfloat16),
            jax.ShapeDtypeStruct((cells, chans), jnp.bfloat16),
            jax.ShapeDtypeStruct((hidden_units, chans), jnp.float32),
            jax.ShapeDtypeStruct((hidden_units, chans), jnp.bfloat16),
            jax.ShapeDtypeStruct((8 + hidden_units // chans, chans), jnp.float32),
        ],
        in_specs=[pl.BlockSpec(memory_space=pltpu.VMEM)] * 11,
        out_specs=[pl.BlockSpec(memory_space=pltpu.VMEM)] * 5,
        scratch_shapes=[
            pltpu.VMEM((tiles, 20, cols + 6, LANES), jnp.float32),
            pltpu.VMEM((tiles, 49, SUBLANES, LANES), jnp.float32),
            pltpu.VMEM((tiles, 8, cols, LANES), jnp.float32),
            pltpu.VMEM((hidden_units, chans), jnp.float32),
            pltpu.VMEM((hidden_units, chans), jnp.float32),
        ],
        compiler_params=pltpu.CompilerParams(vmem_limit_bytes=28 << 20),
        cost_estimate=pl.CostEstimate(
            flops=12 * cells * chans * hidden_units,
            bytes_accessed=8 << 20,
            transcendentals=2 * cells * hidden_units,
        ),
        name="block_main",
    )(top, *band, bottom, inner, cot, dw_kernel, vectors, w_expand, w_project)


def taps_kernel(
    scale_factor,
    top_ref,
    west_ref,
    field_ref,
    east_ref,
    bottom_ref,
    dconv_ref,
    small_ref,
    out_ref,
    wide_ref,
    dwide_ref,
    sums_ref,
):
    tiles, rows, cols = dwide_ref.shape[0], dwide_ref.shape[1], dwide_ref.shape[2]
    slots = cols // SUBLANES
    split_padded(top_ref, (west_ref, field_ref, east_ref), bottom_ref, wide_ref)
    split_lanes(dconv_ref, dwide_ref)
    sums_ref[...] = jnp.zeros_like(sums_ref)
    for lane in range(tiles):
        lanes = slice(lane * LANES, (lane + 1) * LANES)
        for row_off in (0, 2, 4, 6):
            both = row_off < 6

            def padded_row(row):
                return tuple(slot_rows(wide_ref, lane, row, place, slots) for place in range(slots + 6))

            def kernel_row(row, carry):
                totals, low = carry
                grads = [slot_rows(dwide_ref, lane, row, slot, slots) for slot in range(slots)]
                high = padded_row(row + row_off + 1) if both else low
                low = low if both else padded_row(row + row_off)
                sums = []
                for at, loaded in enumerate((low, high) if both else (low,)):
                    for col_off in range(7):
                        product = sum(grads[slot] * loaded[slot + col_off] for slot in range(slots))
                        sums.append(totals[at * 7 + col_off] + product)
                if row_off == 6:
                    sums.append(totals[7] + sum(grads))
                return tuple(sums), (high if both else ())

            count = 14 if both else 8
            zeros = tuple(jnp.zeros((SUBLANES, LANES), jnp.float32) for unused in range(count))
            start = padded_row(row_off) if both else ()
            totals, unused = lax.fori_loop(0, rows, kernel_row, (zeros, start), unroll=8)
            for at in range(count):
                tap = row_off * 7 + at
                sums_ref[tap : tap + 1, lanes] = jnp.sum(totals[at], axis=0, keepdims=True)
    sums_ref[...] = sums_ref[...] * scale_factor
    pieces = small_ref.shape[0] - 8
    sums_ref[50:53] = small_ref[0:3]
    sums_ref[53 : 53 + pieces] = small_ref[8 : 8 + pieces]
    out_ref[...] = sums_ref[...].astype(jnp.bfloat16)


def taps_pass(top, band, bottom, conv_gradient, small, scale_factor):
    rows, cols, chans = conv_gradient.shape
    tiles = chans // LANES
    height = -(-(45 + small.shape[0]) // 32) * 32
    return pl.pallas_call(
        functools.partial(taps_kernel, scale_factor),
        out_shape=jax.ShapeDtypeStruct((height, chans), jnp.bfloat16),
        in_specs=[pl.BlockSpec(memory_space=pltpu.VMEM)] * 7,
        out_specs=pl.BlockSpec(memory_space=pltpu.VMEM),
        scratch_shapes=[
            pltpu.VMEM((tiles, rows + 6, cols + 6, LANES), jnp.float32),
            pltpu.VMEM((tiles, rows, cols, LANES), jnp.float32),
            pltpu.VMEM((height, chans), jnp.float32),
        ],
        compiler_params=pltpu.CompilerParams(vmem_limit_bytes=6 << 20),
        cost_estimate=pl.CostEstimate(
            flops=98 * rows * cols * chans, bytes_accessed=3 << 20, transcendentals=0
        ),
        name="block_taps",
    )(top, *band, bottom, conv_gradient, small)


def write_pieces(
    mine_ref, pair_ref, first, count, expand_ref, project_ref, held_ref, sems
):
    chans = project_ref.shape[1]
    place = places()

    def write(columns_ref, columns_order, rows_ref, rows_order):
        copies = []
        for at in range(count):
            part = slice(at * chans, (at + 1) * chans)
            column = pl.multiple_of(((first + at) ^ columns_order) * chans, chans)
            row = pl.multiple_of(((first + at) ^ rows_order) * chans, chans)
            held_ref[2 * at] = columns_ref[part].astype(jnp.float32)
            copies.append(
                pltpu.make_async_copy(
                    held_ref.at[2 * at], expand_ref.at[:, pl.ds(column, chans)], sems.at[2 * at]
                )
            )
            copies[-1].start()
            held_ref[2 * at + 1] = rows_ref[part].astype(jnp.float32)
            copies.append(
                pltpu.make_async_copy(
                    held_ref.at[2 * at + 1], project_ref.at[pl.ds(row, chans)], sems.at[2 * at + 1]
                )
            )
            copies[-1].start()
        for copy in copies:
            copy.wait()

    @pl.when(place[0] == 0)
    def even():
        write(mine_ref, place[1], pair_ref, place[2])

    @pl.when(place[0] != 0)
    def odd():
        write(pair_ref, place[2], mine_ref, place[1])


def early_kernel(mine_ref, pair_ref, expand_ref, project_ref, held_ref, sems):
    count = mine_ref.shape[0] // project_ref.shape[1]
    write_pieces(mine_ref, pair_ref, 0, count, expand_ref, project_ref, held_ref, sems)


def early_pass(mine, pair, hidden_units):
    chans = mine.shape[1]
    count = mine.shape[0] // chans
    return pl.pallas_call(
        early_kernel,
        out_shape=[
            jax.ShapeDtypeStruct((chans, hidden_units), jnp.float32),
            jax.ShapeDtypeStruct((hidden_units, chans), jnp.float32),
        ],
        in_specs=[pl.BlockSpec(memory_space=pltpu.VMEM)] * 2,
        out_specs=[pl.BlockSpec(memory_space=pl.ANY)] * 2,
        scratch_shapes=[
            pltpu.VMEM((2 * count, chans, chans), jnp.float32),
            pltpu.SemaphoreType.DMA((2 * count,)),
        ],
        compiler_params=pltpu.CompilerParams(vmem_limit_bytes=6 << 20),
        cost_estimate=pl.CostEstimate(flops=0, bytes_accessed=4 << 20, transcendentals=0),
        name="block_early",
    )(mine, pair)


def finish_kernel(
    last_ref,
    pair_last_ref,
    expand_in_ref,
    project_in_ref,
    kern_ref,
    dwb_ref,
    gain_ref,
    shift_ref,
    expand_ref,
    b_expand_ref,
    project_ref,
    b_project_ref,
    sums_ref,
    held_ref,
    sems,
):
    hidden_units, chans = project_ref.shape
    pieces = hidden_units // chans
    count = held_ref.shape[0] // 2
    small = slice(count * chans, last_ref.shape[0])
    sums_ref[...] = last_ref[small].astype(jnp.float32) + pair_last_ref[small].astype(jnp.float32)
    for row_off in range(7):
        kern_ref[row_off] = sums_ref[row_off * 7 : row_off * 7 + 7]
    dwb_ref[...] = sums_ref[49]
    gain_ref[...] = sums_ref[50]
    shift_ref[...] = sums_ref[51]
    b_project_ref[...] = sums_ref[52]
    for piece in range(pieces):
        b_expand_ref[piece * chans : (piece + 1) * chans] = sums_ref[53 + piece]
    write_pieces(
        last_ref,
        pair_last_ref,
        pieces - count,
        count,
        expand_ref,
        project_ref,
        held_ref,
        sems,
    )


def finish_pass(last, pair_last, expand, project, early):
    hidden_units, chans = project.shape
    count = (hidden_units - early) // chans
    one = jax.ShapeDtypeStruct((chans,), jnp.float32)
    whole = pl.BlockSpec(memory_space=pltpu.VMEM)
    left = pl.BlockSpec(memory_space=pl.ANY)
    return pl.pallas_call(
        finish_kernel,
        out_shape=[
            jax.ShapeDtypeStruct((7, 7, chans), jnp.float32),
            one,
            one,
            one,
            jax.ShapeDtypeStruct((chans, hidden_units), jnp.float32),
            jax.ShapeDtypeStruct((hidden_units,), jnp.float32),
            jax.ShapeDtypeStruct((hidden_units, chans), jnp.float32),
            one,
        ],
        in_specs=[whole, whole, left, left],
        out_specs=[whole, whole, whole, whole, left, whole, left, whole],
        scratch_shapes=[
            pltpu.VMEM((last.shape[0] - count * chans, chans), jnp.float32),
            pltpu.VMEM((2 * count, chans, chans), jnp.float32),
            pltpu.SemaphoreType.DMA((2 * count,)),
        ],
        input_output_aliases={2: 4, 3: 6},
        compiler_params=pltpu.CompilerParams(vmem_limit_bytes=6 << 20),
        name="block_finish",
    )(last, pair_last, expand, project)


def adjoint_kernel(
    top_ref,
    west_ref,
    field_ref,
    east_ref,
    bottom_ref,
    inner_ref,
    cot_ref,
    dw_ref,
    out_ref,
    split_ref,
    spread_ref,
    edge_ref,
    sum_ref,
):
    tiles = split_ref.shape[0]
    rows = cot_ref.shape[0]
    spread_weights(dw_ref, spread_ref)
    band_refs = (west_ref, field_ref, east_ref)
    split_lanes(top_ref, split_ref)
    split_band(band_refs, split_ref, to=3, count=7)
    split_band(band_refs, split_ref, start=rows - 7, to=10, count=7)
    split_lanes(bottom_ref, split_ref, to=17)
    for side in range(2):
        at_pole = lax.axis_index("lat") == (0 if side == 0 else lax.axis_size("lat") - 1)
        for lane in range(tiles):
            for row_off in range(3):
                near = row_off if side == 0 else 6 - row_off
                for col_off in range(7):
                    plain = spread_ref[lane, (6 - near) * 7 + col_off]
                    turned = spread_ref[lane, near * 7 + col_off]
                    edge_ref[side, lane, row_off * 7 + col_off] = jnp.where(at_pole, turned, plain)

    def edge_block(lane, carry):
        for side in range(2):

            def weight_of(row, row_off, col_off):
                if side == 0 and row < 3:
                    return edge_ref[0, lane, row_off * 7 + 6 - col_off]
                if side == 1 and row >= 7:
                    return edge_ref[1, lane, (6 - row_off) * 7 + 6 - col_off]
                return spread_ref[lane, 48 - (row_off * 7 + col_off)]

            totals = window_sums(split_ref, lane, side * 10, weight_of)
            store_sums(totals, sum_ref, lane, side * 4)
        return carry

    lax.fori_loop(0, tiles, edge_block, 0)

    def write(ref, start, to, count):
        def body(row, carry):
            total = jnp.concatenate([ref[lane, start + row] for lane in range(tiles)], axis=1)
            out_ref[to + row] = (cot_ref[to + row].astype(jnp.float32) + total).astype(jnp.bfloat16)
            return carry

        lax.fori_loop(0, count, body, 0)

    write(sum_ref, 0, 0, 4)
    write(inner_ref, 0, 4, rows - 8)
    write(sum_ref, 4, rows - 4, 4)


def adjoint_pass(top, band, bottom, inner, cot, dw_kernel):
    rows, cols, chans = cot.shape
    tiles = chans // LANES
    return pl.pallas_call(
        adjoint_kernel,
        out_shape=jax.ShapeDtypeStruct(cot.shape, jnp.bfloat16),
        in_specs=[pl.BlockSpec(memory_space=pltpu.VMEM)] * 8,
        out_specs=pl.BlockSpec(memory_space=pltpu.VMEM),
        scratch_shapes=[
            pltpu.VMEM((tiles, 20, cols + 6, LANES), jnp.float32),
            pltpu.VMEM((tiles, 49, SUBLANES, LANES), jnp.float32),
            pltpu.VMEM((2, tiles, 21, SUBLANES, LANES), jnp.float32),
            pltpu.VMEM((tiles, 8, cols, LANES), jnp.float32),
        ],
        compiler_params=pltpu.CompilerParams(vmem_limit_bytes=6 << 20),
        cost_estimate=pl.CostEstimate(
            flops=25 * rows * cols * chans, bytes_accessed=3 << 20, transcendentals=0
        ),
        name="block_adjoint",
    )(top, *band, bottom, inner, cot, dw_kernel)


def local(
    fields,
    cotangent,
    dw_kernel,
    dw_bias,
    norm_gain,
    layer_norm_offset,
    w_expand,
    b_expand,
    w_project,
    b_project,
):
    rows = fields.shape[0]
    cols = fields.shape[1]
    chans = fields.shape[2]
    scale_factor = 1.0 / math.sqrt(rows * cols * lax.axis_size("lat") * lax.axis_size("lon"))
    hidden_units = w_expand.shape[1]
    count, exchange = partner_steps()
    barrier = lax.optimization_barrier
    band = lon_margins(fields)
    vectors = packed((dw_bias, norm_gain, layer_norm_offset, b_project, b_expand))
    band, vectors = barrier((band, vectors))
    inner = inner_conv(band, dw_kernel, False)
    edges = lat_margins(band)
    block_out, conv_gradient, keep, give, small = main_pass(
        edges[0],
        band,
        edges[1],
        inner,
        cotangent.reshape(-1, chans),
        dw_kernel,
        vectors,
        w_expand,
        w_project,
        scale_factor,
    )
    block_out = block_out.reshape(fields.shape)
    conv_gradient = conv_gradient.reshape(fields.shape)
    half = hidden_units // 2
    quarter = half // 2
    got_far = within_pair(give[half:])
    got_near = within_pair(give[:half])
    outgoing = widened_sum(keep[half:], got_far).astype(jnp.bfloat16)
    outgoing, taps_in = barrier((outgoing, conv_gradient))
    got = exchange(outgoing[quarter:], 0)
    kept = exchange(outgoing[:quarter], 0)
    small = taps_pass(edges[0], band, edges[1], taps_in, small, scale_factor)
    got, small, conv_gradient = barrier((got, small, conv_gradient))
    outgoing = widened_sum(keep[quarter:half], got_near[quarter:], got).astype(jnp.bfloat16)
    outgoing, conv_gradient = barrier((outgoing, conv_gradient))
    got = exchange(outgoing, 1)
    band = lon_margins(conv_gradient)
    payload = widened_sum(keep[:quarter], got_near[:quarter], kept, got).astype(jnp.bfloat16)
    payload = jnp.concatenate([payload, small], axis=0)
    for at in range(2, count):
        got = exchange(payload, at)
        if at == 2:
            got, band = barrier((got, band))
        payload = rounded_sum(payload, got)
    payload, band = barrier((payload, band))
    top, bottom = lat_margins(band)
    got = exchange(payload, 1)
    inner = inner_conv(band, dw_kernel, True)
    got, inner = barrier((got, inner))
    across = exchange(payload[:quarter], 0)
    beside, small = got[:quarter], rounded_sum(payload[quarter:], got[quarter:])
    sent = jnp.concatenate([beside, small], axis=0)
    sent, band = barrier((sent, band))
    got = exchange(sent, 0)
    grad_fields = adjoint_pass(top, band, bottom, inner, cotangent, dw_kernel)
    mine = jnp.concatenate([payload[:quarter], beside, across], axis=0)
    pair = within_pair(mine)
    written = early_pass(mine, pair, hidden_units)
    got, grad_fields, written = barrier((got, grad_fields, written))
    last = jnp.concatenate([got[:quarter], rounded_sum(small, got[quarter:])], axis=0)
    pair_last = within_pair(last)
    sum_kern, sum_dwb, sum_gn, sum_sh, sum_exp, sum_bexp, sum_proj, sum_bproj = finish_pass(
        last, pair_last, *written, mine.shape[0]
    )
    return (
        block_out,
        grad_fields,
        sum_kern,
        sum_dwb,
        sum_gn,
        sum_sh,
        sum_exp,
        sum_bexp,
        sum_proj,
        sum_bproj,
    )


def solution(mesh):
    placed = (P("lat", "lon", None), P("lat", "lon", None), P(), P(), P(), P(), P(), P(), P(), P())
    return jax.shard_map(
        local,
        mesh=mesh,
        in_specs=placed,
        out_specs=(
            P("lat", "lon", None),
            P("lat", "lon", None),
            P(),
            P(),
            P(),
            P(),
            P(),
            P(),
            P(),
            P(),
        ),
        check_vma=False,
    )
```
